32 devices in a mesh: clip: 2 (over core), tm: 8 (over z, x), head: 2 (over y).
Axes of the slice: x: 2, y: 2, z: 4, core: 2. Of those that a mesh axis runs over, the one named last changes fastest.
Arguments:
- video_tokens: bfloat16 [32, 1568, 1024], P(('clip', 'tm')), parts along dimension 0, may hold values from -6 to 6
- window_order: int32 [32, 1568], P(('clip', 'tm')), parts along dimension 0, may hold values from 0 to 1567, each once within a row
- clip_id: int32 [32], P(('clip', 'tm')), parts along dimension 0, may hold values from 0 to 3, never falling along the last dimension, each value on 1 to 8 neighbouring positions
- attend_weight: bfloat16 [3, 1024, 1024], P(None, None, 'head'), may hold values from -0.75 to 0.75
- attend_out: bfloat16 [1024, 1024], P('head'), may hold values from -0.1875 to 0.1875
- recur_weight: bfloat16 [3, 1024, 1024], P(None, None, 'head'), may hold values from -0.1875 to 0.1875
- frame_decay: float32 [32, 1024], P(('clip', 'tm'), 'head'), parts along dimension 0, may hold values from -5.7 to -0.02125, as said below
- recur_out: bfloat16 [1024, 1024], P('head'), may hold values from -0.1875 to 0.1875
Outputs:
- features_out: bfloat16 [32, 1568, 1024], P(('clip', 'tm'), None, 'head'), parts along dimension 0
The draws below stay inside these ranges and needn't reach their ends.
There are 2 independent parts, one for each index of `clip`. The reference program is written for one: setup_inputs(seed, part) draws one part's arguments, and reference() takes and returns one part's arrays. A program takes and returns all parts, laid end to end along the dimension named above; an argument that names none is the same for every part. Nothing has to cross between parts.
Inputs may be any that keep to these rules, and one draw needn't show every extreme that they name: `clip_id`: never falls along the frames; a clip spans 1 to 8 frames. `frame_decay`: negative.
All inputs are finite; a program needn't handle non-finite values.
Results may differ from the reference program's by a relative error of at most 0.01.
Values may be sent and summed in bfloat16 or wider, within the bound.
A program may use at most 128 MiB of HBM per device.

```python
import math
import jax
import jax.numpy as jnp
import numpy as np
from jax import lax

HEAD_DIMENSION = 64
WINDOW = 49
MODEL_DIMENSION = 1024
F_DEV = 2
TOKF = 1568
FRAME_TOTAL = 16
N_TM = 8
N_HEAD = 2


def draw_attend_weight(key, part):
    first_key, second_key, third_key = jax.random.split(jax.random.fold_in(key, 11), 3)
    shared = jnp.clip(jax.random.normal(first_key, (MODEL_DIMENSION, MODEL_DIMENSION), jnp.float32), -4.0, 4.0)
    random_perturbation = jnp.clip(jax.random.normal(second_key, (MODEL_DIMENSION, MODEL_DIMENSION), jnp.float32), -4.0, 4.0)
    value_part = jnp.clip(jax.random.normal(third_key, (MODEL_DIMENSION, MODEL_DIMENSION), jnp.float32), -4.0, 4.0)
    query_part = shared
    key_part = random_perturbation
    return (jnp.stack([query_part, key_part, value_part]) / jnp.sqrt(jnp.float32(MODEL_DIMENSION))).astype(jnp.bfloat16)


def draw_frame_decay(key, part):
    random_child_keys = jax.random.split(jax.random.fold_in(key, 23), 6)
    number_of_heads = MODEL_DIMENSION // HEAD_DIMENSION
    slow_share = 0.5
    slow_head = jax.random.uniform(random_child_keys[0], (number_of_heads,)) < slow_share
    slow_channel = jnp.repeat(slow_head, HEAD_DIMENSION)
    fast_rate = jnp.exp(jax.random.uniform(random_child_keys[1], (MODEL_DIMENSION,), jnp.float32, jnp.log(0.7), jnp.log(2.5)))
    slow_rate = jax.random.uniform(random_child_keys[2], (MODEL_DIMENSION,), jnp.float32, 0.3, 1.0) * 2.3 / FRAME_TOTAL
    default_decay_rate = jnp.where(slow_channel, slow_rate, fast_rate)
    random_perturbation = jnp.exp(jax.random.uniform(random_child_keys[3], (FRAME_TOTAL, MODEL_DIMENSION), jnp.float32, jnp.log(0.5), jnp.log(2.0)))
    spike_head_index = jax.random.uniform(random_child_keys[4], (FRAME_TOTAL, number_of_heads)) < 3.0 / FRAME_TOTAL
    spike_regions = jnp.repeat(spike_head_index, HEAD_DIMENSION, axis=1)
    spike_length = jax.random.uniform(random_child_keys[5], (FRAME_TOTAL, MODEL_DIMENSION), jnp.float32, 0.22, 0.69)
    return -(default_decay_rate[None, :] * random_perturbation + jnp.where(spike_regions, spike_length, 0.0))


def block_scale(key, shape, shards, smallest, top_value):
    def one(position, shards_of):
        draws = jax.random.uniform(jax.random.fold_in(jax.random.fold_in(key, 6), position), (shards_of,), jnp.float32, smallest / len(shards), top_value / len(shards))
        return jnp.repeat(jnp.exp(draws), shape[position] // shards_of).reshape((-1,) + (1,) * (len(shape) - position - 1))

    level = one(*shards[0])
    for cut in shards[1:]:
        level = level * one(*cut)
    return level


def length_profile(number_of, total, limit, lean):
    weights = [(1 << 20) // math.isqrt(grade ** lean) + 1 for grade in range(2, number_of + 1)]
    rest, holding = total - limit - (number_of - 1), [1] * (number_of - 1)
    while rest > 0:
        free = [i for i in range(number_of - 1) if holding[i] < limit]
        pool, left = sum([weights[i] for i in free]), rest
        for i in free:
            addition = min(limit - holding[i], max(1, left * weights[i] // pool), rest)
            holding[i] = holding[i] + addition
            rest = rest - addition
    return np.array([limit] + holding)


def ragged(rng, count, total, limit, lean):
    if count == 2:
        one = jax.random.randint(rng, (), max(1, total - limit), min(limit, total - 1) + 1)
        return jnp.stack([one, total - one])
    sizes = jnp.asarray(length_profile(count, total, limit, lean), jnp.int32)
    couples = (count - 1) // 2
    donor, taker = sizes[1:1 + 2 * couples:2], sizes[2:2 + 2 * couples:2]
    room = jnp.minimum(donor - 1, limit - taker)
    shifted = jax.random.randint(jax.random.fold_in(rng, 1), (couples,), 0, 1 << 20) % (room + 1)
    sizes = sizes.at[1:1 + 2 * couples:2].set(donor - shifted).at[2:2 + 2 * couples:2].set(taker + shifted)
    return sizes[jax.random.permutation(jax.random.fold_in(rng, 2), count)]


def scatter_about(own_key, shape, deviation, bound, cuts=(), kind=jnp.bfloat16):
    entries = deviation * jax.random.normal(own_key, shape, jnp.float32)
    if cuts:
        entries = entries * block_scale(own_key, shape, cuts, -0.22, 0.18)
    return jnp.clip(entries, -bound, bound).astype(kind)


def setup_inputs(seed: int = 0, part: int = 0) -> dict:
    splits = jax.random.split(jax.random.key(seed), 9)
    part_splits = jax.random.split(jax.random.fold_in(splits[8], part), 9)
    return {
        "video_tokens": scatter_about(part_splits[0], (FRAME_TOTAL, TOKF, MODEL_DIMENSION), 1.0, 6.0, ((0, 8),)),
        "window_order": jax.vmap(lambda own: jax.random.permutation(own, TOKF))(jax.random.split(part_splits[1], FRAME_TOTAL)).reshape((FRAME_TOTAL, TOKF)).astype(jnp.int32),
        "clip_id": jnp.searchsorted(jnp.cumsum(ragged(part_splits[2], N_TM // 2, FRAME_TOTAL, 4 * F_DEV, 1)), jnp.arange(FRAME_TOTAL), side="right").astype(jnp.int32),
        "attend_weight": draw_attend_weight(jax.random.fold_in(splits[8], 71), part),
        "attend_out": scatter_about(splits[4], (MODEL_DIMENSION, MODEL_DIMENSION), MODEL_DIMENSION ** -0.5, 0.1875, ((0, 2),)),
        "recur_weight": scatter_about(splits[5], (3, MODEL_DIMENSION, MODEL_DIMENSION), MODEL_DIMENSION ** -0.5, 0.1875, ((2, 2),)),
        "frame_decay": draw_frame_decay(jax.random.fold_in(jax.random.fold_in(splits[8], part), 71), part),
        "recur_out": scatter_about(splits[7], (MODEL_DIMENSION, MODEL_DIMENSION), MODEL_DIMENSION ** -0.5, 0.1875, ((0, 2),)),
    }


EPSILON = 1e-06

def normalize(values):
    return values * lax.rsqrt(lax.optimization_barrier(jnp.mean(values * values, axis=-1, keepdims=True)) + EPSILON)

def window_attention(queries, keys_all, values_all, window_order):
    frame_count, positions, number_of_heads, head_size = queries.shape
    order_index = window_order.astype(jnp.int32)[:, :, None, None]

    def arrange(tensor):
        reordered = jnp.take_along_axis(tensor, order_index, axis=1)
        return reordered.reshape(frame_count, positions // WINDOW, WINDOW, number_of_heads, head_size).astype(jnp.float32)
    scores = jnp.einsum('fwihe,fwjhe->fwhij', arrange(queries), arrange(keys_all)) / jnp.sqrt(jnp.float32(head_size))
    weights = jax.nn.softmax(scores, axis=-1).astype(jnp.bfloat16)
    blended = jnp.einsum('fwhij,fwjhe->fwihe', weights.astype(jnp.float32), arrange(values_all)).astype(jnp.bfloat16)
    blended = blended.reshape(frame_count, positions, number_of_heads, head_size)
    inverse = jnp.argsort(window_order, axis=1).astype(jnp.int32)
    return jnp.take_along_axis(blended, inverse[:, :, None, None], axis=1)

def grouped_product(left_side, right_side):
    group_width = left_side.shape[1] // N_HEAD
    running = jnp.zeros((left_side.shape[0], right_side.shape[1]), jnp.float32)
    for member in range(N_HEAD):
        partial_term = jnp.dot(left_side[:, member * group_width:(member + 1) * group_width], right_side[member * group_width:(member + 1) * group_width], preferred_element_type=jnp.float32)
        rounded = lax.optimization_barrier(partial_term.astype(jnp.bfloat16))
        running = running + rounded.astype(jnp.float32)
    return running

def reference(video_tokens, window_order, clip_id, attend_weight, attend_out, recur_weight, frame_decay, recur_out):
    frame_count, positions, model_width = video_tokens.shape
    number_of_heads = model_width // HEAD_DIMENSION
    inputs = video_tokens.astype(jnp.float32).reshape(-1, model_width)
    normed = normalize(inputs).astype(jnp.bfloat16)
    projected = jnp.einsum('td,kde->kte', normed.astype(jnp.float32), attend_weight.astype(jnp.float32)).astype(jnp.bfloat16)
    shaped = projected.reshape(3, frame_count, positions, number_of_heads, HEAD_DIMENSION)
    attended = window_attention(shaped[0], shaped[1], shaped[2], window_order).reshape(-1, model_width)
    residual = inputs + grouped_product(attended, attend_out)
    normed_again = normalize(residual).astype(jnp.bfloat16)
    recur_proj = jnp.einsum('td,kde->kte', normed_again.astype(jnp.float32), recur_weight.astype(jnp.float32))
    gate_in = jax.nn.sigmoid(recur_proj[0]).reshape(frame_count, positions, model_width)
    value_in = recur_proj[1].reshape(frame_count, positions, model_width)
    out_gate = jax.nn.silu(recur_proj[2]).reshape(frame_count, positions, model_width)
    retain = jnp.exp(frame_decay)
    driven = jnp.sqrt(1.0 - retain * retain)[:, None, :] * gate_in * value_in
    continues = jnp.concatenate([jnp.zeros((1,), jnp.float32), (clip_id[1:] == clip_id[:-1]).astype(jnp.float32)])
    factor = retain * continues[:, None]

    def advance(state_now, inputs_now):
        factor_now, driven_now = inputs_now
        state_now = factor_now[None, :] * state_now + driven_now
        return (state_now, state_now)
    final_state, states = lax.scan(advance, jnp.zeros((positions, model_width), jnp.float32), (factor, driven))
    output_rows = (states * out_gate).astype(jnp.bfloat16).reshape(-1, model_width)
    result = residual + grouped_product(output_rows, recur_out)
    return result.astype(jnp.bfloat16).reshape(frame_count, positions, model_width)
```

```python
import functools

import jax
import jax.numpy as jnp
from jax import lax
from jax.experimental import pallas as pl
from jax.experimental.pallas import tpu as pltpu
from jax.sharding import PartitionSpec as P

HEAD_DIMENSION = 64
WINDOW = 49
LONGEST_CLIP = 8
EPSILON = 1e-06

PAIR = 2 * WINDOW
BLOCK = 112
STEP_BLOCKS = 4
ROWS = 112

F32, BF16 = jnp.float32, jnp.bfloat16
VMEM_LIMIT = 58 * 1024 * 1024
COLUMNS = 256
MESH = pl.DeviceIdType.MESH


def dot(a, b):
    return jnp.dot(a, b, preferred_element_type=F32)


def attend_kernel(place, x_ref, column_ref, row_ref, w_ref, own_ref, other_ref, normed, blended):
    step = pl.program_id(0)
    positions, width = x_ref.shape[1:]
    local = w_ref.shape[2]
    rows = STEP_BLOCKS * BLOCK

    @pl.when(step == 0)
    def _():
        @pl.loop(0, positions // ROWS)
        def _(i):
            at = pl.ds(pl.multiple_of(i * ROWS, ROWS), ROWS)
            x = x_ref[0, at, :].astype(F32)
            scale = lax.rsqrt(jnp.mean(x * x, axis=-1, keepdims=True) + EPSILON)
            normed[at, :] = (x * scale).astype(BF16)

    tokens = lax.broadcasted_iota(jnp.int32, (rows, positions), 1)
    pick = jnp.where(column_ref[...] == tokens, 1.0, 0.0).astype(BF16)
    gathered = dot(pick, normed[...]).astype(BF16)
    queries = (dot(gathered, w_ref[0]) * (HEAD_DIMENSION**-0.5)).astype(BF16)
    keys = dot(gathered, w_ref[1]).astype(BF16)
    values = dot(gathered, w_ref[2]).astype(BF16)

    two = 2 * HEAD_DIMENSION
    first = lax.broadcasted_iota(jnp.int32, (BLOCK, two), 1) < HEAD_DIMENSION
    row = lax.broadcasted_iota(jnp.int32, (2 * BLOCK, BLOCK), 0)
    row = jnp.where(row >= BLOCK, row - BLOCK, row)
    column = lax.broadcasted_iota(jnp.int32, (2 * BLOCK, BLOCK), 1)
    same = ((row < WINDOW) & (column < WINDOW)) | (
        (row >= WINDOW) & (column >= WINDOW) & (column < PAIR)
    )
    for block in range(STEP_BLOCKS):
        low = block * BLOCK
        for lane in range(0, local, two):
            q = queries[low : low + BLOCK, lane : lane + two]
            k = keys[low : low + BLOCK, lane : lane + two]
            v = values[low : low + BLOCK, lane : lane + two]
            none = jnp.zeros_like(q)
            both = jnp.concatenate([jnp.where(first, q, none), jnp.where(first, none, q)], axis=0)
            scores = lax.dot_general(
                both, k, (((1,), (1,)), ((), ())), preferred_element_type=F32
            )
            scores = jnp.where(same, scores, -1e30)
            raised = jnp.exp(scores - jnp.max(scores, axis=-1, keepdims=True))
            weights = raised * (1.0 / jnp.sum(raised, axis=-1, keepdims=True))
            mixed = dot(weights.astype(BF16), v)
            mixed = jnp.where(first, mixed[:BLOCK], mixed[BLOCK:]).astype(BF16)
            at = pl.ds(pl.multiple_of(step * rows + low, BLOCK), BLOCK)
            blended[at, lane : lane + two] = mixed

    @pl.when(step == pl.num_programs(0) - 1)
    def _():
        half = own_ref.shape[0]
        slots = blended.shape[0]
        for out_ref, side in ((own_ref, place[0]), (other_ref, 1 - place[0])):

            @pl.loop(0, half // ROWS)
            def _(i):
                token = lax.broadcasted_iota(jnp.int32, (ROWS, slots), 0) + (side * half + i * ROWS)
                put = jnp.where(token == row_ref[...], 1.0, 0.0).astype(BF16)
                at = pl.ds(pl.multiple_of(i * ROWS, ROWS), ROWS)
                out_ref[at, :] = dot(put, blended[...]).astype(BF16)


def attend(place, frame, video_tokens, order, weight):
    positions, width = video_tokens.shape[1:]
    local = weight.shape[2]
    slots = order.shape[0]
    rows = STEP_BLOCKS * BLOCK
    half = positions // 2
    once = pl.Buffered(1)
    return pl.pallas_call(
        attend_kernel,
        grid_spec=pltpu.PrefetchScalarGridSpec(
            num_scalar_prefetch=1,
            grid=(slots // rows,),
            in_specs=[
                pl.BlockSpec(
                    (1, positions, width), lambda i, s: (frame, 0, 0), pipeline_mode=once
                ),
                pl.BlockSpec((rows, 1), lambda i, s: (i, 0)),
                pl.BlockSpec((1, slots), lambda i, s: (0, 0), pipeline_mode=once),
                pl.BlockSpec((3, width, local), lambda i, s: (0, 0, 0), pipeline_mode=once),
            ],
            out_specs=[pl.BlockSpec((half, local), lambda i, s: (0, 0))] * 2,
            scratch_shapes=[
                pltpu.VMEM((positions, width), BF16),
                pltpu.VMEM((slots, local), BF16),
            ],
        ),
        out_shape=[jax.ShapeDtypeStruct((half, local), BF16)] * 2,
        compiler_params=pltpu.CompilerParams(vmem_limit_bytes=VMEM_LIMIT),
        cost_estimate=pl.CostEstimate(
            flops=2 * slots * width * (positions + 3 * local) + 2 * positions * slots * local,
            bytes_accessed=2 * (positions * (width + local) + 3 * width * local),
            transcendentals=slots * BLOCK * local // HEAD_DIMENSION,
        ),
        name="attend",
    )(place, video_tokens, order[:, None], order[None, :], weight)


def held():
    return pl.BlockSpec(memory_space=pltpu.VMEM)


def tail_kernel(frames, rounds, *refs):
    refs = list(refs)

    def take(count):
        taken, refs[:count] = refs[:count], []
        return taken

    (x_any,) = take(1)
    own_any, other_any, (send_any,) = take(frames), take(frames - 1), take(1)
    weights_any = take(9)
    coef, factor, decay = take(3)
    (out_any,) = take(1)
    x, own, other, arrived, mix_w, recur_w, emit_w = take(7)
    residual, gate, states, pair_out, pair_in, merged, ring_out, ring_in = take(8)
    back_out, back_keep, back_in, result, decay_in = take(5)
    load_sem, y_sem, d_sem, pair_sem, ring_sem, back_sem, out_sem, keep_sem = take(8)

    core, t, h = (lax.axis_index(name) for name in ("clip", "tm", "head"))
    count = lax.axis_size("tm")
    odd = lax.rem(t, 2)
    has_next, has_prev = t + 2 < count, t >= 2
    chunks = arrived.shape[0]
    half = chunks * ROWS
    local = own.shape[2]
    width = 2 * local

    def remote(src, dst, sems, at, **device):
        return pltpu.make_async_remote_copy(
            src_ref=src,
            dst_ref=dst,
            send_sem=sems.at[(0, *at)],
            recv_sem=sems.at[(1, *at)],
            device_id=device,
            device_id_type=MESH,
        )

    def y_copy(i):
        rows = pl.ds(pl.multiple_of(i * ROWS, ROWS), ROWS)
        return remote(send_any.at[rows], arrived.at[i], y_sem, (i,), head=1 - h)

    partner = t + 1 - 2 * odd

    def decay_copy():
        return remote(decay, decay_in, d_sem, (0,), tm=partner)

    def pair_copy(i):
        return remote(pair_out.at[i, 1 - odd], pair_in.at[i], pair_sem, (i,), tm=partner)

    def ring_copy(r, i):
        return remote(ring_out.at[r, i], ring_in.at[r, i], ring_sem, (r, i), tm=t + 2)

    def back_copy(i):
        return remote(back_out.at[i], back_in.at[i], back_sem, (i,), tm=partner)

    def placed(i):
        return out_any.at[:, pl.ds(pl.multiple_of(h * half + i * ROWS, ROWS), ROWS), :]

    def out_copy(i):
        return remote(result.at[i, 1 - h], placed(i), out_sem, (i,), head=1 - h)

    def keep_copy(i):
        return pltpu.make_async_copy(result.at[i, h], placed(i), keep_sem.at[i])

    cut = local // 2
    mine, theirs = core * cut, (1 - core) * cut
    at_rows = [pl.ds(pl.multiple_of(low, cut), cut) for low in (mine, theirs)]
    loads = [(weights_any[0], mix_w.at[0])]
    loads += [(weights_any[1 + k], mix_w.at[1, at_rows[k]]) for k in range(2)]
    loads += [(own_any[f], own.at[f]) for f in range(frames)]
    loads += [(other_any[f], other.at[f]) for f in range(frames - 1)]
    loads += [(x_any.at[:, pl.ds(pl.multiple_of(h * half, ROWS), half), :], x)]
    early = len(loads)
    loads += [(weights_any[3], recur_w.at[0])]
    loads += [(weights_any[4 + k], recur_w.at[1, :, :, at_rows[k]]) for k in range(2)]
    middle = len(loads)
    loads += [(weights_any[6], emit_w.at[0])]
    loads += [(weights_any[7 + k], emit_w.at[1, at_rows[k]]) for k in range(2)]
    loads = [pltpu.make_async_copy(a, b, load_sem.at[k]) for k, (a, b) in enumerate(loads)]
    for load in loads:
        load.start()

    barrier = pltpu.get_barrier_semaphore()
    pl.semaphore_signal(barrier, inc=1, device_id={"head": 1 - h}, device_id_type=MESH)
    pl.semaphore_signal(barrier, inc=1, device_id={"tm": partner}, device_id_type=MESH)

    @pl.when(has_next)
    def _():
        pl.semaphore_signal(barrier, inc=1, device_id={"tm": t + 2}, device_id_type=MESH)

    @pl.when(has_prev)
    def _():
        pl.semaphore_signal(barrier, inc=1, device_id={"tm": t - 2}, device_id_type=MESH)

    pl.semaphore_wait(barrier, 2 + has_next.astype(jnp.int32) + has_prev.astype(jnp.int32))

    @pl.loop(0, chunks)
    def _(i):
        y_copy(i).start()

    decay_copy().start()

    @pl.when(t < 2)
    def _():
        ring_in[...] = jnp.zeros_like(ring_in)

    for load in loads[:middle]:
        load.wait()
    decay_copy().wait()

    is_odd = odd == 1
    last = frames - 1

    def halves(ref):
        low, high = ref[last : last + 1, :local], ref[last : last + 1, local:]
        return jnp.where(is_odd, high, low)

    def decays():
        here, there = halves(decay), halves(decay_in)
        return jnp.where(is_odd, there, here), jnp.where(is_odd, here, there)

    def order(i):
        here, there = pair_out[i, odd].astype(F32), pair_in[i].astype(F32)
        return jnp.where(is_odd, there, here), jnp.where(is_odd, here, there)

    def drive_step(i):
        y_copy(i).wait_recv()
        rows = pl.ds(pl.multiple_of(i * ROWS, ROWS), ROWS)
        left = jnp.concatenate([own[f, rows] for f in range(frames)], axis=0)
        right = jnp.concatenate(
            [other[f, rows] for f in range(frames - 1)] + [arrived[i]], axis=0
        )
        mix = dot(left, mix_w[0]).astype(BF16).astype(F32)
        mix = mix + dot(right, mix_w[1]).astype(BF16).astype(F32)
        total = jnp.concatenate([x[f, rows].astype(F32) for f in range(frames)], axis=0) + mix
        residual[i] = total
        scale = lax.rsqrt(jnp.mean(total * total, axis=-1, keepdims=True) + EPSILON)
        normed = (total * scale).astype(BF16)
        for low in range(0, width, COLUMNS):
            side, lanes = low // local, slice(low % local, low % local + COLUMNS)
            wide = slice(low, low + COLUMNS)
            gate_in = jax.nn.sigmoid(dot(normed, recur_w[side, 0, :, lanes]))
            drive_in = gate_in * dot(normed, recur_w[side, 1, :, lanes])
            opened = dot(normed, recur_w[side, 2, :, lanes])
            gate[i, :, wide] = (opened * jax.nn.sigmoid(opened)).astype(BF16)
            state = None
            for f in range(frames):
                here = slice(f * ROWS, (f + 1) * ROWS)
                driven = coef[f : f + 1, wide] * drive_in[here]
                state = driven if f == 0 else factor[f : f + 1, wide] * state + driven
                states[i, here, wide] = state.astype(BF16)
            pair_out[i, side, :, lanes] = state.astype(BF16)
        pair_copy(i).start()

    def ring_step(r, i):
        earlier_decay, later_decay = decays()
        if r == 0:
            pair_copy(i).wait_recv()
            earlier, later = order(i)
            total = later_decay * earlier + later
            merged[i] = total
        else:

            @pl.when(has_prev)
            def _():
                ring_copy(r - 1, i).wait_recv()

            entering = ring_in[r - 1, i].astype(F32)
            total = merged[i] + (earlier_decay * later_decay) * entering

        @pl.when(has_next)
        def _():
            ring_out[r, i] = total.astype(BF16)
            ring_copy(r, i).start()

    def back_step(i):
        @pl.when(has_prev)
        def _():
            ring_copy(rounds - 1, i).wait_recv()

        entering = ring_in[rounds - 1, i]
        earlier, _ = order(i)
        second = (earlier + decays()[0] * entering.astype(F32)).astype(BF16)
        back_keep[i] = jnp.where(is_odd, second, entering)
        back_out[i] = jnp.where(is_odd, entering, second)
        back_copy(i).start()

    def emit_step(i):
        back_copy(i).wait_recv()
        here, there = back_keep[i], back_in[i]
        incoming = (jnp.where(is_odd, there, here), jnp.where(is_odd, here, there))
        sides = []
        for side in range(2):
            wide = slice(side * local, (side + 1) * local)
            coming = incoming[side].astype(F32)
            parts = []
            for f in range(frames):
                rows = slice(f * ROWS, (f + 1) * ROWS)
                state = states[i, rows, wide].astype(F32) + decay[f : f + 1, wide] * coming
                parts.append((state * gate[i, rows, wide].astype(F32)).astype(BF16))
            sides.append(jnp.concatenate(parts, axis=0))
        for side in range(2):
            wide = slice(side * local, (side + 1) * local)
            mix = dot(sides[0], emit_w[0, :, wide]).astype(BF16).astype(F32)
            mix = mix + dot(sides[1], emit_w[1, :, wide]).astype(BF16).astype(F32)
            done = (residual[i, :, wide] + mix).astype(BF16)
            for f in range(frames):
                result[i, side, f] = done[f * ROWS : (f + 1) * ROWS]
        out_copy(i).start()
        keep_copy(i).start()

    @pl.loop(0, chunks + rounds + 2)
    def _(tick):
        @pl.when(tick < chunks)
        def _():
            drive_step(tick)

        @pl.when(tick == rounds + 2)
        def _():
            for load in loads[middle:]:
                load.wait()

        for lag in range(1, rounds + 3):
            i = tick - lag

            @pl.when((i >= 0) & (i < chunks))
            def _():
                if lag <= rounds:
                    ring_step(lag - 1, i)
                elif lag == rounds + 1:
                    back_step(i)
                else:
                    emit_step(i)

    @pl.loop(0, chunks)
    def _(i):
        y_copy(i).wait_send()
        pair_copy(i).wait_send()
        back_copy(i).wait_send()
        keep_copy(i).wait()

        @pl.when(has_next)
        def _():
            for r in range(rounds):
                ring_copy(r, i).wait_send()

        out_copy(i).wait()


def tail(video_tokens, own, other, send, weights, coef, factor, decay):
    frames, positions, width = video_tokens.shape
    half, local = own[0].shape
    chunks = half // ROWS
    pairs = lax.axis_size("tm") // 2
    rounds = min(pairs - 1, -(-(LONGEST_CLIP - 1) // (2 * frames)))
    rows = frames * ROWS
    dma = pltpu.SemaphoreType.DMA
    anywhere = pl.BlockSpec(memory_space=pl.ANY)
    arrays = [video_tokens, *own, *other, send, *weights]
    return pl.pallas_call(
        functools.partial(tail_kernel, frames, rounds),
        in_specs=[anywhere] * len(arrays) + [held()] * 3,
        out_specs=anywhere,
        out_shape=jax.ShapeDtypeStruct((frames, positions, local), BF16),
        scratch_shapes=[
            pltpu.VMEM((frames, half, width), BF16),
            pltpu.VMEM((frames, half, local), BF16),
            pltpu.VMEM((max(1, frames - 1), half, local), BF16),
            pltpu.VMEM((chunks, ROWS, local), BF16),
            pltpu.VMEM((2, local, width), BF16),
            pltpu.VMEM((2, 3, width, local), BF16),
            pltpu.VMEM((2, local, width), BF16),
            pltpu.VMEM((chunks, rows, width), F32),
            pltpu.VMEM((chunks, rows, width), BF16),
            pltpu.VMEM((chunks, rows, width), BF16),
            pltpu.VMEM((chunks, 2, ROWS, local), BF16),
            pltpu.VMEM((chunks, ROWS, local), BF16),
            pltpu.VMEM((chunks, ROWS, local), F32),
            pltpu.VMEM((rounds, chunks, ROWS, local), BF16),
            pltpu.VMEM((rounds, chunks, ROWS, local), BF16),
            pltpu.VMEM((chunks, ROWS, local), BF16),
            pltpu.VMEM((chunks, ROWS, local), BF16),
            pltpu.VMEM((chunks, ROWS, local), BF16),
            pltpu.VMEM((chunks, 2, frames, ROWS, local), BF16),
            pltpu.VMEM((frames, width), F32),
            dma((len(arrays),)),
            dma((2, chunks)),
            dma((2, 1)),
            dma((2, chunks)),
            dma((2, rounds, chunks)),
            dma((2, chunks)),
            dma((2, chunks)),
            dma((chunks,)),
        ],
        compiler_params=pltpu.CompilerParams(
            vmem_limit_bytes=VMEM_LIMIT, collective_id=0, has_side_effects=True
        ),
        cost_estimate=pl.CostEstimate(
            flops=10 * frames * half * width * width,
            bytes_accessed=frames * half * width * 12,
            transcendentals=2 * frames * half * width,
        ),
        name="tail",
    )(*arrays, coef, factor, decay)


def swap(value, axis):
    count = lax.axis_size(axis)
    return lax.ppermute(value, axis, [(i, i ^ 1) for i in range(count)])


def shift(value, axis, steps):
    count = lax.axis_size(axis)
    return lax.ppermute(value, axis, [(i, i + steps) for i in range(count - steps)])


def fetch(value, dimension):
    size = value.shape[dimension] // 2
    start = lax.axis_index("clip") * size
    piece = swap(lax.dynamic_slice_in_dim(value, start, size, dimension), "head")
    return piece, swap(piece, "clip")


def per_device(
    video_tokens,
    window_order,
    clip_id,
    attend_weight,
    attend_out,
    recur_weight,
    frame_decay,
    recur_out,
):
    frames, positions, width = video_tokens.shape
    side = lax.axis_index("head")
    place = side.astype(jnp.int32).reshape(1)
    mix_a, mix_b = fetch(attend_out, 0)
    frame_decay = jnp.concatenate([frame_decay, swap(frame_decay, "head")], axis=1)
    recur_a, recur_b = fetch(recur_weight, 2)
    emit_a, emit_b = fetch(recur_out, 0)

    retain = jnp.exp(frame_decay)
    coef = jnp.sqrt(1.0 - retain * retain)
    previous = shift(clip_id[frames - 1 :], "tm", 1)
    continues = (clip_id == jnp.concatenate([previous, clip_id[:-1]])).astype(F32)
    factor = retain * continues[:, None]
    decay_all = jnp.cumprod(factor, axis=0)

    order = window_order.reshape(frames, positions // PAIR, PAIR)
    order = jnp.pad(order, ((0, 0), (0, 0), (0, BLOCK - PAIR)), constant_values=-1)
    order = order.reshape(frames, -1)
    weights = (attend_out, mix_a, mix_b, recur_weight, recur_a, recur_b, recur_out, emit_a, emit_b)
    own, other = [], []
    for f in range(frames):
        placed = order[f]
        if f:
            placed, coef, factor, mix_a = lax.optimization_barrier((placed, coef, factor, mix_a))
        mine, theirs = attend(place, f, video_tokens, placed, attend_weight)
        own.append(mine)
        other.append(theirs if f == frames - 1 else swap(theirs, "head"))
    return tail(video_tokens, own, other[:-1], other[-1], weights, coef, factor, decay_all)


def from_behind(value, axis, steps):
    count = lax.axis_size(axis)
    leading, last = (max(0, -steps), min(count, count - steps))
    return lax.ppermute(value, axis, [(source, source + steps) for source in range(leading, last)])


def prefix_2(value, axis, combine, identity):
    count, position = (lax.axis_size(axis), lax.axis_index(axis))
    everything = jax.tree.map(
        lambda part, kind: lax.all_gather(part.astype(kind), axis),
        value,
        (jnp.bfloat16, jnp.bfloat16),
    )
    start = jax.tree.map(
        lambda part, zero: jnp.broadcast_to(jnp.asarray(zero, part.dtype), part.shape),
        value,
        identity,
    )

    def hop(k, before):
        reached = k < position
        new = combine(
            before, jax.tree.map(lambda part, own: part[k].astype(own.dtype), everything, value)
        )
        return jax.tree.map(lambda a, b: jnp.where(reached, a, b), new, before)

    return lax.fori_loop(0, count, hop, start)


def normalize(values):
    return values * lax.rsqrt(jnp.mean(values * values, axis=-1, keepdims=True) + EPSILON)


def window_attention(queries, keys_all, values_all, window_order):
    frame_count, positions, number_of_heads, head_size = queries.shape
    order_index = window_order[:, :, None, None]

    def arrange(tensor):
        reordered = jnp.take_along_axis(tensor, order_index, axis=1)
        return reordered.reshape(
            frame_count, positions // WINDOW, WINDOW, number_of_heads, head_size
        )

    scores = jnp.einsum(
        "fwihe,fwjhe->fwhij",
        arrange(queries),
        arrange(keys_all),
        preferred_element_type=jnp.float32,
    ) / jnp.sqrt(jnp.float32(head_size))
    weights = jax.nn.softmax(scores, axis=-1).astype(jnp.bfloat16)
    blended = jnp.einsum(
        "fwhij,fwjhe->fwihe", weights, arrange(values_all), preferred_element_type=jnp.float32
    ).astype(jnp.bfloat16)
    blended = blended.reshape(frame_count, positions, number_of_heads, head_size)
    inverse = jnp.argsort(window_order, axis=1)
    return jnp.take_along_axis(blended, inverse[:, :, None, None], axis=1)


def per_device_any(
    video_tokens,
    window_order,
    clip_id,
    attend_weight,
    attend_out,
    recur_weight,
    frame_decay,
    recur_out,
):
    frame_count, positions, model_width = video_tokens.shape
    local_width = attend_weight.shape[2]
    row_count = frame_count * positions
    inputs = video_tokens.reshape(row_count, model_width).astype(jnp.float32)
    normed = normalize(inputs).astype(jnp.bfloat16)
    projected = jnp.einsum(
        "td,kde->kte", normed, attend_weight, preferred_element_type=jnp.float32
    ).astype(jnp.bfloat16)
    shaped = projected.reshape(
        3, frame_count, positions, local_width // HEAD_DIMENSION, HEAD_DIMENSION
    )
    attended = window_attention(shaped[0], shaped[1], shaped[2], window_order).reshape(
        row_count, local_width
    )
    partial_mix = jnp.dot(attended, attend_out, preferred_element_type=jnp.float32)
    offset = lax.axis_index("head") * local_width
    residual = inputs + lax.psum(partial_mix.astype(jnp.bfloat16), "head").astype(jnp.float32)
    normed_again = normalize(residual).astype(jnp.bfloat16)
    recur_proj = jnp.einsum(
        "td,kde->kte", normed_again, recur_weight, preferred_element_type=jnp.float32
    )
    residual_own = lax.dynamic_slice_in_dim(residual, offset, local_width, 1)
    gate_in = jax.nn.sigmoid(recur_proj[0]).reshape(frame_count, positions, local_width)
    value_in = recur_proj[1].reshape(frame_count, positions, local_width)
    out_gate = jax.nn.silu(recur_proj[2]).reshape(frame_count, positions, local_width)
    retain = jnp.exp(frame_decay)
    driven = jnp.sqrt(1.0 - retain * retain)[:, None, :] * gate_in * value_in
    previous = from_behind(clip_id[frame_count - 1 :], "tm", 1)
    continues = jnp.concatenate(
        [
            (clip_id[:1] == previous).astype(jnp.float32),
            (clip_id[1:] == clip_id[:-1]).astype(jnp.float32),
        ]
    )
    factor = retain * continues[:, None]

    def advance(carried, inputs_now):
        decay_total, state_now = carried
        factor_now, driven_now = inputs_now
        decay_total = factor_now * decay_total
        state_now = factor_now[None, :] * state_now + driven_now
        return ((decay_total, state_now), (decay_total, state_now))

    start_carry = (
        jnp.ones((local_width,), jnp.float32),
        jnp.zeros((positions, local_width), jnp.float32),
    )
    last_carry, all_carry = lax.scan(advance, start_carry, (factor, driven))
    decay_last, state_last = last_carry
    decay_all, state_all = all_carry

    def combine(earlier, later_part):
        return (later_part[0] * earlier[0], later_part[0][None, :] * earlier[1] + later_part[1])

    prefix = prefix_2(
        (decay_last, state_last),
        "tm",
        combine,
        (jnp.ones_like(decay_last), jnp.zeros_like(state_last)),
    )
    incoming = prefix[1]
    states = state_all + decay_all[:, None, :] * incoming[None, :, :]
    output_rows = (states * out_gate).astype(jnp.bfloat16).reshape(row_count, local_width)
    partial_out = jnp.dot(output_rows, recur_out, preferred_element_type=jnp.float32)
    result = residual_own + lax.psum_scatter(
        partial_out.astype(jnp.bfloat16), "head", scatter_dimension=1, tiled=True
    ).astype(jnp.float32)
    return result.astype(jnp.bfloat16).reshape(frame_count, positions, local_width)


def solution(mesh):
    halves = mesh.shape["head"] == 2 and mesh.shape["clip"] == 2 and mesh.shape["tm"] % 2 == 0 and mesh.shape["tm"] > 2
    return jax.shard_map(
        per_device if halves else per_device_any,
        mesh=mesh,
        in_specs=(
            P(("clip", "tm"), None, None),
            P(("clip", "tm"), None),
            P(("clip", "tm")),
            P(None, None, "head"),
            P("head", None),
            P(None, None, "head"),
            P(("clip", "tm"), "head"),
            P("head", None),
        ),
        out_specs=P(("clip", "tm"), None, "head"),
        check_vma=False,
    )
```

```python
import functools

import jax
import jax.numpy as jnp
from jax import lax
from jax.experimental import pallas as pl
from jax.experimental.pallas import tpu as pltpu
from jax.sharding import PartitionSpec as P

HEAD_DIMENSION = 64
WINDOW = 49
LONGEST_CLIP = 8
EPSILON = 1e-06

PAIR = 2 * WINDOW
BLOCK = 112
STEP_BLOCKS = 4
ROWS = 112

F32, BF16 = jnp.float32, jnp.bfloat16
VMEM_LIMIT = 67043328
COLUMNS = 256
MESH = pl.DeviceIdType.MESH


def dot(a, b):
    return jnp.dot(a, b, preferred_element_type=F32)


def held():
    return pl.BlockSpec(memory_space=pltpu.VMEM)


def block_kernel(frames, rounds, *refs):
    refs = list(refs)

    def take(count):
        taken, refs[:count] = refs[:count], []
        return taken

    (clip,) = take(1)
    x_any, attend_any, mix_any, recur_any, emit_any = take(5)
    slots_ref, rows_ref, frame_decay = take(3)
    (out_any,) = take(1)
    x, attend_w, normed, blended, own, theirs, arrived = take(7)
    mix_w, recur_w, emit_w, residual, gate, states = take(6)
    pair_out, pair_in, merged, ring_out, ring_in = take(5)
    back_out, back_keep, back_in, result = take(4)
    coef, factor, decay, decay_in, channel_in, clip_out, clip_in = take(7)
    load_sem, weight_sem, small_sem, y_sem, pair_sem, ring_sem, back_sem, out_sem, keep_sem = take(9)

    core, t, h = (lax.axis_index(name) for name in ("clip", "tm", "head"))
    count = lax.axis_size("tm")
    odd = lax.rem(t, 2)
    has_next, has_prev = t + 2 < count, t >= 2
    has_after, has_before = t + 1 < count, t >= 1
    chunks = arrived.shape[1]
    half = chunks * ROWS
    positions, width = x.shape[1:]
    local = own.shape[2]
    steps = slots_ref.shape[0] // frames
    rows_step = STEP_BLOCKS * BLOCK
    partner = t + 1 - 2 * odd
    pair_parity = lax.rem(lax.div(t, 2), 2)
    across = t + 2 - 4 * pair_parity
    last = frames - 1

    def remote(src, dst, sems, at, **device):
        return pltpu.make_async_remote_copy(
            src_ref=src,
            dst_ref=dst,
            send_sem=sems.at[(0, *at)],
            recv_sem=sems.at[(1, *at)],
            device_id=device,
            device_id_type=MESH,
        )

    def chunk(i):
        return pl.ds(pl.multiple_of(i * ROWS, ROWS), ROWS)

    def y_copy(f, i):
        return remote(theirs.at[f, i], arrived.at[f, i], y_sem, (f, i), head=1 - h)

    def decay_copy():
        return remote(decay, decay_in, small_sem, (0,), tm=partner)

    def channel_copy():
        return remote(frame_decay, channel_in, small_sem, (1,), head=1 - h)

    def clip_copy():
        return remote(clip_out, clip_in, small_sem, (2,), tm=t + 1)

    def pair_copy(i):
        return remote(pair_out.at[i, 1 - odd], pair_in.at[i], pair_sem, (i,), tm=partner)

    def ring_copy(r, i):
        return remote(ring_out.at[r, i], ring_in.at[r, i], ring_sem, (r, i), tm=t + 2)

    def back_copy(i):
        return remote(back_out.at[i], back_in.at[i], back_sem, (i,), tm=partner)

    def placed(i):
        return out_any.at[:, pl.ds(pl.multiple_of(h * half + i * ROWS, ROWS), ROWS), :]

    def out_copy(i):
        return remote(result.at[i, 1 - h], placed(i), out_sem, (i,), head=1 - h)

    def keep_copy(i):
        return pltpu.make_async_copy(result.at[i, h], placed(i), keep_sem.at[i])

    def quarters(stage, p, fresh, **device):
        few = pl.ds(pl.multiple_of(p * (local // 4), local // 4), local // 4)
        many = pl.ds(pl.multiple_of(p * (width // 4), width // 4), width // 4)
        places = [mix_w.at[1, few], recur_w.at[1, :, many, :], emit_w.at[1, few]]
        sources = places
        if fresh:
            sources = [mix_any.at[few], recur_any.at[:, many, :], emit_any.at[few]]
        return [
            remote(a, b, weight_sem, (stage, k), **device)
            for k, (a, b) in enumerate(zip(sources, places))
        ]

    part = 2 * pair_parity + core
    facing = 2 * (1 - pair_parity) + core

    def over_y():
        return quarters(0, part, True, head=1 - h)

    def over_core():
        return quarters(1, part, False, clip=1 - core)

    def over_z():
        return quarters(2, part, False, tm=across)

    def onward():
        return quarters(3, facing, False, clip=1 - core)

    loads = [(x_any.at[f], x.at[f]) for f in range(frames)]
    loads[1:1] = [(attend_any, attend_w)]
    early = 2
    loads += [(mix_any, mix_w.at[0]), (recur_any, recur_w.at[0]), (emit_any, emit_w.at[0])]
    loads = [pltpu.make_async_copy(a, b, load_sem.at[k]) for k, (a, b) in enumerate(loads)]
    for load in loads:
        load.start()

    barrier = pltpu.get_barrier_semaphore()

    def greet(**device):
        pl.semaphore_signal(barrier, inc=1, device_id=device, device_id_type=MESH)

    greet(head=1 - h)
    greet(clip=1 - core)
    for there, step in ((has_after, 1), (has_before, -1), (has_next, 2), (has_prev, -2)):

        @pl.when(there)
        def _():
            greet(tm=t + step)

    near = [has_after, has_before, has_next, has_prev]
    pl.semaphore_wait(barrier, 2 + sum(there.astype(jnp.int32) for there in near))

    for copy in over_y():
        copy.start()
    channel_copy().start()
    for f in range(frames):
        clip_out[f : f + 1] = jnp.full((1, clip_out.shape[1]), clip[f], jnp.int32)

    @pl.when(has_after)
    def _():
        clip_copy().start()

    @pl.when(t < 2)
    def _():
        ring_in[...] = jnp.zeros_like(ring_in)

    @pl.when(t < 1)
    def _():
        clip_in[...] = jnp.full(clip_in.shape, -1, jnp.int32)

    def prepare():
        channel_copy().wait()

        @pl.when(has_before)
        def _():
            clip_copy().wait_recv()

        @pl.when(has_after)
        def _():
            clip_copy().wait_send()

        logs = jnp.concatenate([frame_decay[...], channel_in[...]], axis=1)
        retain = jnp.exp(logs)
        coef[...] = jnp.sqrt(1.0 - retain * retain)
        before = clip_in[last : last + 1]
        product = None
        for f in range(frames):
            now = clip_out[f : f + 1]
            follows = jnp.where(now == before, 1.0, 0.0)
            follows = jnp.concatenate([follows] * (width // follows.shape[1]), axis=1)
            here = retain[f : f + 1] * follows
            product = here if f == 0 else product * here
            factor[f : f + 1] = here
            decay[f : f + 1] = product
            before = now
        decay_copy().start()

    two = 2 * HEAD_DIMENSION

    def attend_step(g):
        f = lax.div(g, steps)
        step = lax.rem(g, steps)

        @pl.when(step == 0)
        def _():
            @pl.loop(0, positions // ROWS)
            def _(i):
                values = x[f, chunk(i)].astype(F32)
                scale = lax.rsqrt(jnp.mean(values * values, axis=-1, keepdims=True) + EPSILON)
                normed[chunk(i)] = (values * scale).astype(BF16)

        line = slots_ref[pl.ds(g, 1)]
        column = jnp.transpose(jnp.broadcast_to(line, (8, line.shape[1])))[:rows_step, :1]
        tokens = lax.broadcasted_iota(jnp.int32, (rows_step, positions), 1)
        pick = jnp.where(column == tokens, 1.0, 0.0).astype(BF16)
        gathered = dot(pick, normed[...]).astype(BF16)
        queries = (dot(gathered, attend_w[0]) * (HEAD_DIMENSION**-0.5)).astype(BF16)
        keys = dot(gathered, attend_w[1]).astype(BF16)
        values = dot(gathered, attend_w[2]).astype(BF16)

        first = lax.broadcasted_iota(jnp.int32, (BLOCK, two), 1) < HEAD_DIMENSION
        row = lax.broadcasted_iota(jnp.int32, (2 * BLOCK, BLOCK), 0)
        row = jnp.where(row >= BLOCK, row - BLOCK, row)
        column = lax.broadcasted_iota(jnp.int32, (2 * BLOCK, BLOCK), 1)
        same = ((row < WINDOW) & (column < WINDOW)) | (
            (row >= WINDOW) & (column >= WINDOW) & (column < PAIR)
        )
        for block in range(STEP_BLOCKS):
            low = block * BLOCK
            for lane in range(0, local, two):
                q = queries[low : low + BLOCK, lane : lane + two]
                k = keys[low : low + BLOCK, lane : lane + two]
                v = values[low : low + BLOCK, lane : lane + two]
                none = jnp.zeros_like(q)
                both = jnp.concatenate(
                    [jnp.where(first, q, none), jnp.where(first, none, q)], axis=0
                )
                scores = lax.dot_general(
                    both, k, (((1,), (1,)), ((), ())), preferred_element_type=F32
                )
                scores = jnp.where(same, scores, -1e30)
                raised = jnp.exp(scores - jnp.max(scores, axis=-1, keepdims=True))
                weights = raised * (1.0 / jnp.sum(raised, axis=-1, keepdims=True))
                mixed = dot(weights.astype(BF16), v)
                mixed = jnp.where(first, mixed[:BLOCK], mixed[BLOCK:]).astype(BF16)
                at = pl.ds(pl.multiple_of(step * rows_step + low, BLOCK), BLOCK)
                blended[at, lane : lane + two] = mixed

        @pl.when(step == steps - 1)
        def _():
            slots = blended.shape[0]

            def put_back(side, i):
                token = lax.broadcasted_iota(jnp.int32, (ROWS, slots), 0) + (side * half + i * ROWS)
                put = jnp.where(token == rows_ref[pl.ds(f, 1)], 1.0, 0.0).astype(BF16)
                return dot(put, blended[...]).astype(BF16)

            @pl.loop(0, 2 * chunks)
            def _(i):
                away = i < chunks
                j = lax.rem(i, chunks)
                block = put_back(jnp.where(away, 1 - h, h), j)

                @pl.when(away)
                def _():
                    theirs[f, j] = block
                    y_copy(f, j).start()

                @pl.when(jnp.logical_not(away))
                def _():
                    own[f, chunk(j)] = block

    for load in loads[:early]:
        load.wait()

    @pl.loop(0, frames * steps)
    def _(g):
        @pl.when(g == 1)
        def _():
            prepare()

        @pl.when(g == 3)
        def _():
            for copy in over_y():
                copy.wait_recv()
            for copy in over_core() + over_z():
                copy.start()

        @pl.when(g == steps)
        def _():
            loads[early].wait()

        @pl.when(g == frames * steps - 2)
        def _():
            for copy in over_z():
                copy.wait_recv()
            for copy in onward():
                copy.start()

        attend_step(g)

    for load in loads[early + 1 :]:
        load.wait()
    for f in range(last):

        @pl.loop(0, chunks)
        def _(i):
            y_copy(f, i).wait_recv()

    for copy in over_core() + onward():
        copy.wait_recv()
    decay_copy().wait()

    is_odd = odd == 1

    def halves(ref):
        low, high = ref[last : last + 1, :local], ref[last : last + 1, local:]
        return jnp.where(is_odd, high, low)

    def decays():
        here, there = halves(decay), halves(decay_in)
        return jnp.where(is_odd, there, here), jnp.where(is_odd, here, there)

    def order(i):
        here, there = pair_out[i, odd].astype(F32), pair_in[i].astype(F32)
        return jnp.where(is_odd, there, here), jnp.where(is_odd, here, there)

    def drive_step(i):
        y_copy(last, i).wait_recv()
        left = jnp.concatenate([own[f, chunk(i)] for f in range(frames)], axis=0)
        right = jnp.concatenate([arrived[f, i] for f in range(frames)], axis=0)
        mix = dot(left, mix_w[0]).astype(BF16).astype(F32)
        mix = mix + dot(right, mix_w[1]).astype(BF16).astype(F32)
        at = pl.ds(pl.multiple_of(h * half + i * ROWS, ROWS), ROWS)
        total = jnp.concatenate([x[f, at].astype(F32) for f in range(frames)], axis=0) + mix
        residual[i] = total
        scale = lax.rsqrt(jnp.mean(total * total, axis=-1, keepdims=True) + EPSILON)
        again = (total * scale).astype(BF16)
        for low in range(0, width, COLUMNS):
            side, lanes = low // local, slice(low % local, low % local + COLUMNS)
            wide = slice(low, low + COLUMNS)
            gate_in = jax.nn.sigmoid(dot(again, recur_w[side, 0, :, lanes]))
            drive_in = gate_in * dot(again, recur_w[side, 1, :, lanes])
            opened = dot(again, recur_w[side, 2, :, lanes])
            gate[i, :, wide] = (opened * jax.nn.sigmoid(opened)).astype(BF16)
            state = None
            for f in range(frames):
                here = slice(f * ROWS, (f + 1) * ROWS)
                driven = coef[f : f + 1, wide] * drive_in[here]
                state = driven if f == 0 else factor[f : f + 1, wide] * state + driven
                states[i, here, wide] = state.astype(BF16)
            pair_out[i, side, :, lanes] = state.astype(BF16)
        pair_copy(i).start()

    def ring_step(r, i):
        earlier_decay, later_decay = decays()
        if r == 0:
            pair_copy(i).wait_recv()
            earlier, later = order(i)
            total = later_decay * earlier + later
            merged[i] = total
        else:

            @pl.when(has_prev)
            def _():
                ring_copy(r - 1, i).wait_recv()

            entering = ring_in[r - 1, i].astype(F32)
            total = merged[i] + (earlier_decay * later_decay) * entering

        @pl.when(has_next)
        def _():
            ring_out[r, i] = total.astype(BF16)
            ring_copy(r, i).start()

    def back_step(i):
        @pl.when(has_prev)
        def _():
            ring_copy(rounds - 1, i).wait_recv()

        entering = ring_in[rounds - 1, i]
        earlier, _ = order(i)
        second = (earlier + decays()[0] * entering.astype(F32)).astype(BF16)
        back_keep[i] = jnp.where(is_odd, second, entering)
        back_out[i] = jnp.where(is_odd, entering, second)
        back_copy(i).start()

    def emit_step(i):
        back_copy(i).wait_recv()
        here, there = back_keep[i], back_in[i]
        incoming = (jnp.where(is_odd, there, here), jnp.where(is_odd, here, there))
        sides = []
        for side in range(2):
            wide = slice(side * local, (side + 1) * local)
            coming = incoming[side].astype(F32)
            parts = []
            for f in range(frames):
                rows = slice(f * ROWS, (f + 1) * ROWS)
                state = states[i, rows, wide].astype(F32) + decay[f : f + 1, wide] * coming
                parts.append((state * gate[i, rows, wide].astype(F32)).astype(BF16))
            sides.append(jnp.concatenate(parts, axis=0))
        for side in range(2):
            wide = slice(side * local, (side + 1) * local)
            mix = dot(sides[0], emit_w[0, :, wide]).astype(BF16).astype(F32)
            mix = mix + dot(sides[1], emit_w[1, :, wide]).astype(BF16).astype(F32)
            done = (residual[i, :, wide] + mix).astype(BF16)
            for f in range(frames):
                result[i, side, f] = done[f * ROWS : (f + 1) * ROWS]
        out_copy(i).start()
        keep_copy(i).start()

    @pl.loop(0, chunks + rounds + 2)
    def _(tick):
        @pl.when(tick < chunks)
        def _():
            drive_step(tick)

        for lag in range(1, rounds + 3):
            i = tick - lag

            @pl.when((i >= 0) & (i < chunks))
            def _():
                if lag <= rounds:
                    ring_step(lag - 1, i)
                elif lag == rounds + 1:
                    back_step(i)
                else:
                    emit_step(i)

    @pl.loop(0, chunks)
    def _(i):
        for f in range(frames):
            y_copy(f, i).wait_send()
        pair_copy(i).wait_send()
        back_copy(i).wait_send()
        keep_copy(i).wait()

        @pl.when(has_next)
        def _():
            for r in range(rounds):
                ring_copy(r, i).wait_send()

        out_copy(i).wait()

    for copy in over_y() + over_core() + over_z() + onward():
        copy.wait_send()


def whole_block(clip_id, video_tokens, order, weights, frame_decay):
    frames, positions, width = video_tokens.shape
    local = frame_decay.shape[1]
    half = positions // 2
    chunks = half // ROWS
    pairs = lax.axis_size("tm") // 2
    rounds = min(pairs - 1, -(-(LONGEST_CLIP - 1) // (2 * frames)))
    rows = frames * ROWS
    slots = order.shape[1]
    step = STEP_BLOCKS * BLOCK
    lines = jnp.pad(order.reshape(-1, step), ((0, 0), (0, -step % 128)), constant_values=-1)
    dma = pltpu.SemaphoreType.DMA
    anywhere = pl.BlockSpec(memory_space=pl.ANY)
    many = 1 + len(weights)
    return pl.pallas_call(
        functools.partial(block_kernel, frames, rounds),
        in_specs=[pl.BlockSpec(memory_space=pltpu.SMEM)] + [anywhere] * many + [held()] * 3,
        out_specs=anywhere,
        out_shape=jax.ShapeDtypeStruct((frames, positions, local), BF16),
        scratch_shapes=[
            pltpu.VMEM((frames, positions, width), BF16),
            pltpu.VMEM((3, width, local), BF16),
            pltpu.VMEM((positions, width), BF16),
            pltpu.VMEM((slots, local), BF16),
            pltpu.VMEM((frames, half, local), BF16),
            pltpu.VMEM((frames, chunks, ROWS, local), BF16),
            pltpu.VMEM((frames, chunks, ROWS, local), BF16),
            pltpu.VMEM((2, local, width), BF16),
            pltpu.VMEM((2, 3, width, local), BF16),
            pltpu.VMEM((2, local, width), BF16),
            pltpu.VMEM((chunks, rows, width), F32),
            pltpu.VMEM((chunks, rows, width), BF16),
            pltpu.VMEM((chunks, rows, width), BF16),
            pltpu.VMEM((chunks, 2, ROWS, local), BF16),
            pltpu.VMEM((chunks, ROWS, local), BF16),
            pltpu.VMEM((chunks, ROWS, local), F32),
            pltpu.VMEM((rounds, chunks, ROWS, local), BF16),
            pltpu.VMEM((rounds, chunks, ROWS, local), BF16),
            pltpu.VMEM((chunks, ROWS, local), BF16),
            pltpu.VMEM((chunks, ROWS, local), BF16),
            pltpu.VMEM((chunks, ROWS, local), BF16),
            pltpu.VMEM((chunks, 2, frames, ROWS, local), BF16),
            pltpu.VMEM((frames, width), F32),
            pltpu.VMEM((frames, width), F32),
            pltpu.VMEM((frames, width), F32),
            pltpu.VMEM((frames, width), F32),
            pltpu.VMEM((frames, local), F32),
            pltpu.VMEM((frames, 128), jnp.int32),
            pltpu.VMEM((frames, 128), jnp.int32),
            dma((frames + 4,)),
            dma((2, 4, 3)),
            dma((2, 3)),
            dma((2, frames, chunks)),
            dma((2, chunks)),
            dma((2, rounds, chunks)),
            dma((2, chunks)),
            dma((2, chunks)),
            dma((chunks,)),
        ],
        compiler_params=pltpu.CompilerParams(
            vmem_limit_bytes=VMEM_LIMIT, collective_id=0, has_side_effects=True
        ),
        cost_estimate=pl.CostEstimate(
            flops=30 * frames * half * width * width,
            bytes_accessed=frames * half * width * 12,
            transcendentals=2 * frames * half * width,
        ),
        name="block",
    )(clip_id, video_tokens, *weights, lines, order, frame_decay)


def per_device(
    video_tokens,
    window_order,
    clip_id,
    attend_weight,
    attend_out,
    recur_weight,
    frame_decay,
    recur_out,
):
    frames, positions, _ = video_tokens.shape
    order = window_order.reshape(frames, positions // PAIR, PAIR)
    order = jnp.pad(order, ((0, 0), (0, 0), (0, BLOCK - PAIR)), constant_values=-1)
    order = order.reshape(frames, -1)
    weights = (attend_weight, attend_out, recur_weight, recur_out)
    return whole_block(clip_id, video_tokens, order, weights, frame_decay)


def from_behind(value, axis, steps):
    count = lax.axis_size(axis)
    leading, last = (max(0, -steps), min(count, count - steps))
    return lax.ppermute(value, axis, [(source, source + steps) for source in range(leading, last)])


def prefix_2(value, axis, combine, identity):
    count, position = (lax.axis_size(axis), lax.axis_index(axis))
    everything = jax.tree.map(
        lambda part, kind: lax.all_gather(part.astype(kind), axis),
        value,
        (jnp.bfloat16, jnp.bfloat16),
    )
    start = jax.tree.map(
        lambda part, zero: jnp.broadcast_to(jnp.asarray(zero, part.dtype), part.shape),
        value,
        identity,
    )

    def hop(k, before):
        reached = k < position
        new = combine(
            before, jax.tree.map(lambda part, own: part[k].astype(own.dtype), everything, value)
        )
        return jax.tree.map(lambda a, b: jnp.where(reached, a, b), new, before)

    return lax.fori_loop(0, count, hop, start)


def normalize(values):
    return values * lax.rsqrt(jnp.mean(values * values, axis=-1, keepdims=True) + EPSILON)


def window_attention(queries, keys_all, values_all, window_order):
    frame_count, positions, number_of_heads, head_size = queries.shape
    order_index = window_order[:, :, None, None]

    def arrange(tensor):
        reordered = jnp.take_along_axis(tensor, order_index, axis=1)
        return reordered.reshape(
            frame_count, positions // WINDOW, WINDOW, number_of_heads, head_size
        )

    scores = jnp.einsum(
        "fwihe,fwjhe->fwhij",
        arrange(queries),
        arrange(keys_all),
        preferred_element_type=jnp.float32,
    ) / jnp.sqrt(jnp.float32(head_size))
    weights = jax.nn.softmax(scores, axis=-1).astype(jnp.bfloat16)
    blended = jnp.einsum(
        "fwhij,fwjhe->fwihe", weights, arrange(values_all), preferred_element_type=jnp.float32
    ).astype(jnp.bfloat16)
    blended = blended.reshape(frame_count, positions, number_of_heads, head_size)
    inverse = jnp.argsort(window_order, axis=1)
    return jnp.take_along_axis(blended, inverse[:, :, None, None], axis=1)


def per_device_any(
    video_tokens,
    window_order,
    clip_id,
    attend_weight,
    attend_out,
    recur_weight,
    frame_decay,
    recur_out,
):
    frame_count, positions, model_width = video_tokens.shape
    local_width = attend_weight.shape[2]
    row_count = frame_count * positions
    inputs = video_tokens.reshape(row_count, model_width).astype(jnp.float32)
    normed = normalize(inputs).astype(jnp.bfloat16)
    projected = jnp.einsum(
        "td,kde->kte", normed, attend_weight, preferred_element_type=jnp.float32
    ).astype(jnp.bfloat16)
    shaped = projected.reshape(
        3, frame_count, positions, local_width // HEAD_DIMENSION, HEAD_DIMENSION
    )
    attended = window_attention(shaped[0], shaped[1], shaped[2], window_order).reshape(
        row_count, local_width
    )
    partial_mix = jnp.dot(attended, attend_out, preferred_element_type=jnp.float32)
    offset = lax.axis_index("head") * local_width
    residual = inputs + lax.psum(partial_mix.astype(jnp.bfloat16), "head").astype(jnp.float32)
    normed_again = normalize(residual).astype(jnp.bfloat16)
    recur_proj = jnp.einsum(
        "td,kde->kte", normed_again, recur_weight, preferred_element_type=jnp.float32
    )
    residual_own = lax.dynamic_slice_in_dim(residual, offset, local_width, 1)
    gate_in = jax.nn.sigmoid(recur_proj[0]).reshape(frame_count, positions, local_width)
    value_in = recur_proj[1].reshape(frame_count, positions, local_width)
    out_gate = jax.nn.silu(recur_proj[2]).reshape(frame_count, positions, local_width)
    retain = jnp.exp(frame_decay)
    driven = jnp.sqrt(1.0 - retain * retain)[:, None, :] * gate_in * value_in
    previous = from_behind(clip_id[frame_count - 1 :], "tm", 1)
    continues = jnp.concatenate(
        [
            (clip_id[:1] == previous).astype(jnp.float32),
            (clip_id[1:] == clip_id[:-1]).astype(jnp.float32),
        ]
    )
    factor = retain * continues[:, None]

    def advance(carried, inputs_now):
        decay_total, state_now = carried
        factor_now, driven_now = inputs_now
        decay_total = factor_now * decay_total
        state_now = factor_now[None, :] * state_now + driven_now
        return ((decay_total, state_now), (decay_total, state_now))

    start_carry = (
        jnp.ones((local_width,), jnp.float32),
        jnp.zeros((positions, local_width), jnp.float32),
    )
    last_carry, all_carry = lax.scan(advance, start_carry, (factor, driven))
    decay_last, state_last = last_carry
    decay_all, state_all = all_carry

    def combine(earlier, later_part):
        return (later_part[0] * earlier[0], later_part[0][None, :] * earlier[1] + later_part[1])

    prefix = prefix_2(
        (decay_last, state_last),
        "tm",
        combine,
        (jnp.ones_like(decay_last), jnp.zeros_like(state_last)),
    )
    incoming = prefix[1]
    states = state_all + decay_all[:, None, :] * incoming[None, :, :]
    output_rows = (states * out_gate).astype(jnp.bfloat16).reshape(row_count, local_width)
    partial_out = jnp.dot(output_rows, recur_out, preferred_element_type=jnp.float32)
    result = residual_own + lax.psum_scatter(
        partial_out.astype(jnp.bfloat16), "head", scatter_dimension=1, tiled=True
    ).astype(jnp.float32)
    return result.astype(jnp.bfloat16).reshape(frame_count, positions, local_width)


def solution(mesh):
    halves = mesh.shape["head"] == 2 and mesh.shape["clip"] == 2 and mesh.shape["tm"] % 4 == 0
    return jax.shard_map(
        per_device if halves else per_device_any,
        mesh=mesh,
        in_specs=(
            P(("clip", "tm"), None, None),
            P(("clip", "tm"), None),
            P(("clip", "tm")),
            P(None, None, "head"),
            P("head", None),
            P(None, None, "head"),
            P(("clip", "tm"), "head"),
            P("head", None),
        ),
        out_specs=P(("clip", "tm"), None, "head"),
        check_vma=False,
    )
```

```python
import functools

import jax
import jax.numpy as jnp
from jax import lax
from jax.experimental import pallas as pl
from jax.experimental.pallas import tpu as pltpu
from jax.sharding import PartitionSpec as P

HEAD_DIMENSION = 64
WINDOW = 49
LONGEST_CLIP = 8
EPSILON = 1e-06

PAIR = 2 * WINDOW
BLOCK = 112
LANES = 128
STEP_BLOCKS = 4
ROWS = 112

F32, BF16 = jnp.float32, jnp.bfloat16
VMEM_LIMIT = 67043328
COLUMNS = 256
PIECES = 5
MESH = pl.DeviceIdType.MESH


def dot(a, b):
    return jnp.dot(a, b, preferred_element_type=F32)


def held():
    return pl.BlockSpec(memory_space=pltpu.VMEM)


def block_kernel(frames, rounds, *refs):
    refs = list(refs)

    def take(count):
        taken, refs[:count] = refs[:count], []
        return taken

    (clip,) = take(1)
    x_any, attend_any, mix_any, recur_any, emit_any = take(5)
    slots_ref, frame_decay = take(2)
    (out_any,) = take(1)
    x, attend_w, normed, blended, own, theirs, arrived = take(7)
    mix_w, recur_w, emit_w, residual, gate, states = take(6)
    pair_out, pair_in, merged, ring_out, ring_in = take(5)
    back_out, back_keep, back_in, result = take(4)
    coef, factor, decay, decay_in, channel_in, clip_out, clip_in = take(7)
    load_sem, weight_sem, small_sem, y_sem, pair_sem, ring_sem, back_sem, out_sem, keep_sem = take(9)

    core, t, h = (lax.axis_index(name) for name in ("clip", "tm", "head"))
    count = lax.axis_size("tm")
    odd = lax.rem(t, 2)
    has_next, has_prev = t + 2 < count, t >= 2
    has_after, has_before = t + 1 < count, t >= 1
    chunks = arrived.shape[1]
    half = chunks * ROWS
    positions, width = x.shape[1:]
    local = own.shape[2]
    steps = slots_ref.shape[0] // (frames * STEP_BLOCKS)
    partner = t + 1 - 2 * odd
    pair_parity = lax.rem(lax.div(t, 2), 2)
    across = t + 2 - 4 * pair_parity
    last = frames - 1

    def remote(src, dst, sems, at, **device):
        return pltpu.make_async_remote_copy(
            src_ref=src,
            dst_ref=dst,
            send_sem=sems.at[(0, *at)],
            recv_sem=sems.at[(1, *at)],
            device_id=device,
            device_id_type=MESH,
        )

    def chunk(i):
        return pl.ds(pl.multiple_of(i * ROWS, ROWS), ROWS)

    def y_copy(f, i):
        return remote(theirs.at[f, i], arrived.at[f, i], y_sem, (f, i), head=1 - h)

    def decay_copy():
        return remote(decay, decay_in, small_sem, (0,), tm=partner)

    def channel_copy():
        return remote(frame_decay, channel_in, small_sem, (1,), head=1 - h)

    def clip_copy():
        return remote(clip_out, clip_in, small_sem, (2,), tm=t + 1)

    def pair_copy(i):
        return remote(pair_out.at[i, 1 - odd], pair_in.at[i], pair_sem, (i,), tm=partner)

    def ring_copy(r, i):
        return remote(ring_out.at[r, i], ring_in.at[r, i], ring_sem, (r, i), tm=t + 2)

    def back_copy(i):
        return remote(back_out.at[i], back_in.at[i], back_sem, (i,), tm=partner)

    def placed(i):
        return out_any.at[:, pl.ds(pl.multiple_of(h * half + i * ROWS, ROWS), ROWS), :]

    def out_copy(i):
        return remote(result.at[i, 1 - h], placed(i), out_sem, (i,), head=1 - h)

    def keep_copy(i):
        return pltpu.make_async_copy(result.at[i, h], placed(i), keep_sem.at[i])

    def quarter(stage, k, p, fresh, **device):
        few = pl.ds(pl.multiple_of(p * (local // 4), local // 4), local // 4)
        many = pl.ds(pl.multiple_of(p * (width // 4), width // 4), width // 4)
        places = [mix_w.at[1, few]] + [recur_w.at[1, j, many] for j in range(3)]
        places += [emit_w.at[1, few]]
        sources = [mix_any.at[few]] + [recur_any.at[j, many] for j in range(3)]
        sources += [emit_any.at[few]]
        source = sources[k] if fresh else places[k]
        return remote(source, places[k], weight_sem, (stage, k), **device)

    part = 2 * pair_parity + core
    facing = 2 * (1 - pair_parity) + core

    def over_y(k):
        return quarter(0, k, part, True, head=1 - h)

    def over_core(k):
        return quarter(1, k, part, False, clip=1 - core)

    def over_z(k):
        return quarter(2, k, part, False, tm=across)

    def onward(k):
        return quarter(3, k, facing, False, clip=1 - core)

    loads = [(x_any.at[f], x.at[f]) for f in range(frames)]
    loads[1:1] = [(attend_any, attend_w)]
    early = 2
    loads += [(mix_any, mix_w.at[0]), (recur_any, recur_w.at[0]), (emit_any, emit_w.at[0])]
    loads = [pltpu.make_async_copy(a, b, load_sem.at[k]) for k, (a, b) in enumerate(loads)]
    for load in loads:
        load.start()

    barrier = pltpu.get_barrier_semaphore()

    def greet(**device):
        pl.semaphore_signal(barrier, inc=1, device_id=device, device_id_type=MESH)

    greet(head=1 - h)
    greet(clip=1 - core)
    for there, step in ((has_after, 1), (has_before, -1), (has_next, 2), (has_prev, -2)):

        @pl.when(there)
        def _():
            greet(tm=t + step)

    near = [has_after, has_before, has_next, has_prev]
    pl.semaphore_wait(barrier, 2 + sum(there.astype(jnp.int32) for there in near))

    channel_copy().start()
    for f in range(frames):
        clip_out[f : f + 1] = jnp.full((1, clip_out.shape[1]), clip[f], jnp.int32)

    @pl.when(has_after)
    def _():
        clip_copy().start()

    for k in range(PIECES):
        over_y(k).start()

    @pl.when(t < 2)
    def _():
        ring_in[...] = jnp.zeros_like(ring_in)

    @pl.when(t < 1)
    def _():
        clip_in[...] = jnp.full(clip_in.shape, -1, jnp.int32)

    def prepare():
        channel_copy().wait()

        @pl.when(has_before)
        def _():
            clip_copy().wait_recv()

        @pl.when(has_after)
        def _():
            clip_copy().wait_send()

        logs = jnp.concatenate([frame_decay[...], channel_in[...]], axis=1)
        retain = jnp.exp(logs)
        coef[...] = jnp.sqrt(1.0 - retain * retain)
        before = clip_in[last : last + 1]
        product = None
        for f in range(frames):
            now = clip_out[f : f + 1]
            follows = jnp.where(now == before, 1.0, 0.0)
            follows = jnp.concatenate([follows] * (width // follows.shape[1]), axis=1)
            here = retain[f : f + 1] * follows
            product = here if f == 0 else product * here
            factor[f : f + 1] = here
            decay[f : f + 1] = product
            before = now
        decay_copy().start()

    two = 2 * HEAD_DIMENSION
    cuts = (0, chunks - chunks // 2, chunks)

    def attend_step(g):
        f = lax.div(g, steps)
        step = lax.rem(g, steps)

        @pl.when(step == 0)
        def _():
            @pl.loop(0, positions // ROWS)
            def _(i):
                values = x[f, chunk(i)].astype(F32)
                scale = lax.rsqrt(jnp.mean(values * values, axis=-1, keepdims=True) + EPSILON)
                normed[chunk(i)] = (values * scale).astype(BF16)

        lines = [slots_ref[pl.ds(g * STEP_BLOCKS + b, 1)] for b in range(STEP_BLOCKS)]
        lines = jnp.transpose(jnp.concatenate(lines * (8 // STEP_BLOCKS), axis=0))
        tokens = lax.broadcasted_iota(jnp.int32, (BLOCK, positions), 1)
        pick = jnp.concatenate(
            [
                jnp.where(lines[:BLOCK, b : b + 1] == tokens, 1.0, 0.0).astype(BF16)
                for b in range(STEP_BLOCKS)
            ],
            axis=0,
        )
        gathered = dot(pick, normed[...]).astype(BF16)
        queries = (dot(gathered, attend_w[0]) * (HEAD_DIMENSION**-0.5)).astype(BF16)
        keys = dot(gathered, attend_w[1]).astype(BF16)
        values = dot(gathered, attend_w[2]).astype(BF16)

        first = lax.broadcasted_iota(jnp.int32, (BLOCK, two), 1) < HEAD_DIMENSION
        wide_first = lax.broadcasted_iota(jnp.int32, (BLOCK, 2 * two), 1)
        wide_first = lax.rem(wide_first, two) < HEAD_DIMENSION
        ones = jnp.ones((BLOCK, two), BF16)
        row = lax.broadcasted_iota(jnp.int32, (2 * BLOCK, BLOCK), 0)
        row = jnp.where(row >= BLOCK, row - BLOCK, row)
        column = lax.broadcasted_iota(jnp.int32, (2 * BLOCK, BLOCK), 1)
        same = ((row < WINDOW) & (column < WINDOW)) | (
            (row >= WINDOW) & (column >= WINDOW) & (column < PAIR)
        )
        for block in range(STEP_BLOCKS):
            low = block * BLOCK
            for lane in range(0, local, two):
                q = queries[low : low + BLOCK, lane : lane + two]
                k = keys[low : low + BLOCK, lane : lane + two]
                v = values[low : low + BLOCK, lane : lane + two]
                none = jnp.zeros_like(q)
                both = jnp.concatenate(
                    [jnp.where(first, q, none), jnp.where(first, none, q)], axis=0
                )
                scores = lax.dot_general(
                    both, k, (((1,), (1,)), ((), ())), preferred_element_type=F32
                )
                scores = jnp.where(same, scores, -1e30)
                raised = jnp.exp(scores - jnp.max(scores, axis=-1, keepdims=True))
                mixed = dot(raised.astype(BF16), jnp.concatenate([v, ones], axis=1))
                mixed = jnp.where(wide_first, mixed[:BLOCK], mixed[BLOCK:])
                mixed = mixed[:, :two] * (1.0 / mixed[:, two:])
                at = pl.ds(pl.multiple_of((step * STEP_BLOCKS + block) * LANES, LANES), BLOCK)
                blended[at, lane : lane + two] = mixed.astype(BF16)

        @pl.when(step == steps - 1)
        def _():
            slots = blended.shape[0]
            line = [slots_ref[pl.ds(f * (slots // LANES) + b, 1)] for b in range(slots // LANES)]
            line = jnp.concatenate(line, axis=1)

            @pl.loop(0, 2)
            def _(turn):
                side = jnp.where(turn == 0, 1 - h, h)
                for begin, end in zip(cuts, cuts[1:]):
                    size = (end - begin) * ROWS
                    token = lax.broadcasted_iota(jnp.int32, (size, slots), 0)
                    put = jnp.where(token + (side * half + begin * ROWS) == line, 1.0, 0.0)
                    block = dot(put.astype(BF16), blended[...]).astype(BF16)

                    @pl.when(turn == 0)
                    def _():
                        for j in range(begin, end):
                            theirs[f, j] = block[(j - begin) * ROWS : (j - begin + 1) * ROWS]
                            y_copy(f, j).start()

                    @pl.when(turn == 1)
                    def _():
                        own[f, begin * ROWS : end * ROWS] = block

    blended[...] = jnp.zeros_like(blended)
    for load in loads[:early]:
        load.wait()

    @pl.loop(0, frames * steps)
    def _(g):
        @pl.when(g == 1)
        def _():
            prepare()

        for k in range(PIECES):

            @pl.when(g == k + 1)
            def _():
                over_y(k).wait_recv()
                over_core(k).start()
                over_z(k).start()

            @pl.when(g == k + 3)
            def _():
                over_z(k).wait_recv()
                onward(k).start()

        @pl.when(g == steps)
        def _():
            loads[early].wait()

        attend_step(g)

    for load in loads[early + 1 :]:
        load.wait()
    for f in range(last):

        @pl.loop(0, chunks)
        def _(i):
            y_copy(f, i).wait_recv()

    for k in range(PIECES):
        over_core(k).wait_recv()
        onward(k).wait_recv()
    decay_copy().wait()

    is_odd = odd == 1

    def halves(ref):
        low, high = ref[last : last + 1, :local], ref[last : last + 1, local:]
        return jnp.where(is_odd, high, low)

    def decays():
        here, there = halves(decay), halves(decay_in)
        return jnp.where(is_odd, there, here), jnp.where(is_odd, here, there)

    def order(i):
        here, there = pair_out[i, odd].astype(F32), pair_in[i].astype(F32)
        return jnp.where(is_odd, there, here), jnp.where(is_odd, here, there)

    def drive_step(i):
        y_copy(last, i).wait_recv()
        left = jnp.concatenate([own[f, chunk(i)] for f in range(frames)], axis=0)
        right = jnp.concatenate([arrived[f, i] for f in range(frames)], axis=0)
        mix = dot(left, mix_w[0]).astype(BF16).astype(F32)
        mix = mix + dot(right, mix_w[1]).astype(BF16).astype(F32)
        at = pl.ds(pl.multiple_of(h * half + i * ROWS, ROWS), ROWS)
        total = jnp.concatenate([x[f, at].astype(F32) for f in range(frames)], axis=0) + mix
        residual[i] = total
        scale = lax.rsqrt(jnp.mean(total * total, axis=-1, keepdims=True) + EPSILON)
        again = (total * scale).astype(BF16)
        for low in range(0, width, COLUMNS):
            side, lanes = low // local, slice(low % local, low % local + COLUMNS)
            wide = slice(low, low + COLUMNS)
            gate_in = jax.nn.sigmoid(dot(again, recur_w[side, 0, :, lanes]))
            drive_in = gate_in * dot(again, recur_w[side, 1, :, lanes])
            opened = dot(again, recur_w[side, 2, :, lanes])
            gate[i, :, wide] = (opened * jax.nn.sigmoid(opened)).astype(BF16)
            state = None
            for f in range(frames):
                here = slice(f * ROWS, (f + 1) * ROWS)
                driven = coef[f : f + 1, wide] * drive_in[here]
                state = driven if f == 0 else factor[f : f + 1, wide] * state + driven
                states[i, here, wide] = state.astype(BF16)
            pair_out[i, side, :, lanes] = state.astype(BF16)
        pair_copy(i).start()

    def ring_step(r, i):
        earlier_decay, later_decay = decays()
        if r == 0:
            pair_copy(i).wait_recv()
            earlier, later = order(i)
            total = later_decay * earlier + later
            merged[i] = total
        else:

            @pl.when(has_prev)
            def _():
                ring_copy(r - 1, i).wait_recv()

            entering = ring_in[r - 1, i].astype(F32)
            total = merged[i] + (earlier_decay * later_decay) * entering

        @pl.when(has_next)
        def _():
            ring_out[r, i] = total.astype(BF16)
            ring_copy(r, i).start()

    def back_step(i):
        @pl.when(has_prev)
        def _():
            ring_copy(rounds - 1, i).wait_recv()

        entering = ring_in[rounds - 1, i]
        earlier, _ = order(i)
        second = (earlier + decays()[0] * entering.astype(F32)).astype(BF16)
        back_keep[i] = jnp.where(is_odd, second, entering)
        back_out[i] = jnp.where(is_odd, entering, second)
        back_copy(i).start()

    def emit_step(i):
        back_copy(i).wait_recv()
        here, there = back_keep[i], back_in[i]
        incoming = (jnp.where(is_odd, there, here), jnp.where(is_odd, here, there))
        sides = []
        for side in range(2):
            wide = slice(side * local, (side + 1) * local)
            coming = incoming[side].astype(F32)
            parts = []
            for f in range(frames):
                rows = slice(f * ROWS, (f + 1) * ROWS)
                state = states[i, rows, wide].astype(F32) + decay[f : f + 1, wide] * coming
                parts.append((state * gate[i, rows, wide].astype(F32)).astype(BF16))
            sides.append(jnp.concatenate(parts, axis=0))
        for side in range(2):
            wide = slice(side * local, (side + 1) * local)
            mix = dot(sides[0], emit_w[0, :, wide]).astype(BF16).astype(F32)
            mix = mix + dot(sides[1], emit_w[1, :, wide]).astype(BF16).astype(F32)
            done = (residual[i, :, wide] + mix).astype(BF16)
            for f in range(frames):
                result[i, side, f] = done[f * ROWS : (f + 1) * ROWS]
        out_copy(i).start()
        keep_copy(i).start()

    @pl.loop(0, chunks + rounds + 2)
    def _(tick):
        @pl.when(tick < chunks)
        def _():
            drive_step(tick)

        for lag in range(1, rounds + 3):
            i = tick - lag

            @pl.when((i >= 0) & (i < chunks))
            def _():
                if lag <= rounds:
                    ring_step(lag - 1, i)
                elif lag == rounds + 1:
                    back_step(i)
                else:
                    emit_step(i)

    @pl.loop(0, chunks)
    def _(i):
        for f in range(frames):
            y_copy(f, i).wait_send()
        pair_copy(i).wait_send()
        back_copy(i).wait_send()
        keep_copy(i).wait()

        @pl.when(has_next)
        def _():
            for r in range(rounds):
                ring_copy(r, i).wait_send()

        out_copy(i).wait()

    for k in range(PIECES):
        for copy in (over_y, over_core, over_z, onward):
            copy(k).wait_send()


def whole_block(clip_id, video_tokens, order, weights, frame_decay):
    frames, positions, width = video_tokens.shape
    local = frame_decay.shape[1]
    half = positions // 2
    chunks = half // ROWS
    pairs = lax.axis_size("tm") // 2
    rounds = min(pairs - 1, -(-(LONGEST_CLIP - 1) // (2 * frames)))
    rows = frames * ROWS
    slots = order.size // frames
    dma = pltpu.SemaphoreType.DMA
    anywhere = pl.BlockSpec(memory_space=pl.ANY)
    many = 1 + len(weights)
    return pl.pallas_call(
        functools.partial(block_kernel, frames, rounds),
        in_specs=[pl.BlockSpec(memory_space=pltpu.SMEM)] + [anywhere] * many + [held()] * 2,
        out_specs=anywhere,
        out_shape=jax.ShapeDtypeStruct((frames, positions, local), BF16),
        scratch_shapes=[
            pltpu.VMEM((frames, positions, width), BF16),
            pltpu.VMEM((3, width, local), BF16),
            pltpu.VMEM((positions, width), BF16),
            pltpu.VMEM((slots, local), BF16),
            pltpu.VMEM((frames, half, local), BF16),
            pltpu.VMEM((frames, chunks, ROWS, local), BF16),
            pltpu.VMEM((frames, chunks, ROWS, local), BF16),
            pltpu.VMEM((2, local, width), BF16),
            pltpu.VMEM((2, 3, width, local), BF16),
            pltpu.VMEM((2, local, width), BF16),
            pltpu.VMEM((chunks, rows, width), F32),
            pltpu.VMEM((chunks, rows, width), BF16),
            pltpu.VMEM((chunks, rows, width), BF16),
            pltpu.VMEM((chunks, 2, ROWS, local), BF16),
            pltpu.VMEM((chunks, ROWS, local), BF16),
            pltpu.VMEM((chunks, ROWS, local), F32),
            pltpu.VMEM((rounds, chunks, ROWS, local), BF16),
            pltpu.VMEM((rounds, chunks, ROWS, local), BF16),
            pltpu.VMEM((chunks, ROWS, local), BF16),
            pltpu.VMEM((chunks, ROWS, local), BF16),
            pltpu.VMEM((chunks, ROWS, local), BF16),
            pltpu.VMEM((chunks, 2, frames, ROWS, local), BF16),
            pltpu.VMEM((frames, width), F32),
            pltpu.VMEM((frames, width), F32),
            pltpu.VMEM((frames, width), F32),
            pltpu.VMEM((frames, width), F32),
            pltpu.VMEM((frames, local), F32),
            pltpu.VMEM((frames, 128), jnp.int32),
            pltpu.VMEM((frames, 128), jnp.int32),
            dma((frames + 4,)),
            dma((2, 4, PIECES)),
            dma((2, 3)),
            dma((2, frames, chunks)),
            dma((2, chunks)),
            dma((2, rounds, chunks)),
            dma((2, chunks)),
            dma((2, chunks)),
            dma((chunks,)),
        ],
        compiler_params=pltpu.CompilerParams(
            vmem_limit_bytes=VMEM_LIMIT, collective_id=0, has_side_effects=True
        ),
        cost_estimate=pl.CostEstimate(
            flops=30 * frames * half * width * width,
            bytes_accessed=frames * half * width * 12,
            transcendentals=2 * frames * half * width,
        ),
        name="block",
    )(clip_id, video_tokens, *weights, order, frame_decay)


def per_device(
    video_tokens,
    window_order,
    clip_id,
    attend_weight,
    attend_out,
    recur_weight,
    frame_decay,
    recur_out,
):
    frames, positions, _ = video_tokens.shape
    order = window_order.reshape(frames * (positions // PAIR), PAIR)
    order = jnp.pad(order, ((0, 0), (0, LANES - PAIR)), constant_values=-1)
    weights = (attend_weight, attend_out, recur_weight, recur_out)
    return whole_block(clip_id, video_tokens, order, weights, frame_decay)


def from_behind(value, axis, steps):
    count = lax.axis_size(axis)
    leading, last = (max(0, -steps), min(count, count - steps))
    return lax.ppermute(value, axis, [(source, source + steps) for source in range(leading, last)])


def prefix_2(value, axis, combine, identity):
    count, position = (lax.axis_size(axis), lax.axis_index(axis))
    everything = jax.tree.map(
        lambda part, kind: lax.all_gather(part.astype(kind), axis),
        value,
        (jnp.bfloat16, jnp.bfloat16),
    )
    start = jax.tree.map(
        lambda part, zero: jnp.broadcast_to(jnp.asarray(zero, part.dtype), part.shape),
        value,
        identity,
    )

    def hop(k, before):
        reached = k < position
        new = combine(
            before, jax.tree.map(lambda part, own: part[k].astype(own.dtype), everything, value)
        )
        return jax.tree.map(lambda a, b: jnp.where(reached, a, b), new, before)

    return lax.fori_loop(0, count, hop, start)


def normalize(values):
    return values * lax.rsqrt(jnp.mean(values * values, axis=-1, keepdims=True) + EPSILON)


def window_attention(queries, keys_all, values_all, window_order):
    frame_count, positions, number_of_heads, head_size = queries.shape
    order_index = window_order[:, :, None, None]

    def arrange(tensor):
        reordered = jnp.take_along_axis(tensor, order_index, axis=1)
        return reordered.reshape(
            frame_count, positions // WINDOW, WINDOW, number_of_heads, head_size
        )

    scores = jnp.einsum(
        "fwihe,fwjhe->fwhij",
        arrange(queries),
        arrange(keys_all),
        preferred_element_type=jnp.float32,
    ) / jnp.sqrt(jnp.float32(head_size))
    weights = jax.nn.softmax(scores, axis=-1).astype(jnp.bfloat16)
    blended = jnp.einsum(
        "fwhij,fwjhe->fwihe", weights, arrange(values_all), preferred_element_type=jnp.float32
    ).astype(jnp.bfloat16)
    blended = blended.reshape(frame_count, positions, number_of_heads, head_size)
    inverse = jnp.argsort(window_order, axis=1)
    return jnp.take_along_axis(blended, inverse[:, :, None, None], axis=1)


def per_device_any(
    video_tokens,
    window_order,
    clip_id,
    attend_weight,
    attend_out,
    recur_weight,
    frame_decay,
    recur_out,
):
    frame_count, positions, model_width = video_tokens.shape
    local_width = attend_weight.shape[2]
    row_count = frame_count * positions
    inputs = video_tokens.reshape(row_count, model_width).astype(jnp.float32)
    normed = normalize(inputs).astype(jnp.bfloat16)
    projected = jnp.einsum(
        "td,kde->kte", normed, attend_weight, preferred_element_type=jnp.float32
    ).astype(jnp.bfloat16)
    shaped = projected.reshape(
        3, frame_count, positions, local_width // HEAD_DIMENSION, HEAD_DIMENSION
    )
    attended = window_attention(shaped[0], shaped[1], shaped[2], window_order).reshape(
        row_count, local_width
    )
    partial_mix = jnp.dot(attended, attend_out, preferred_element_type=jnp.float32)
    offset = lax.axis_index("head") * local_width
    residual = inputs + lax.psum(partial_mix.astype(jnp.bfloat16), "head").astype(jnp.float32)
    normed_again = normalize(residual).astype(jnp.bfloat16)
    recur_proj = jnp.einsum(
        "td,kde->kte", normed_again, recur_weight, preferred_element_type=jnp.float32
    )
    residual_own = lax.dynamic_slice_in_dim(residual, offset, local_width, 1)
    gate_in = jax.nn.sigmoid(recur_proj[0]).reshape(frame_count, positions, local_width)
    value_in = recur_proj[1].reshape(frame_count, positions, local_width)
    out_gate = jax.nn.silu(recur_proj[2]).reshape(frame_count, positions, local_width)
    retain = jnp.exp(frame_decay)
    driven = jnp.sqrt(1.0 - retain * retain)[:, None, :] * gate_in * value_in
    previous = from_behind(clip_id[frame_count - 1 :], "tm", 1)
    continues = jnp.concatenate(
        [
            (clip_id[:1] == previous).astype(jnp.float32),
            (clip_id[1:] == clip_id[:-1]).astype(jnp.float32),
        ]
    )
    factor = retain * continues[:, None]

    def advance(carried, inputs_now):
        decay_total, state_now = carried
        factor_now, driven_now = inputs_now
        decay_total = factor_now * decay_total
        state_now = factor_now[None, :] * state_now + driven_now
        return ((decay_total, state_now), (decay_total, state_now))

    start_carry = (
        jnp.ones((local_width,), jnp.float32),
        jnp.zeros((positions, local_width), jnp.float32),
    )
    last_carry, all_carry = lax.scan(advance, start_carry, (factor, driven))
    decay_last, state_last = last_carry
    decay_all, state_all = all_carry

    def combine(earlier, later_part):
        return (later_part[0] * earlier[0], later_part[0][None, :] * earlier[1] + later_part[1])

    prefix = prefix_2(
        (decay_last, state_last),
        "tm",
        combine,
        (jnp.ones_like(decay_last), jnp.zeros_like(state_last)),
    )
    incoming = prefix[1]
    states = state_all + decay_all[:, None, :] * incoming[None, :, :]
    output_rows = (states * out_gate).astype(jnp.bfloat16).reshape(row_count, local_width)
    partial_out = jnp.dot(output_rows, recur_out, preferred_element_type=jnp.float32)
    result = residual_own + lax.psum_scatter(
        partial_out.astype(jnp.bfloat16), "head", scatter_dimension=1, tiled=True
    ).astype(jnp.float32)
    return result.astype(jnp.bfloat16).reshape(frame_count, positions, local_width)


def solution(mesh):
    halves = mesh.shape["head"] == 2 and mesh.shape["clip"] == 2 and mesh.shape["tm"] % 4 == 0
    return jax.shard_map(
        per_device if halves else per_device_any,
        mesh=mesh,
        in_specs=(
            P(("clip", "tm"), None, None),
            P(("clip", "tm"), None),
            P(("clip", "tm")),
            P(None, None, "head"),
            P("head", None),
            P(None, None, "head"),
            P(("clip", "tm"), "head"),
            P("head", None),
        ),
        out_specs=P(("clip", "tm"), None, "head"),
        check_vma=False,
    )
```

```python
import functools

import jax
import jax.numpy as jnp
from jax import lax
from jax.experimental import pallas as pl
from jax.experimental.pallas import tpu as pltpu
from jax.sharding import PartitionSpec as P

HEAD_DIMENSION = 64
WINDOW = 49
LONGEST_CLIP = 8
EPSILON = 1e-06

PAIR = 2 * WINDOW
BLOCK = 112
LANES = 128
STEP_BLOCKS = 4
ROWS = 112

F32, BF16 = jnp.float32, jnp.bfloat16
VMEM_LIMIT = 67043328
COLUMNS = 256
PIECES = 5
MESH = pl.DeviceIdType.MESH


def dot(a, b):
    return jnp.dot(a, b, preferred_element_type=F32)


def held():
    return pl.BlockSpec(memory_space=pltpu.VMEM)


def block_kernel(frames, rounds, *refs):
    refs = list(refs)

    def take(count):
        taken, refs[:count] = refs[:count], []
        return taken

    clip, starts = take(2)
    x_any, attend_any, mix_any, recur_any, emit_any = take(5)
    slots_ref, frame_decay = take(2)
    (out_any,) = take(1)
    x, attend_w, normed, gathered, blended, own, theirs, arrived = take(8)
    mix_w, recur_w, emit_w, residual, gate, states = take(6)
    pair_out, pair_in, merged, ring_out, ring_in = take(5)
    back_out, back_keep, back_in, result = take(4)
    coef, factor, decay, decay_in, channel_in, clip_out, clip_in = take(7)
    load_sem, weight_sem, small_sem, y_sem, pair_sem, ring_sem, back_sem, out_sem, keep_sem = take(9)

    core, t, h = (lax.axis_index(name) for name in ("clip", "tm", "head"))
    count = lax.axis_size("tm")
    odd = lax.rem(t, 2)
    has_next, has_prev = t + 2 < count, t >= 2
    has_after, has_before = t + 1 < count, t >= 1
    chunks = arrived.shape[1]
    half = chunks * ROWS
    positions, width = x.shape[1:]
    local = own.shape[2]
    steps = slots_ref.shape[0] // (frames * STEP_BLOCKS)
    partner = t + 1 - 2 * odd
    pair_parity = lax.rem(lax.div(t, 2), 2)
    across = t + 2 - 4 * pair_parity
    last = frames - 1

    def remote(src, dst, sems, at, **device):
        return pltpu.make_async_remote_copy(
            src_ref=src,
            dst_ref=dst,
            send_sem=sems.at[(0, *at)],
            recv_sem=sems.at[(1, *at)],
            device_id=device,
            device_id_type=MESH,
        )

    def chunk(i):
        return pl.ds(pl.multiple_of(i * ROWS, ROWS), ROWS)

    def y_copy(f, i):
        return remote(theirs.at[f, i], arrived.at[f, i], y_sem, (f, i), head=1 - h)

    def decay_copy():
        return remote(decay, decay_in, small_sem, (0,), tm=partner)

    def channel_copy():
        return remote(frame_decay, channel_in, small_sem, (1,), head=1 - h)

    def clip_copy():
        return remote(clip_out, clip_in, small_sem, (2,), tm=t + 1)

    def pair_copy(i):
        return remote(pair_out.at[i, 1 - odd], pair_in.at[i], pair_sem, (i,), tm=partner)

    def ring_copy(r, i):
        return remote(ring_out.at[r, i], ring_in.at[r, i], ring_sem, (r, i), tm=t + 2)

    def back_copy(i):
        return remote(back_out.at[i], back_in.at[i], back_sem, (i,), tm=partner)

    def placed(i):
        return out_any.at[:, pl.ds(pl.multiple_of(h * half + i * ROWS, ROWS), ROWS), :]

    def out_copy(i):
        return remote(result.at[i, 1 - h], placed(i), out_sem, (i,), head=1 - h)

    def keep_copy(i):
        return pltpu.make_async_copy(result.at[i, h], placed(i), keep_sem.at[i])

    def quarter(stage, k, p, fresh, **device):
        few = pl.ds(pl.multiple_of(p * (local // 4), local // 4), local // 4)
        many = pl.ds(pl.multiple_of(p * (width // 4), width // 4), width // 4)
        places = [mix_w.at[1, few]] + [recur_w.at[1, j, many] for j in range(3)]
        places += [emit_w.at[1, few]]
        sources = [mix_any.at[few]] + [recur_any.at[j, many] for j in range(3)]
        sources += [emit_any.at[few]]
        source = sources[k] if fresh else places[k]
        return remote(source, places[k], weight_sem, (stage, k), **device)

    part = 2 * pair_parity + core
    facing = 2 * (1 - pair_parity) + core

    def over_y(k):
        return quarter(0, k, part, True, head=1 - h)

    def over_core(k):
        return quarter(1, k, part, False, clip=1 - core)

    def over_z(k):
        return quarter(2, k, part, False, tm=across)

    def onward(k):
        return quarter(3, k, facing, False, clip=1 - core)

    loads = [(x_any.at[f], x.at[f]) for f in range(frames)]
    loads[1:1] = [(attend_any, attend_w)]
    early = 2
    loads += [(mix_any, mix_w.at[0]), (recur_any, recur_w.at[0]), (emit_any, emit_w.at[0])]
    loads = [pltpu.make_async_copy(a, b, load_sem.at[k]) for k, (a, b) in enumerate(loads)]
    for load in loads:
        load.start()

    barrier = pltpu.get_barrier_semaphore()

    def greet(**device):
        pl.semaphore_signal(barrier, inc=1, device_id=device, device_id_type=MESH)

    greet(head=1 - h)
    greet(clip=1 - core)
    for there, step in ((has_after, 1), (has_before, -1), (has_next, 2), (has_prev, -2)):

        @pl.when(there)
        def _():
            greet(tm=t + step)

    near = [has_after, has_before, has_next, has_prev]
    pl.semaphore_wait(barrier, 2 + sum(there.astype(jnp.int32) for there in near))

    channel_copy().start()
    for f in range(frames):
        clip_out[f : f + 1] = jnp.full((1, clip_out.shape[1]), clip[f], jnp.int32)

    @pl.when(has_after)
    def _():
        clip_copy().start()

    for k in range(PIECES):
        over_y(k).start()

    @pl.when(t < 2)
    def _():
        ring_in[...] = jnp.zeros_like(ring_in)

    @pl.when(t < 1)
    def _():
        clip_in[...] = jnp.full(clip_in.shape, -1, jnp.int32)

    def prepare():
        channel_copy().wait()

        @pl.when(has_before)
        def _():
            clip_copy().wait_recv()

        @pl.when(has_after)
        def _():
            clip_copy().wait_send()

        logs = jnp.concatenate([frame_decay[...], channel_in[...]], axis=1)
        retain = jnp.exp(logs)
        coef[...] = jnp.sqrt(1.0 - retain * retain)
        before = clip_in[last : last + 1]
        product = None
        for f in range(frames):
            now = clip_out[f : f + 1]
            follows = jnp.where(now == before, 1.0, 0.0)
            follows = jnp.concatenate([follows] * (width // follows.shape[1]), axis=1)
            here = retain[f : f + 1] * follows
            product = here if f == 0 else product * here
            factor[f : f + 1] = here
            decay[f : f + 1] = product
            before = now
        decay_copy().start()

    two = 2 * HEAD_DIMENSION
    tiles = width // LANES
    cuts = (0, chunks - chunks // 2, chunks)

    def attend_step(g):
        f = lax.div(g, steps)
        step = lax.rem(g, steps)

        @pl.when(step == 0)
        def _():
            @pl.loop(0, positions // ROWS)
            def _(i):
                values = x[f, chunk(i)].astype(F32)
                scale = lax.rsqrt(jnp.mean(values * values, axis=-1, keepdims=True) + EPSILON)
                values = (values * scale).reshape(ROWS // 8, 8, width)
                values = [values[:, :, k * LANES : (k + 1) * LANES] for k in range(tiles)]
                values = jnp.stack(values, axis=1).reshape(ROWS * tiles, LANES)
                normed[pl.ds(pl.multiple_of(i * (ROWS * tiles), 8), ROWS * tiles)] = values

        def fetch_row(block, i, k):
            start = starts[f, (step * STEP_BLOCKS + block) * PAIR + i * 8 + k]
            there = pl.ds(i * (8 * tiles) + (block * BLOCK * tiles + k), tiles, stride=8)
            gathered[there, :] = normed[pl.ds(start, tiles, stride=8), :]

        @pl.loop(0, PAIR // 8)
        def _(i):
            for block in range(STEP_BLOCKS):
                for k in range(8):
                    fetch_row(block, i, k)

        for block in range(STEP_BLOCKS):
            for k in range(PAIR % 8):
                fetch_row(block, PAIR // 8, k)

        rows = gathered[...].reshape(-1, tiles, 8, LANES)
        rows = [rows[:, k].reshape(STEP_BLOCKS * BLOCK, LANES) for k in range(tiles)]
        rows = jnp.concatenate(rows, axis=1).astype(BF16)
        queries = (dot(rows, attend_w[0]) * (HEAD_DIMENSION**-0.5)).astype(BF16)
        keys = dot(rows, attend_w[1]).astype(BF16)
        values = dot(rows, attend_w[2]).astype(BF16)

        first = lax.broadcasted_iota(jnp.int32, (LANES, two), 1) < HEAD_DIMENSION
        row = lax.broadcasted_iota(jnp.int32, (BLOCK, LANES), 0)
        column = lax.broadcasted_iota(jnp.int32, (BLOCK, LANES), 1)
        same = ((row < WINDOW) & (column < WINDOW)) | (
            (row >= WINDOW) & (column >= WINDOW) & (column < PAIR)
        )
        none = jnp.zeros((LANES, two), BF16)
        ones = jnp.ones((LANES, two), BF16)
        counted = (jnp.where(first, ones, none), jnp.where(first, none, ones))

        def padded(values, low, lane):
            few = jnp.zeros((LANES - BLOCK, two), values.dtype)
            return jnp.concatenate([values[low : low + BLOCK, lane : lane + two], few], axis=0)

        def split(values, low, lane):
            values = padded(values, low, lane)
            return jnp.where(first, values, none), jnp.where(first, none, values)

        def scored(low, lane):
            q = queries[low : low + BLOCK, lane : lane + two]
            k = jnp.concatenate(split(keys, low, lane), axis=0)
            return lax.dot_general(q, k, (((1,), (1,)), ((), ())), preferred_element_type=F32)

        def raised(scores):
            sides = []
            for head in range(2):
                part = jnp.where(same, scores[:, head * LANES : (head + 1) * LANES], -1e30)
                part = jnp.exp(part - jnp.max(part, axis=-1, keepdims=True))
                sides.append(part.astype(BF16))
            return jnp.concatenate(sides, axis=1)

        for block in range(STEP_BLOCKS):
            low = block * BLOCK
            at = pl.ds(pl.multiple_of((step * STEP_BLOCKS + block) * LANES, LANES), BLOCK)
            lanes = range(0, local, two)
            weights = [scored(low, lane) for lane in lanes]
            weights = [raised(scores) for scores in weights]
            for lane, weight in zip(lanes, weights):
                v = split(values, low, lane)
                v = [jnp.concatenate(pair, axis=1) for pair in zip(v, counted)]
                mixed = dot(weight, jnp.concatenate(v, axis=0))
                mixed = mixed[:, :two] * (1.0 / mixed[:, two:])
                blended[at, lane : lane + two] = mixed.astype(BF16)

        @pl.when(step == steps - 1)
        def _():
            slots = blended.shape[0]
            line = [slots_ref[pl.ds(f * (slots // LANES) + b, 1)] for b in range(slots // LANES)]
            line = jnp.concatenate(line, axis=1)

            @pl.loop(0, 2)
            def _(turn):
                side = jnp.where(turn == 0, 1 - h, h)
                for begin, end in zip(cuts, cuts[1:]):
                    size = (end - begin) * ROWS
                    token = lax.broadcasted_iota(jnp.int32, (size, slots), 0)
                    put = jnp.where(token + (side * half + begin * ROWS) == line, 1.0, 0.0)
                    block = dot(put.astype(BF16), blended[...]).astype(BF16)

                    @pl.when(turn == 0)
                    def _():
                        for j in range(begin, end):
                            theirs[f, j] = block[(j - begin) * ROWS : (j - begin + 1) * ROWS]
                            y_copy(f, j).start()

                    @pl.when(turn == 1)
                    def _():
                        own[f, begin * ROWS : end * ROWS] = block

    blended[...] = jnp.zeros_like(blended)
    gathered[...] = jnp.zeros_like(gathered)
    for load in loads[:early]:
        load.wait()

    @pl.loop(0, frames * steps)
    def _(g):
        @pl.when(g == 1)
        def _():
            prepare()

        for k in range(PIECES):

            @pl.when(g == k + 1)
            def _():
                over_y(k).wait_recv()
                over_core(k).start()
                over_z(k).start()

            @pl.when(g == k + 3)
            def _():
                over_z(k).wait_recv()
                onward(k).start()

        @pl.when(g == steps)
        def _():
            loads[early].wait()

        attend_step(g)

    for load in loads[early + 1 :]:
        load.wait()
    for f in range(last):

        @pl.loop(0, chunks)
        def _(i):
            y_copy(f, i).wait_recv()

    for k in range(PIECES):
        over_core(k).wait_recv()
        onward(k).wait_recv()
    decay_copy().wait()

    is_odd = odd == 1

    def halves(ref):
        low, high = ref[last : last + 1, :local], ref[last : last + 1, local:]
        return jnp.where(is_odd, high, low)

    def decays():
        here, there = halves(decay), halves(decay_in)
        return jnp.where(is_odd, there, here), jnp.where(is_odd, here, there)

    def order(i):
        here, there = pair_out[i, odd].astype(F32), pair_in[i].astype(F32)
        return jnp.where(is_odd, there, here), jnp.where(is_odd, here, there)

    def drive_step(i):
        y_copy(last, i).wait_recv()
        left = jnp.concatenate([own[f, chunk(i)] for f in range(frames)], axis=0)
        right = jnp.concatenate([arrived[f, i] for f in range(frames)], axis=0)
        mix = dot(left, mix_w[0]).astype(BF16).astype(F32)
        mix = mix + dot(right, mix_w[1]).astype(BF16).astype(F32)
        at = pl.ds(pl.multiple_of(h * half + i * ROWS, ROWS), ROWS)
        total = jnp.concatenate([x[f, at].astype(F32) for f in range(frames)], axis=0) + mix
        residual[i] = total
        scale = lax.rsqrt(jnp.mean(total * total, axis=-1, keepdims=True) + EPSILON)
        again = (total * scale).astype(BF16)
        for low in range(0, width, COLUMNS):
            side, lanes = low // local, slice(low % local, low % local + COLUMNS)
            wide = slice(low, low + COLUMNS)
            gate_in = jax.nn.sigmoid(dot(again, recur_w[side, 0, :, lanes]))
            drive_in = gate_in * dot(again, recur_w[side, 1, :, lanes])
            opened = dot(again, recur_w[side, 2, :, lanes])
            gate[i, :, wide] = (opened * jax.nn.sigmoid(opened)).astype(BF16)
            state = None
            for f in range(frames):
                here = slice(f * ROWS, (f + 1) * ROWS)
                driven = coef[f : f + 1, wide] * drive_in[here]
                state = driven if f == 0 else factor[f : f + 1, wide] * state + driven
                states[i, here, wide] = state.astype(BF16)
            pair_out[i, side, :, lanes] = state.astype(BF16)
        pair_copy(i).start()

    def ring_step(r, i):
        earlier_decay, later_decay = decays()
        if r == 0:
            pair_copy(i).wait_recv()
            earlier, later = order(i)
            total = later_decay * earlier + later
            merged[i] = total
        else:

            @pl.when(has_prev)
            def _():
                ring_copy(r - 1, i).wait_recv()

            entering = ring_in[r - 1, i].astype(F32)
            total = merged[i] + (earlier_decay * later_decay) * entering

        @pl.when(has_next)
        def _():
            ring_out[r, i] = total.astype(BF16)
            ring_copy(r, i).start()

    def back_step(i):
        @pl.when(has_prev)
        def _():
            ring_copy(rounds - 1, i).wait_recv()

        entering = ring_in[rounds - 1, i]
        earlier, _ = order(i)
        second = (earlier + decays()[0] * entering.astype(F32)).astype(BF16)
        back_keep[i] = jnp.where(is_odd, second, entering)
        back_out[i] = jnp.where(is_odd, entering, second)
        back_copy(i).start()

    def emit_step(i):
        back_copy(i).wait_recv()
        here, there = back_keep[i], back_in[i]
        incoming = (jnp.where(is_odd, there, here), jnp.where(is_odd, here, there))
        sides = []
        for side in range(2):
            wide = slice(side * local, (side + 1) * local)
            coming = incoming[side].astype(F32)
            parts = []
            for f in range(frames):
                rows = slice(f * ROWS, (f + 1) * ROWS)
                state = states[i, rows, wide].astype(F32) + decay[f : f + 1, wide] * coming
                parts.append((state * gate[i, rows, wide].astype(F32)).astype(BF16))
            sides.append(jnp.concatenate(parts, axis=0))
        for side in range(2):
            wide = slice(side * local, (side + 1) * local)
            mix = dot(sides[0], emit_w[0, :, wide]).astype(BF16).astype(F32)
            mix = mix + dot(sides[1], emit_w[1, :, wide]).astype(BF16).astype(F32)
            done = (residual[i, :, wide] + mix).astype(BF16)
            for f in range(frames):
                result[i, side, f] = done[f * ROWS : (f + 1) * ROWS]
        out_copy(i).start()
        keep_copy(i).start()

    @pl.loop(0, chunks + rounds + 2)
    def _(tick):
        @pl.when(tick < chunks)
        def _():
            drive_step(tick)

        for lag in range(1, rounds + 3):
            i = tick - lag

            @pl.when((i >= 0) & (i < chunks))
            def _():
                if lag <= rounds:
                    ring_step(lag - 1, i)
                elif lag == rounds + 1:
                    back_step(i)
                else:
                    emit_step(i)

    @pl.loop(0, chunks)
    def _(i):
        for f in range(frames):
            y_copy(f, i).wait_send()
        pair_copy(i).wait_send()
        back_copy(i).wait_send()
        keep_copy(i).wait()

        @pl.when(has_next)
        def _():
            for r in range(rounds):
                ring_copy(r, i).wait_send()

        out_copy(i).wait()

    for k in range(PIECES):
        for copy in (over_y, over_core, over_z, onward):
            copy(k).wait_send()


def whole_block(clip_id, starts, video_tokens, order, weights, frame_decay):
    frames, positions, width = video_tokens.shape
    local = frame_decay.shape[1]
    half = positions // 2
    chunks = half // ROWS
    pairs = lax.axis_size("tm") // 2
    rounds = min(pairs - 1, -(-(LONGEST_CLIP - 1) // (2 * frames)))
    rows = frames * ROWS
    slots = order.size // frames
    dma = pltpu.SemaphoreType.DMA
    anywhere = pl.BlockSpec(memory_space=pl.ANY)
    many = 1 + len(weights)
    return pl.pallas_call(
        functools.partial(block_kernel, frames, rounds),
        in_specs=[pl.BlockSpec(memory_space=pltpu.SMEM)] * 2 + [anywhere] * many + [held()] * 2,
        out_specs=anywhere,
        out_shape=jax.ShapeDtypeStruct((frames, positions, local), BF16),
        scratch_shapes=[
            pltpu.VMEM((frames, positions, width), BF16),
            pltpu.VMEM((3, width, local), BF16),
            pltpu.VMEM((positions * width // LANES, LANES), F32),
            pltpu.VMEM((STEP_BLOCKS * BLOCK * width // LANES, LANES), F32),
            pltpu.VMEM((slots, local), BF16),
            pltpu.VMEM((frames, half, local), BF16),
            pltpu.VMEM((frames, chunks, ROWS, local), BF16),
            pltpu.VMEM((frames, chunks, ROWS, local), BF16),
            pltpu.VMEM((2, local, width), BF16),
            pltpu.VMEM((2, 3, width, local), BF16),
            pltpu.VMEM((2, local, width), BF16),
            pltpu.VMEM((chunks, rows, width), F32),
            pltpu.VMEM((chunks, rows, width), BF16),
            pltpu.VMEM((chunks, rows, width), BF16),
            pltpu.VMEM((chunks, 2, ROWS, local), BF16),
            pltpu.VMEM((chunks, ROWS, local), BF16),
            pltpu.VMEM((chunks, ROWS, local), F32),
            pltpu.VMEM((rounds, chunks, ROWS, local), BF16),
            pltpu.VMEM((rounds, chunks, ROWS, local), BF16),
            pltpu.VMEM((chunks, ROWS, local), BF16),
            pltpu.VMEM((chunks, ROWS, local), BF16),
            pltpu.VMEM((chunks, ROWS, local), BF16),
            pltpu.VMEM((chunks, 2, frames, ROWS, local), BF16),
            pltpu.VMEM((frames, width), F32),
            pltpu.VMEM((frames, width), F32),
            pltpu.VMEM((frames, width), F32),
            pltpu.VMEM((frames, width), F32),
            pltpu.VMEM((frames, local), F32),
            pltpu.VMEM((frames, 128), jnp.int32),
            pltpu.VMEM((frames, 128), jnp.int32),
            dma((frames + 4,)),
            dma((2, 4, PIECES)),
            dma((2, 3)),
            dma((2, frames, chunks)),
            dma((2, chunks)),
            dma((2, rounds, chunks)),
            dma((2, chunks)),
            dma((2, chunks)),
            dma((chunks,)),
        ],
        compiler_params=pltpu.CompilerParams(
            vmem_limit_bytes=VMEM_LIMIT, collective_id=0, has_side_effects=True
        ),
        cost_estimate=pl.CostEstimate(
            flops=30 * frames * half * width * width,
            bytes_accessed=frames * half * width * 12,
            transcendentals=2 * frames * half * width,
        ),
        name="block",
    )(clip_id, starts, video_tokens, *weights, order, frame_decay)


def per_device(
    video_tokens,
    window_order,
    clip_id,
    attend_weight,
    attend_out,
    recur_weight,
    frame_decay,
    recur_out,
):
    frames, positions, width = video_tokens.shape
    order = window_order.reshape(frames * (positions // PAIR), PAIR)
    order = jnp.pad(order, ((0, 0), (0, LANES - PAIR)), constant_values=-1)
    weights = (attend_weight, attend_out, recur_weight, recur_out)
    tiles = width // LANES
    starts = window_order // 8 * (8 * tiles) + window_order % 8
    return whole_block(clip_id, starts, video_tokens, order, weights, frame_decay)


def from_behind(value, axis, steps):
    count = lax.axis_size(axis)
    leading, last = (max(0, -steps), min(count, count - steps))
    return lax.ppermute(value, axis, [(source, source + steps) for source in range(leading, last)])


def prefix_2(value, axis, combine, identity):
    count, position = (lax.axis_size(axis), lax.axis_index(axis))
    everything = jax.tree.map(
        lambda part, kind: lax.all_gather(part.astype(kind), axis),
        value,
        (jnp.bfloat16, jnp.bfloat16),
    )
    start = jax.tree.map(
        lambda part, zero: jnp.broadcast_to(jnp.asarray(zero, part.dtype), part.shape),
        value,
        identity,
    )

    def hop(k, before):
        reached = k < position
        new = combine(
            before, jax.tree.map(lambda part, own: part[k].astype(own.dtype), everything, value)
        )
        return jax.tree.map(lambda a, b: jnp.where(reached, a, b), new, before)

    return lax.fori_loop(0, count, hop, start)


def normalize(values):
    return values * lax.rsqrt(jnp.mean(values * values, axis=-1, keepdims=True) + EPSILON)


def window_attention(queries, keys_all, values_all, window_order):
    frame_count, positions, number_of_heads, head_size = queries.shape
    order_index = window_order[:, :, None, None]

    def arrange(tensor):
        reordered = jnp.take_along_axis(tensor, order_index, axis=1)
        return reordered.reshape(
            frame_count, positions // WINDOW, WINDOW, number_of_heads, head_size
        )

    scores = jnp.einsum(
        "fwihe,fwjhe->fwhij",
        arrange(queries),
        arrange(keys_all),
        preferred_element_type=jnp.float32,
    ) / jnp.sqrt(jnp.float32(head_size))
    weights = jax.nn.softmax(scores, axis=-1).astype(jnp.bfloat16)
    blended = jnp.einsum(
        "fwhij,fwjhe->fwihe", weights, arrange(values_all), preferred_element_type=jnp.float32
    ).astype(jnp.bfloat16)
    blended = blended.reshape(frame_count, positions, number_of_heads, head_size)
    inverse = jnp.argsort(window_order, axis=1)
    return jnp.take_along_axis(blended, inverse[:, :, None, None], axis=1)


def per_device_any(
    video_tokens,
    window_order,
    clip_id,
    attend_weight,
    attend_out,
    recur_weight,
    frame_decay,
    recur_out,
):
    frame_count, positions, model_width = video_tokens.shape
    local_width = attend_weight.shape[2]
    row_count = frame_count * positions
    inputs = video_tokens.reshape(row_count, model_width).astype(jnp.float32)
    normed = normalize(inputs).astype(jnp.bfloat16)
    projected = jnp.einsum(
        "td,kde->kte", normed, attend_weight, preferred_element_type=jnp.float32
    ).astype(jnp.bfloat16)
    shaped = projected.reshape(
        3, frame_count, positions, local_width // HEAD_DIMENSION, HEAD_DIMENSION
    )
    attended = window_attention(shaped[0], shaped[1], shaped[2], window_order).reshape(
        row_count, local_width
    )
    partial_mix = jnp.dot(attended, attend_out, preferred_element_type=jnp.float32)
    offset = lax.axis_index("head") * local_width
    residual = inputs + lax.psum(partial_mix.astype(jnp.bfloat16), "head").astype(jnp.float32)
    normed_again = normalize(residual).astype(jnp.bfloat16)
    recur_proj = jnp.einsum(
        "td,kde->kte", normed_again, recur_weight, preferred_element_type=jnp.float32
    )
    residual_own = lax.dynamic_slice_in_dim(residual, offset, local_width, 1)
    gate_in = jax.nn.sigmoid(recur_proj[0]).reshape(frame_count, positions, local_width)
    value_in = recur_proj[1].reshape(frame_count, positions, local_width)
    out_gate = jax.nn.silu(recur_proj[2]).reshape(frame_count, positions, local_width)
    retain = jnp.exp(frame_decay)
    driven = jnp.sqrt(1.0 - retain * retain)[:, None, :] * gate_in * value_in
    previous = from_behind(clip_id[frame_count - 1 :], "tm", 1)
    continues = jnp.concatenate(
        [
            (clip_id[:1] == previous).astype(jnp.float32),
            (clip_id[1:] == clip_id[:-1]).astype(jnp.float32),
        ]
    )
    factor = retain * continues[:, None]

    def advance(carried, inputs_now):
        decay_total, state_now = carried
        factor_now, driven_now = inputs_now
        decay_total = factor_now * decay_total
        state_now = factor_now[None, :] * state_now + driven_now
        return ((decay_total, state_now), (decay_total, state_now))

    start_carry = (
        jnp.ones((local_width,), jnp.float32),
        jnp.zeros((positions, local_width), jnp.float32),
    )
    last_carry, all_carry = lax.scan(advance, start_carry, (factor, driven))
    decay_last, state_last = last_carry
    decay_all, state_all = all_carry

    def combine(earlier, later_part):
        return (later_part[0] * earlier[0], later_part[0][None, :] * earlier[1] + later_part[1])

    prefix = prefix_2(
        (decay_last, state_last),
        "tm",
        combine,
        (jnp.ones_like(decay_last), jnp.zeros_like(state_last)),
    )
    incoming = prefix[1]
    states = state_all + decay_all[:, None, :] * incoming[None, :, :]
    output_rows = (states * out_gate).astype(jnp.bfloat16).reshape(row_count, local_width)
    partial_out = jnp.dot(output_rows, recur_out, preferred_element_type=jnp.float32)
    result = residual_own + lax.psum_scatter(
        partial_out.astype(jnp.bfloat16), "head", scatter_dimension=1, tiled=True
    ).astype(jnp.float32)
    return result.astype(jnp.bfloat16).reshape(frame_count, positions, local_width)


def solution(mesh):
    halves = mesh.shape["head"] == 2 and mesh.shape["clip"] == 2 and mesh.shape["tm"] % 4 == 0
    return jax.shard_map(
        per_device if halves else per_device_any,
        mesh=mesh,
        in_specs=(
            P(("clip", "tm"), None, None),
            P(("clip", "tm"), None),
            P(("clip", "tm")),
            P(None, None, "head"),
            P("head", None),
            P(None, None, "head"),
            P(("clip", "tm"), "head"),
            P("head", None),
        ),
        out_specs=P(("clip", "tm"), None, "head"),
        check_vma=False,
    )
```

```python
import functools

import jax
import jax.numpy as jnp
from jax import lax
from jax.experimental import pallas as pl
from jax.experimental.pallas import tpu as pltpu
from jax.sharding import PartitionSpec as P

HEAD_DIMENSION = 64
WINDOW = 49
LONGEST_CLIP = 8
EPSILON = 1e-06

PAIR = 2 * WINDOW
BLOCK = 112
LANES = 128
STEP_BLOCKS = 4
ROWS = 112

F32, BF16 = jnp.float32, jnp.bfloat16
VMEM_LIMIT = 67043328
COLUMNS = 256
PIECES = 5
GROUP = 2
MESH = pl.DeviceIdType.MESH


def dot(a, b):
    return jnp.dot(a, b, preferred_element_type=F32)


def held():
    return pl.BlockSpec(memory_space=pltpu.VMEM)


def block_kernel(frames, rounds, *refs):
    refs = list(refs)

    def take(count):
        taken, refs[:count] = refs[:count], []
        return taken

    (clip,) = take(1)
    x_any, attend_any, mix_any, recur_any, emit_any = take(5)
    order_ref, frame_decay = take(2)
    (out_any,) = take(1)
    slots_ref, order_starts, starts, order_sem = take(4)
    x, attend_w, normed, gathered, blended, own, theirs, arrived = take(8)
    mix_w, recur_w, emit_w, residual, gate, states = take(6)
    pair_out, pair_in, merged, ring_out, ring_in = take(5)
    back_out, back_keep, back_in, result = take(4)
    coef, factor, decay, decay_in, channel_in, clip_out, clip_in = take(7)
    load_sem, weight_sem, small_sem, y_sem, pair_sem, ring_sem, back_sem, out_sem, keep_sem = take(9)

    core, t, h = (lax.axis_index(name) for name in ("clip", "tm", "head"))
    count = lax.axis_size("tm")
    odd = lax.rem(t, 2)
    has_next, has_prev = t + 2 < count, t >= 2
    has_after, has_before = t + 1 < count, t >= 1
    chunks = arrived.shape[1]
    half = chunks * ROWS
    positions, width = x.shape[1:]
    local = own.shape[2]
    steps = slots_ref.shape[0] // (frames * STEP_BLOCKS)
    partner = t + 1 - 2 * odd
    pair_parity = lax.rem(lax.div(t, 2), 2)
    across = t + 2 - 4 * pair_parity
    last = frames - 1
    tiles = width // LANES

    def remote(src, dst, sems, at, **device):
        return pltpu.make_async_remote_copy(
            src_ref=src,
            dst_ref=dst,
            send_sem=sems.at[(0, *at)],
            recv_sem=sems.at[(1, *at)],
            device_id=device,
            device_id_type=MESH,
        )

    def chunk(i):
        return pl.ds(pl.multiple_of(i * ROWS, ROWS), ROWS)

    def y_copy(f, i):
        return remote(theirs.at[f, i], arrived.at[f, i], y_sem, (f, i), head=1 - h)

    def decay_copy():
        return remote(decay, decay_in, small_sem, (0,), tm=partner)

    def channel_copy():
        return remote(frame_decay, channel_in, small_sem, (1,), head=1 - h)

    def clip_copy():
        return remote(clip_out, clip_in, small_sem, (2,), tm=t + 1)

    def pair_copy(i):
        return remote(pair_out.at[i, 1 - odd], pair_in.at[i], pair_sem, (i,), tm=partner)

    def ring_copy(r, i):
        return remote(ring_out.at[r, i], ring_in.at[r, i], ring_sem, (r, i), tm=t + 2)

    def back_copy(i):
        return remote(back_out.at[i], back_in.at[i], back_sem, (i,), tm=partner)

    def placed(i):
        return out_any.at[:, pl.ds(pl.multiple_of(h * half + i * ROWS, ROWS), ROWS), :]

    def out_copy(i):
        return remote(result.at[i, 1 - h], placed(i), out_sem, (i,), head=1 - h)

    def keep_copy(i):
        return pltpu.make_async_copy(result.at[i, h], placed(i), keep_sem.at[i])

    def quarter(stage, k, p, fresh, **device):
        few = pl.ds(pl.multiple_of(p * (local // 4), local // 4), local // 4)
        many = pl.ds(pl.multiple_of(p * (width // 4), width // 4), width // 4)
        places = [mix_w.at[1, few]] + [recur_w.at[1, j, many] for j in range(3)]
        places += [emit_w.at[1, few]]
        sources = [mix_any.at[few]] + [recur_any.at[j, many] for j in range(3)]
        sources += [emit_any.at[few]]
        source = sources[k] if fresh else places[k]
        return remote(source, places[k], weight_sem, (stage, k), **device)

    part = 2 * pair_parity + core
    facing = 2 * (1 - pair_parity) + core

    def over_y(k):
        return quarter(0, k, part, True, head=1 - h)

    def over_core(k):
        return quarter(1, k, part, False, clip=1 - core)

    def over_z(k):
        return quarter(2, k, part, False, tm=across)

    def onward(k):
        return quarter(3, k, facing, False, clip=1 - core)

    loads = [(x_any.at[f], x.at[f]) for f in range(frames)]
    loads[1:1] = [(attend_any, attend_w)]
    early = 2
    loads += [(mix_any, mix_w.at[0]), (recur_any, recur_w.at[0]), (emit_any, emit_w.at[0])]
    loads = [pltpu.make_async_copy(a, b, load_sem.at[k]) for k, (a, b) in enumerate(loads)]
    for load in loads:
        load.start()

    order = order_ref[...]
    order_starts[...] = lax.div(order, 8) * (8 * tiles) + lax.rem(order, 8)
    starts_copy = pltpu.make_async_copy(order_starts, starts, order_sem)
    starts_copy.start()
    slots_ref[...] = jnp.full_like(slots_ref, -1)
    for f in range(frames):
        for block in range(positions // PAIR):
            piece = order[f : f + 1, block * PAIR : (block + 1) * PAIR]
            line = f * (positions // PAIR) + block
            slots_ref[line : line + 1, :PAIR] = piece

    barrier = pltpu.get_barrier_semaphore()

    def greet(**device):
        pl.semaphore_signal(barrier, inc=1, device_id=device, device_id_type=MESH)

    greet(head=1 - h)
    greet(clip=1 - core)
    for there, step in ((has_after, 1), (has_before, -1), (has_next, 2), (has_prev, -2)):

        @pl.when(there)
        def _():
            greet(tm=t + step)

    near = [has_after, has_before, has_next, has_prev]
    pl.semaphore_wait(barrier, 2 + sum(there.astype(jnp.int32) for there in near))

    channel_copy().start()
    for f in range(frames):
        clip_out[f : f + 1] = jnp.full((1, clip_out.shape[1]), clip[f], jnp.int32)

    @pl.when(has_after)
    def _():
        clip_copy().start()

    for k in range(PIECES):
        over_y(k).start()

    @pl.when(t < 2)
    def _():
        ring_in[...] = jnp.zeros_like(ring_in)

    @pl.when(t < 1)
    def _():
        clip_in[...] = jnp.full(clip_in.shape, -1, jnp.int32)

    def prepare():
        channel_copy().wait()

        @pl.when(has_before)
        def _():
            clip_copy().wait_recv()

        @pl.when(has_after)
        def _():
            clip_copy().wait_send()

        logs = jnp.concatenate([frame_decay[...], channel_in[...]], axis=1)
        retain = jnp.exp(logs)
        coef[...] = jnp.sqrt(1.0 - retain * retain)
        before = clip_in[last : last + 1]
        product = None
        for f in range(frames):
            now = clip_out[f : f + 1]
            follows = jnp.where(now == before, 1.0, 0.0)
            follows = jnp.concatenate([follows] * (width // follows.shape[1]), axis=1)
            here = retain[f : f + 1] * follows
            product = here if f == 0 else product * here
            factor[f : f + 1] = here
            decay[f : f + 1] = product
            before = now
        decay_copy().start()

    two = 2 * HEAD_DIMENSION
    cuts = (0, chunks - chunks // 2, chunks)

    def attend_step(g):
        f = lax.div(g, steps)
        step = lax.rem(g, steps)

        @pl.when(step == 0)
        def _():
            @pl.loop(0, positions // ROWS)
            def _(i):
                values = x[f, chunk(i)].astype(F32)
                scale = lax.rsqrt(jnp.mean(values * values, axis=-1, keepdims=True) + EPSILON)
                values = (values * scale).reshape(ROWS // 8, 8, width)
                values = [values[:, :, k * LANES : (k + 1) * LANES] for k in range(tiles)]
                values = jnp.stack(values, axis=1).reshape(ROWS * tiles, LANES)
                normed[pl.ds(pl.multiple_of(i * (ROWS * tiles), 8), ROWS * tiles)] = values

        def fetch_row(block, i, k):
            start = starts[f, (step * STEP_BLOCKS + block) * PAIR + i * 8 + k]
            there = pl.ds(i * (8 * tiles) + (block * BLOCK * tiles + k), tiles, stride=8)
            gathered[there, :] = normed[pl.ds(start, tiles, stride=8), :]

        @pl.loop(0, PAIR // 8)
        def _(i):
            for block in range(STEP_BLOCKS):
                for k in range(8):
                    fetch_row(block, i, k)

        for block in range(STEP_BLOCKS):
            for k in range(PAIR % 8):
                fetch_row(block, PAIR // 8, k)

        rows = gathered[...].reshape(-1, tiles, 8, LANES)
        rows = [rows[:, k].reshape(STEP_BLOCKS * BLOCK, LANES) for k in range(tiles)]
        rows = jnp.concatenate(rows, axis=1).astype(BF16)
        queries = (dot(rows, attend_w[0]) * (HEAD_DIMENSION**-0.5)).astype(BF16)
        keys = dot(rows, attend_w[1]).astype(BF16)
        values = dot(rows, attend_w[2]).astype(BF16)

        first = lax.broadcasted_iota(jnp.int32, (LANES, two), 1) < HEAD_DIMENSION
        row = lax.broadcasted_iota(jnp.int32, (BLOCK, LANES), 0)
        column = lax.broadcasted_iota(jnp.int32, (BLOCK, LANES), 1)
        same = ((row < WINDOW) & (column < WINDOW)) | (
            (row >= WINDOW) & (column >= WINDOW) & (column < PAIR)
        )
        lanes = range(0, local, two)
        none = jnp.zeros((LANES, two), BF16)
        ones = jnp.ones((LANES, two), BF16)
        counted = (jnp.where(first, ones, none), jnp.where(first, none, ones))

        def padded(values, low, lane):
            few = jnp.zeros((LANES - BLOCK, two), values.dtype)
            return jnp.concatenate([values[low : low + BLOCK, lane : lane + two], few], axis=0)

        def split(values, low, lane):
            values = padded(values, low, lane)
            return jnp.where(first, values, none), jnp.where(first, none, values)

        def scored(low, lane):
            q = queries[low : low + BLOCK, lane : lane + two]
            k = jnp.concatenate(split(keys, low, lane), axis=0)
            return lax.dot_general(q, k, (((1,), (1,)), ((), ())), preferred_element_type=F32)

        def raised(scores):
            sides = []
            for head in range(2):
                part = jnp.where(same, scores[:, head * LANES : (head + 1) * LANES], -1e30)
                part = jnp.exp(part - jnp.max(part, axis=-1, keepdims=True))
                sides.append(part.astype(BF16))
            return jnp.concatenate(sides, axis=1)

        for group in range(0, STEP_BLOCKS, GROUP):
            pairs = [(block, lane) for block in range(group, group + GROUP) for lane in lanes]
            weights = [scored(block * BLOCK, lane) for block, lane in pairs]
            weights = [raised(scores) for scores in weights]
            for (block, lane), weight in zip(pairs, weights):
                v = split(values, block * BLOCK, lane)
                v = [jnp.concatenate(pair, axis=1) for pair in zip(v, counted)]
                mixed = dot(weight, jnp.concatenate(v, axis=0))
                mixed = mixed[:, :two] * (1.0 / mixed[:, two:])
                at = pl.ds(pl.multiple_of((step * STEP_BLOCKS + block) * LANES, LANES), BLOCK)
                blended[at, lane : lane + two] = mixed.astype(BF16)

        @pl.when(step == steps - 1)
        def _():
            slots = blended.shape[0]
            line = [slots_ref[pl.ds(f * (slots // LANES) + b, 1)] for b in range(slots // LANES)]
            line = jnp.concatenate(line, axis=1)

            @pl.loop(0, 2)
            def _(turn):
                side = jnp.where(turn == 0, 1 - h, h)
                for begin, end in zip(cuts, cuts[1:]):
                    size = (end - begin) * ROWS
                    token = lax.broadcasted_iota(jnp.int32, (size, slots), 0)
                    put = jnp.where(token + (side * half + begin * ROWS) == line, 1.0, 0.0)
                    block = dot(put.astype(BF16), blended[...]).astype(BF16)

                    @pl.when(turn == 0)
                    def _():
                        for j in range(begin, end):
                            theirs[f, j] = block[(j - begin) * ROWS : (j - begin + 1) * ROWS]
                            y_copy(f, j).start()

                    @pl.when(turn == 1)
                    def _():
                        own[f, begin * ROWS : end * ROWS] = block

    blended[...] = jnp.zeros_like(blended)
    gathered[...] = jnp.zeros_like(gathered)
    for load in loads[:early]:
        load.wait()
    starts_copy.wait()

    @pl.loop(0, frames * steps)
    def _(g):
        @pl.when(g == 1)
        def _():
            prepare()

        for k in range(PIECES):

            @pl.when(g == k + 1)
            def _():
                over_y(k).wait_recv()
                over_core(k).start()
                over_z(k).start()

            @pl.when(g == k + 3)
            def _():
                over_z(k).wait_recv()
                onward(k).start()

        @pl.when(g == steps)
        def _():
            loads[early].wait()

        attend_step(g)

    for load in loads[early + 1 :]:
        load.wait()
    for f in range(last):

        @pl.loop(0, chunks)
        def _(i):
            y_copy(f, i).wait_recv()

    for k in range(PIECES):
        over_core(k).wait_recv()
        onward(k).wait_recv()
    decay_copy().wait()

    is_odd = odd == 1

    def halves(ref):
        low, high = ref[last : last + 1, :local], ref[last : last + 1, local:]
        return jnp.where(is_odd, high, low)

    def decays():
        here, there = halves(decay), halves(decay_in)
        return jnp.where(is_odd, there, here), jnp.where(is_odd, here, there)

    def order(i):
        here, there = pair_out[i, odd].astype(F32), pair_in[i].astype(F32)
        return jnp.where(is_odd, there, here), jnp.where(is_odd, here, there)

    def drive_step(i):
        y_copy(last, i).wait_recv()
        left = jnp.concatenate([own[f, chunk(i)] for f in range(frames)], axis=0)
        right = jnp.concatenate([arrived[f, i] for f in range(frames)], axis=0)
        mix = dot(left, mix_w[0]).astype(BF16).astype(F32)
        mix = mix + dot(right, mix_w[1]).astype(BF16).astype(F32)
        at = pl.ds(pl.multiple_of(h * half + i * ROWS, ROWS), ROWS)
        total = jnp.concatenate([x[f, at].astype(F32) for f in range(frames)], axis=0) + mix
        residual[i] = total
        scale = lax.rsqrt(jnp.mean(total * total, axis=-1, keepdims=True) + EPSILON)
        again = (total * scale).astype(BF16)
        for low in range(0, width, COLUMNS):
            side, lanes = low // local, slice(low % local, low % local + COLUMNS)
            wide = slice(low, low + COLUMNS)
            gate_in = jax.nn.sigmoid(dot(again, recur_w[side, 0, :, lanes]))
            drive_in = gate_in * dot(again, recur_w[side, 1, :, lanes])
            state = None
            for f in range(frames):
                here = slice(f * ROWS, (f + 1) * ROWS)
                driven = coef[f : f + 1, wide] * drive_in[here]
                state = driven if f == 0 else factor[f : f + 1, wide] * state + driven
                states[i, here, wide] = state.astype(BF16)
            pair_out[i, side, :, lanes] = state.astype(BF16)
        pair_copy(i).start()
        for low in range(0, width, COLUMNS):
            side, lanes = low // local, slice(low % local, low % local + COLUMNS)
            opened = dot(again, recur_w[side, 2, :, lanes])
            gate[i, :, low : low + COLUMNS] = (opened * jax.nn.sigmoid(opened)).astype(BF16)

    def ring_step(r, i):
        earlier_decay, later_decay = decays()
        if r == 0:
            pair_copy(i).wait_recv()
            earlier, later = order(i)
            total = later_decay * earlier + later
            merged[i] = total
        else:

            @pl.when(has_prev)
            def _():
                ring_copy(r - 1, i).wait_recv()

            entering = ring_in[r - 1, i].astype(F32)
            total = merged[i] + (earlier_decay * later_decay) * entering

        @pl.when(has_next)
        def _():
            ring_out[r, i] = total.astype(BF16)
            ring_copy(r, i).start()

    def back_step(i):
        @pl.when(has_prev)
        def _():
            ring_copy(rounds - 1, i).wait_recv()

        entering = ring_in[rounds - 1, i]
        earlier, _ = order(i)
        second = (earlier + decays()[0] * entering.astype(F32)).astype(BF16)
        back_keep[i] = jnp.where(is_odd, second, entering)
        back_out[i] = jnp.where(is_odd, entering, second)
        back_copy(i).start()

    def emit_step(i):
        back_copy(i).wait_recv()
        here, there = back_keep[i], back_in[i]
        incoming = (jnp.where(is_odd, there, here), jnp.where(is_odd, here, there))
        sides = []
        for side in range(2):
            wide = slice(side * local, (side + 1) * local)
            coming = incoming[side].astype(F32)
            parts = []
            for f in range(frames):
                rows = slice(f * ROWS, (f + 1) * ROWS)
                state = states[i, rows, wide].astype(F32) + decay[f : f + 1, wide] * coming
                parts.append((state * gate[i, rows, wide].astype(F32)).astype(BF16))
            sides.append(jnp.concatenate(parts, axis=0))
        for side in range(2):
            wide = slice(side * local, (side + 1) * local)
            mix = dot(sides[0], emit_w[0, :, wide]).astype(BF16).astype(F32)
            mix = mix + dot(sides[1], emit_w[1, :, wide]).astype(BF16).astype(F32)
            done = (residual[i, :, wide] + mix).astype(BF16)
            for f in range(frames):
                result[i, side, f] = done[f * ROWS : (f + 1) * ROWS]
        out_copy(i).start()
        keep_copy(i).start()

    @pl.loop(0, chunks + rounds + 2)
    def _(tick):
        @pl.when(tick < chunks)
        def _():
            drive_step(tick)

        for lag in range(1, rounds + 3):
            i = tick - lag

            @pl.when((i >= 0) & (i < chunks))
            def _():
                if lag <= rounds:
                    ring_step(lag - 1, i)
                elif lag == rounds + 1:
                    back_step(i)
                else:
                    emit_step(i)

    @pl.loop(0, chunks)
    def _(i):
        for f in range(frames):
            y_copy(f, i).wait_send()
        pair_copy(i).wait_send()
        back_copy(i).wait_send()
        keep_copy(i).wait()

        @pl.when(has_next)
        def _():
            for r in range(rounds):
                ring_copy(r, i).wait_send()

        out_copy(i).wait()

    for k in range(PIECES):
        for copy in (over_y, over_core, over_z, onward):
            copy(k).wait_send()


def whole_block(clip_id, video_tokens, order, weights, frame_decay):
    frames, positions, width = video_tokens.shape
    local = frame_decay.shape[1]
    half = positions // 2
    chunks = half // ROWS
    pairs = lax.axis_size("tm") // 2
    rounds = min(pairs - 1, -(-(LONGEST_CLIP - 1) // (2 * frames)))
    rows = frames * ROWS
    slots = positions // PAIR * LANES
    dma = pltpu.SemaphoreType.DMA
    anywhere = pl.BlockSpec(memory_space=pl.ANY)
    many = 1 + len(weights)
    return pl.pallas_call(
        functools.partial(block_kernel, frames, rounds),
        in_specs=[pl.BlockSpec(memory_space=pltpu.SMEM)] + [anywhere] * many + [held()] * 2,
        out_specs=anywhere,
        out_shape=jax.ShapeDtypeStruct((frames, positions, local), BF16),
        scratch_shapes=[
            pltpu.VMEM((frames * positions // PAIR, LANES), jnp.int32),
            pltpu.VMEM((frames, positions), jnp.int32),
            pltpu.SMEM((frames, positions), jnp.int32),
            dma,
            pltpu.VMEM((frames, positions, width), BF16),
            pltpu.VMEM((3, width, local), BF16),
            pltpu.VMEM((positions * width // LANES, LANES), F32),
            pltpu.VMEM((STEP_BLOCKS * BLOCK * width // LANES, LANES), F32),
            pltpu.VMEM((slots, local), BF16),
            pltpu.VMEM((frames, half, local), BF16),
            pltpu.VMEM((frames, chunks, ROWS, local), BF16),
            pltpu.VMEM((frames, chunks, ROWS, local), BF16),
            pltpu.VMEM((2, local, width), BF16),
            pltpu.VMEM((2, 3, width, local), BF16),
            pltpu.VMEM((2, local, width), BF16),
            pltpu.VMEM((chunks, rows, width), F32),
            pltpu.VMEM((chunks, rows, width), BF16),
            pltpu.VMEM((chunks, rows, width), BF16),
            pltpu.VMEM((chunks, 2, ROWS, local), BF16),
            pltpu.VMEM((chunks, ROWS, local), BF16),
            pltpu.VMEM((chunks, ROWS, local), F32),
            pltpu.VMEM((rounds, chunks, ROWS, local), BF16),
            pltpu.VMEM((rounds, chunks, ROWS, local), BF16),
            pltpu.VMEM((chunks, ROWS, local), BF16),
            pltpu.VMEM((chunks, ROWS, local), BF16),
            pltpu.VMEM((chunks, ROWS, local), BF16),
            pltpu.VMEM((chunks, 2, frames, ROWS, local), BF16),
            pltpu.VMEM((frames, width), F32),
            pltpu.VMEM((frames, width), F32),
            pltpu.VMEM((frames, width), F32),
            pltpu.VMEM((frames, width), F32),
            pltpu.VMEM((frames, local), F32),
            pltpu.VMEM((frames, 128), jnp.int32),
            pltpu.VMEM((frames, 128), jnp.int32),
            dma((frames + 4,)),
            dma((2, 4, PIECES)),
            dma((2, 3)),
            dma((2, frames, chunks)),
            dma((2, chunks)),
            dma((2, rounds, chunks)),
            dma((2, chunks)),
            dma((2, chunks)),
            dma((chunks,)),
        ],
        compiler_params=pltpu.CompilerParams(
            vmem_limit_bytes=VMEM_LIMIT, collective_id=0, has_side_effects=True
        ),
        cost_estimate=pl.CostEstimate(
            flops=30 * frames * half * width * width,
            bytes_accessed=frames * half * width * 12,
            transcendentals=2 * frames * half * width,
        ),
        name="block",
    )(clip_id, video_tokens, *weights, order, frame_decay)


def per_device(
    video_tokens,
    window_order,
    clip_id,
    attend_weight,
    attend_out,
    recur_weight,
    frame_decay,
    recur_out,
):
    weights = (attend_weight, attend_out, recur_weight, recur_out)
    return whole_block(clip_id, video_tokens, window_order, weights, frame_decay)


def from_behind(value, axis, steps):
    count = lax.axis_size(axis)
    leading, last = (max(0, -steps), min(count, count - steps))
    return lax.ppermute(value, axis, [(source, source + steps) for source in range(leading, last)])


def prefix_2(value, axis, combine, identity):
    count, position = (lax.axis_size(axis), lax.axis_index(axis))
    everything = jax.tree.map(
        lambda part, kind: lax.all_gather(part.astype(kind), axis),
        value,
        (jnp.bfloat16, jnp.bfloat16),
    )
    start = jax.tree.map(
        lambda part, zero: jnp.broadcast_to(jnp.asarray(zero, part.dtype), part.shape),
        value,
        identity,
    )

    def hop(k, before):
        reached = k < position
        new = combine(
            before, jax.tree.map(lambda part, own: part[k].astype(own.dtype), everything, value)
        )
        return jax.tree.map(lambda a, b: jnp.where(reached, a, b), new, before)

    return lax.fori_loop(0, count, hop, start)


def normalize(values):
    return values * lax.rsqrt(jnp.mean(values * values, axis=-1, keepdims=True) + EPSILON)


def window_attention(queries, keys_all, values_all, window_order):
    frame_count, positions, number_of_heads, head_size = queries.shape
    order_index = window_order[:, :, None, None]

    def arrange(tensor):
        reordered = jnp.take_along_axis(tensor, order_index, axis=1)
        return reordered.reshape(
            frame_count, positions // WINDOW, WINDOW, number_of_heads, head_size
        )

    scores = jnp.einsum(
        "fwihe,fwjhe->fwhij",
        arrange(queries),
        arrange(keys_all),
        preferred_element_type=jnp.float32,
    ) / jnp.sqrt(jnp.float32(head_size))
    weights = jax.nn.softmax(scores, axis=-1).astype(jnp.bfloat16)
    blended = jnp.einsum(
        "fwhij,fwjhe->fwihe", weights, arrange(values_all), preferred_element_type=jnp.float32
    ).astype(jnp.bfloat16)
    blended = blended.reshape(frame_count, positions, number_of_heads, head_size)
    inverse = jnp.argsort(window_order, axis=1)
    return jnp.take_along_axis(blended, inverse[:, :, None, None], axis=1)


def per_device_any(
    video_tokens,
    window_order,
    clip_id,
    attend_weight,
    attend_out,
    recur_weight,
    frame_decay,
    recur_out,
):
    frame_count, positions, model_width = video_tokens.shape
    local_width = attend_weight.shape[2]
    row_count = frame_count * positions
    inputs = video_tokens.reshape(row_count, model_width).astype(jnp.float32)
    normed = normalize(inputs).astype(jnp.bfloat16)
    projected = jnp.einsum(
        "td,kde->kte", normed, attend_weight, preferred_element_type=jnp.float32
    ).astype(jnp.bfloat16)
    shaped = projected.reshape(
        3, frame_count, positions, local_width // HEAD_DIMENSION, HEAD_DIMENSION
    )
    attended = window_attention(shaped[0], shaped[1], shaped[2], window_order).reshape(
        row_count, local_width
    )
    partial_mix = jnp.dot(attended, attend_out, preferred_element_type=jnp.float32)
    offset = lax.axis_index("head") * local_width
    residual = inputs + lax.psum(partial_mix.astype(jnp.bfloat16), "head").astype(jnp.float32)
    normed_again = normalize(residual).astype(jnp.bfloat16)
    recur_proj = jnp.einsum(
        "td,kde->kte", normed_again, recur_weight, preferred_element_type=jnp.float32
    )
    residual_own = lax.dynamic_slice_in_dim(residual, offset, local_width, 1)
    gate_in = jax.nn.sigmoid(recur_proj[0]).reshape(frame_count, positions, local_width)
    value_in = recur_proj[1].reshape(frame_count, positions, local_width)
    out_gate = jax.nn.silu(recur_proj[2]).reshape(frame_count, positions, local_width)
    retain = jnp.exp(frame_decay)
    driven = jnp.sqrt(1.0 - retain * retain)[:, None, :] * gate_in * value_in
    previous = from_behind(clip_id[frame_count - 1 :], "tm", 1)
    continues = jnp.concatenate(
        [
            (clip_id[:1] == previous).astype(jnp.float32),
            (clip_id[1:] == clip_id[:-1]).astype(jnp.float32),
        ]
    )
    factor = retain * continues[:, None]

    def advance(carried, inputs_now):
        decay_total, state_now = carried
        factor_now, driven_now = inputs_now
        decay_total = factor_now * decay_total
        state_now = factor_now[None, :] * state_now + driven_now
        return ((decay_total, state_now), (decay_total, state_now))

    start_carry = (
        jnp.ones((local_width,), jnp.float32),
        jnp.zeros((positions, local_width), jnp.float32),
    )
    last_carry, all_carry = lax.scan(advance, start_carry, (factor, driven))
    decay_last, state_last = last_carry
    decay_all, state_all = all_carry

    def combine(earlier, later_part):
        return (later_part[0] * earlier[0], later_part[0][None, :] * earlier[1] + later_part[1])

    prefix = prefix_2(
        (decay_last, state_last),
        "tm",
        combine,
        (jnp.ones_like(decay_last), jnp.zeros_like(state_last)),
    )
    incoming = prefix[1]
    states = state_all + decay_all[:, None, :] * incoming[None, :, :]
    output_rows = (states * out_gate).astype(jnp.bfloat16).reshape(row_count, local_width)
    partial_out = jnp.dot(output_rows, recur_out, preferred_element_type=jnp.float32)
    result = residual_own + lax.psum_scatter(
        partial_out.astype(jnp.bfloat16), "head", scatter_dimension=1, tiled=True
    ).astype(jnp.float32)
    return result.astype(jnp.bfloat16).reshape(frame_count, positions, local_width)


def solution(mesh):
    halves = mesh.shape["head"] == 2 and mesh.shape["clip"] == 2 and mesh.shape["tm"] % 4 == 0
    return jax.shard_map(
        per_device if halves else per_device_any,
        mesh=mesh,
        in_specs=(
            P(("clip", "tm"), None, None),
            P(("clip", "tm"), None),
            P(("clip", "tm")),
            P(None, None, "head"),
            P("head", None),
            P(None, None, "head"),
            P(("clip", "tm"), "head"),
            P("head", None),
        ),
        out_specs=P(("clip", "tm"), None, "head"),
        check_vma=False,
    )
```

```python
import functools

import jax
import jax.numpy as jnp
from jax import lax
from jax.experimental import pallas as pl
from jax.experimental.pallas import tpu as pltpu
from jax.sharding import PartitionSpec as P

HEAD_DIMENSION = 64
WINDOW = 49
LONGEST_CLIP = 8
EPSILON = 1e-06

PAIR = 2 * WINDOW
BLOCK = 112
LANES = 128
STEP_BLOCKS = 4
ROWS = 112

F32, BF16 = jnp.float32, jnp.bfloat16
VMEM_LIMIT = 67043328
COLUMNS = 256
PIECES = 5
PUTS = 2
SHARES = (5, 5, 5, 5, 5, 5, 5, 5, 5, 4)
GROUP = 2
MESH = pl.DeviceIdType.MESH


def dot(a, b):
    return jnp.dot(a, b, preferred_element_type=F32)


def held():
    return pl.BlockSpec(memory_space=pltpu.VMEM)


def block_kernel(frames, rounds, spans, *refs):
    refs = list(refs)

    def take(count):
        taken, refs[:count] = refs[:count], []
        return taken

    (clip,) = take(1)
    x_any, attend_any, mix_any, recur_any, emit_any = take(5)
    order_ref, frame_decay = take(2)
    (out_any,) = take(1)
    slots_ref, order_starts, starts, order_sem = take(4)
    x, attend_w, normed, gathered, blended, own, theirs, arrived = take(8)
    mix_w, recur_w, emit_w, residual, gate, states = take(6)
    pair_out, pair_in, merged, ring_out, ring_in = take(5)
    back_out, back_keep, back_in, result = take(4)
    coef, factor, decay, decay_in, channel_in, clip_out, clip_in = take(7)
    load_sem, weight_sem, small_sem, y_sem, pair_sem, ring_sem, back_sem, out_sem, keep_sem = take(9)

    core, t, h = (lax.axis_index(name) for name in ("clip", "tm", "head"))
    count = lax.axis_size("tm")
    odd = lax.rem(t, 2)
    has_next, has_prev = t + 2 < count, t >= 2
    has_after, has_before = t + 1 < count, t >= 1
    half = arrived.shape[1]
    chunks = len(spans)
    positions, width = x.shape[1:]
    local = own.shape[2]
    steps = slots_ref.shape[0] // (frames * STEP_BLOCKS)
    partner = t + 1 - 2 * odd
    pair_parity = lax.rem(lax.div(t, 2), 2)
    across = t + 2 - 4 * pair_parity
    last = frames - 1
    tiles = width // LANES

    def remote(src, dst, sems, at, **device):
        return pltpu.make_async_remote_copy(
            src_ref=src,
            dst_ref=dst,
            send_sem=sems.at[(0, *at)],
            recv_sem=sems.at[(1, *at)],
            device_id=device,
            device_id_type=MESH,
        )

    def chunk(i):
        return pl.ds(pl.multiple_of(i * ROWS, ROWS), ROWS)

    def span(i):
        return pl.ds(spans[i][0], spans[i][1])

    def y_copy(f, i):
        return remote(theirs.at[f, span(i)], arrived.at[f, span(i)], y_sem, (f, i), head=1 - h)

    def decay_copy():
        return remote(decay, decay_in, small_sem, (0,), tm=partner)

    def channel_copy():
        return remote(frame_decay, channel_in, small_sem, (1,), head=1 - h)

    def clip_copy():
        return remote(clip_out, clip_in, small_sem, (2,), tm=t + 1)

    def pair_copy(i):
        source = pair_out.at[1 - odd, span(i)]
        return remote(source, pair_in.at[span(i)], pair_sem, (i,), tm=partner)

    def ring_copy(r, i):
        source, place = ring_out.at[r, span(i)], ring_in.at[r, span(i)]
        return remote(source, place, ring_sem, (r, i), tm=t + 2)

    def back_copy(i):
        return remote(back_out.at[span(i)], back_in.at[span(i)], back_sem, (i,), tm=partner)

    def placed(i):
        low, size = spans[i]
        return out_any.at[:, pl.ds(pl.multiple_of(h * half + low, 16), size), :]

    def out_copy(i):
        return remote(result.at[1 - h, :, span(i)], placed(i), out_sem, (i,), head=1 - h)

    def keep_copy(i):
        return pltpu.make_async_copy(result.at[h, :, span(i)], placed(i), keep_sem.at[i])

    def quarter(stage, k, p, fresh, **device):
        few = pl.ds(pl.multiple_of(p * (local // 4), local // 4), local // 4)
        many = pl.ds(pl.multiple_of(p * (width // 4), width // 4), width // 4)
        places = [mix_w.at[1, few]] + [recur_w.at[1, j, many] for j in range(3)]
        places += [emit_w.at[1, few]]
        sources = [mix_any.at[few]] + [recur_any.at[j, many] for j in range(3)]
        sources += [emit_any.at[few]]
        source = sources[k] if fresh else places[k]
        return remote(source, places[k], weight_sem, (stage, k), **device)

    part = 2 * pair_parity + core
    facing = 2 * (1 - pair_parity) + core

    def over_y(k):
        return quarter(0, k, part, True, head=1 - h)

    def over_core(k):
        return quarter(1, k, part, False, clip=1 - core)

    def over_z(k):
        return quarter(2, k, part, False, tm=across)

    def onward(k):
        return quarter(3, k, facing, False, clip=1 - core)

    loads = [(x_any.at[f], x.at[f]) for f in range(frames)]
    loads[1:1] = [(attend_any, attend_w)]
    early = 2
    loads += [(mix_any, mix_w.at[0]), (recur_any, recur_w.at[0]), (emit_any, emit_w.at[0])]
    loads = [pltpu.make_async_copy(a, b, load_sem.at[k]) for k, (a, b) in enumerate(loads)]
    for load in loads:
        load.start()

    order = order_ref[...]
    order_starts[...] = lax.div(order, 8) * (8 * tiles) + lax.rem(order, 8)
    starts_copy = pltpu.make_async_copy(order_starts, starts, order_sem)
    starts_copy.start()
    slots_ref[...] = jnp.full_like(slots_ref, -1)
    for f in range(frames):
        for block in range(positions // PAIR):
            piece = order[f : f + 1, block * PAIR : (block + 1) * PAIR]
            line = f * (positions // PAIR) + block
            slots_ref[line : line + 1, :PAIR] = piece

    barrier = pltpu.get_barrier_semaphore()

    def greet(**device):
        pl.semaphore_signal(barrier, inc=1, device_id=device, device_id_type=MESH)

    greet(head=1 - h)
    greet(clip=1 - core)
    for there, step in ((has_after, 1), (has_before, -1), (has_next, 2), (has_prev, -2)):

        @pl.when(there)
        def _():
            greet(tm=t + step)

    near = [has_after, has_before, has_next, has_prev]
    pl.semaphore_wait(barrier, 2 + sum(there.astype(jnp.int32) for there in near))

    channel_copy().start()
    for f in range(frames):
        clip_out[f : f + 1] = jnp.full((1, clip_out.shape[1]), clip[f], jnp.int32)

    @pl.when(has_after)
    def _():
        clip_copy().start()

    for k in range(PIECES):
        over_y(k).start()

    @pl.when(t < 2)
    def _():
        ring_in[...] = jnp.zeros_like(ring_in)

    @pl.when(t < 1)
    def _():
        clip_in[...] = jnp.full(clip_in.shape, -1, jnp.int32)

    def prepare():
        channel_copy().wait()

        @pl.when(has_before)
        def _():
            clip_copy().wait_recv()

        @pl.when(has_after)
        def _():
            clip_copy().wait_send()

        logs = jnp.concatenate([frame_decay[...], channel_in[...]], axis=1)
        retain = jnp.exp(logs)
        coef[...] = jnp.sqrt(1.0 - retain * retain)
        before = clip_in[last : last + 1]
        product = None
        for f in range(frames):
            now = clip_out[f : f + 1]
            follows = jnp.where(now == before, 1.0, 0.0)
            follows = jnp.concatenate([follows] * (width // follows.shape[1]), axis=1)
            here = retain[f : f + 1] * follows
            product = here if f == 0 else product * here
            factor[f : f + 1] = here
            decay[f : f + 1] = product
            before = now
        decay_copy().start()

    two = 2 * HEAD_DIMENSION
    cuts = [chunks * k // PUTS for k in range(PUTS + 1)]

    def attend_step(g):
        f = lax.div(g, steps)
        step = lax.rem(g, steps)

        @pl.when(step == 0)
        def _():
            @pl.loop(0, positions // ROWS)
            def _(i):
                values = x[f, chunk(i)].astype(F32)
                scale = lax.rsqrt(jnp.mean(values * values, axis=-1, keepdims=True) + EPSILON)
                values = (values * scale).reshape(ROWS // 8, 8, width)
                values = [values[:, :, k * LANES : (k + 1) * LANES] for k in range(tiles)]
                values = jnp.stack(values, axis=1).reshape(ROWS * tiles, LANES)
                normed[pl.ds(pl.multiple_of(i * (ROWS * tiles), 8), ROWS * tiles)] = values

        def fetch_row(block, i, k):
            start = starts[f, (step * STEP_BLOCKS + block) * PAIR + i * 8 + k]
            there = pl.ds(i * (8 * tiles) + (block * BLOCK * tiles + k), tiles, stride=8)
            gathered[there, :] = normed[pl.ds(start, tiles, stride=8), :]

        @pl.loop(0, PAIR // 8)
        def _(i):
            for block in range(STEP_BLOCKS):
                for k in range(8):
                    fetch_row(block, i, k)

        for block in range(STEP_BLOCKS):
            for k in range(PAIR % 8):
                fetch_row(block, PAIR // 8, k)

        rows = gathered[...].reshape(-1, tiles, 8, LANES)
        rows = [rows[:, k].reshape(STEP_BLOCKS * BLOCK, LANES) for k in range(tiles)]
        rows = jnp.concatenate(rows, axis=1).astype(BF16)
        queries = (dot(rows, attend_w[0]) * (HEAD_DIMENSION**-0.5)).astype(BF16)
        keys = dot(rows, attend_w[1]).astype(BF16)
        values = dot(rows, attend_w[2]).astype(BF16)

        first = lax.broadcasted_iota(jnp.int32, (LANES, two), 1) < HEAD_DIMENSION
        row = lax.broadcasted_iota(jnp.int32, (BLOCK, LANES), 0)
        column = lax.broadcasted_iota(jnp.int32, (BLOCK, LANES), 1)
        same = ((row < WINDOW) & (column < WINDOW)) | (
            (row >= WINDOW) & (column >= WINDOW) & (column < PAIR)
        )
        lanes = range(0, local, two)
        none = jnp.zeros((LANES, two), BF16)
        ones = jnp.ones((LANES, two), BF16)
        counted = (jnp.where(first, ones, none), jnp.where(first, none, ones))

        def padded(values, low, lane):
            few = jnp.zeros((LANES - BLOCK, two), values.dtype)
            return jnp.concatenate([values[low : low + BLOCK, lane : lane + two], few], axis=0)

        def split(values, low, lane):
            values = padded(values, low, lane)
            return jnp.where(first, values, none), jnp.where(first, none, values)

        def scored(low, lane):
            q = queries[low : low + BLOCK, lane : lane + two]
            k = jnp.concatenate(split(keys, low, lane), axis=0)
            return lax.dot_general(q, k, (((1,), (1,)), ((), ())), preferred_element_type=F32)

        def raised(scores):
            sides = []
            for head in range(2):
                part = jnp.where(same, scores[:, head * LANES : (head + 1) * LANES], -1e30)
                part = jnp.exp(part - jnp.max(part, axis=-1, keepdims=True))
                sides.append(part.astype(BF16))
            return jnp.concatenate(sides, axis=1)

        for group in range(0, STEP_BLOCKS, GROUP):
            pairs = [(block, lane) for block in range(group, group + GROUP) for lane in lanes]
            weights = [scored(block * BLOCK, lane) for block, lane in pairs]
            weights = [raised(scores) for scores in weights]
            for (block, lane), weight in zip(pairs, weights):
                v = split(values, block * BLOCK, lane)
                v = [jnp.concatenate(pair, axis=1) for pair in zip(v, counted)]
                mixed = dot(weight, jnp.concatenate(v, axis=0))
                mixed = mixed[:, :two] * (1.0 / mixed[:, two:])
                at = pl.ds(pl.multiple_of((step * STEP_BLOCKS + block) * LANES, LANES), BLOCK)
                blended[at, lane : lane + two] = mixed.astype(BF16)

        @pl.when(step == steps - 1)
        def _():
            slots = blended.shape[0]
            line = [slots_ref[pl.ds(f * (slots // LANES) + b, 1)] for b in range(slots // LANES)]
            line = jnp.concatenate(line, axis=1)

            @pl.loop(0, 2)
            def _(turn):
                side = jnp.where(turn == 0, 1 - h, h)
                for begin, end in zip(cuts, cuts[1:]):
                    low = spans[begin][0]
                    size = sum(spans[end - 1]) - low
                    token = lax.broadcasted_iota(jnp.int32, (size, slots), 0)
                    put = jnp.where(token + (side * half + low) == line, 1.0, 0.0)
                    block = dot(put.astype(BF16), blended[...]).astype(BF16)

                    @pl.when(turn == 0)
                    def _():
                        theirs[f, low : low + size] = block
                        for j in range(begin, end):
                            y_copy(f, j).start()

                    @pl.when(turn == 1)
                    def _():
                        own[f, low : low + size] = block

    blended[...] = jnp.zeros_like(blended)
    gathered[...] = jnp.zeros_like(gathered)
    for load in loads[:early]:
        load.wait()
    starts_copy.wait()

    @pl.loop(0, frames * steps)
    def _(g):
        @pl.when(g == 1)
        def _():
            prepare()

        for k in range(PIECES):

            @pl.when(g == k + 1)
            def _():
                over_y(k).wait_recv()
                over_core(k).start()
                over_z(k).start()

            @pl.when(g == k + 3)
            def _():
                over_z(k).wait_recv()
                onward(k).start()

        @pl.when(g == steps)
        def _():
            loads[early].wait()

        attend_step(g)

    for load in loads[early + 1 :]:
        load.wait()
    for f in range(last):
        for i in range(chunks):
            y_copy(f, i).wait_recv()

    for k in range(PIECES):
        over_core(k).wait_recv()
        onward(k).wait_recv()
    decay_copy().wait()

    is_odd = odd == 1

    def halves(ref):
        low, high = ref[last : last + 1, :local], ref[last : last + 1, local:]
        return jnp.where(is_odd, high, low)

    def decays():
        here, there = halves(decay), halves(decay_in)
        return jnp.where(is_odd, there, here), jnp.where(is_odd, here, there)

    def order(i):
        here, there = pair_out[odd, span(i)].astype(F32), pair_in[span(i)].astype(F32)
        return jnp.where(is_odd, there, here), jnp.where(is_odd, here, there)

    def drive_step(i):
        low, size = spans[i]
        y_copy(last, i).wait_recv()
        left = jnp.concatenate([own[f, span(i)] for f in range(frames)], axis=0)
        right = jnp.concatenate([arrived[f, span(i)] for f in range(frames)], axis=0)
        mix = dot(left, mix_w[0]).astype(BF16).astype(F32)
        mix = mix + dot(right, mix_w[1]).astype(BF16).astype(F32)
        at = pl.ds(pl.multiple_of(h * half + low, 16), size)
        total = jnp.concatenate([x[f, at].astype(F32) for f in range(frames)], axis=0) + mix
        pieces = [slice(f * size, (f + 1) * size) for f in range(frames)]
        for f in range(frames):
            residual[f, span(i)] = total[pieces[f]]
        scale = lax.rsqrt(jnp.mean(total * total, axis=-1, keepdims=True) + EPSILON)
        again = (total * scale).astype(BF16)

        def projected(which, low):
            side, lanes = low // local, slice(low % local, low % local + COLUMNS)
            return dot(again, recur_w[side, which, :, lanes])

        for low in range(0, width, COLUMNS):
            wide = slice(low, low + COLUMNS)
            drive_in = jax.nn.sigmoid(projected(0, low)) * projected(1, low)
            state = None
            for f in range(frames):
                driven = coef[f : f + 1, wide] * drive_in[pieces[f]]
                state = driven if f == 0 else factor[f : f + 1, wide] * state + driven
                states[f, span(i), wide] = state.astype(BF16)
            side, lanes = low // local, slice(low % local, low % local + COLUMNS)
            pair_out[side, span(i), lanes] = state.astype(BF16)
        pair_copy(i).start()
        for low in range(0, width, COLUMNS):
            opened = projected(2, low)
            opened = (opened * jax.nn.sigmoid(opened)).astype(BF16)
            for f in range(frames):
                gate[f, span(i), low : low + COLUMNS] = opened[pieces[f]]

    def ring_step(r, i):
        earlier_decay, later_decay = decays()
        if r == 0:
            pair_copy(i).wait_recv()
            earlier, later = order(i)
            total = later_decay * earlier + later
            merged[span(i)] = total
        else:

            @pl.when(has_prev)
            def _():
                ring_copy(r - 1, i).wait_recv()

            entering = ring_in[r - 1, span(i)].astype(F32)
            total = merged[span(i)] + (earlier_decay * later_decay) * entering

        @pl.when(has_next)
        def _():
            ring_out[r, span(i)] = total.astype(BF16)
            ring_copy(r, i).start()

    def back_step(i):
        @pl.when(has_prev)
        def _():
            ring_copy(rounds - 1, i).wait_recv()

        entering = ring_in[rounds - 1, span(i)]
        earlier, _ = order(i)
        second = (earlier + decays()[0] * entering.astype(F32)).astype(BF16)
        back_keep[span(i)] = jnp.where(is_odd, second, entering)
        back_out[span(i)] = jnp.where(is_odd, entering, second)
        back_copy(i).start()

    def emit_step(i):
        size = spans[i][1]
        back_copy(i).wait_recv()
        here, there = back_keep[span(i)], back_in[span(i)]
        incoming = (jnp.where(is_odd, there, here), jnp.where(is_odd, here, there))
        sides = []
        for side in range(2):
            wide = slice(side * local, (side + 1) * local)
            coming = incoming[side].astype(F32)
            parts = []
            for f in range(frames):
                state = states[f, span(i), wide].astype(F32) + decay[f : f + 1, wide] * coming
                parts.append((state * gate[f, span(i), wide].astype(F32)).astype(BF16))
            sides.append(jnp.concatenate(parts, axis=0))
        for side in range(2):
            wide = slice(side * local, (side + 1) * local)
            mix = dot(sides[0], emit_w[0, :, wide]).astype(BF16).astype(F32)
            mix = mix + dot(sides[1], emit_w[1, :, wide]).astype(BF16).astype(F32)
            for f in range(frames):
                done = residual[f, span(i), wide] + mix[f * size : (f + 1) * size]
                result[side, f, span(i)] = done.astype(BF16)
        out_copy(i).start()
        keep_copy(i).start()

    for tick in range(chunks + rounds + 2):
        if tick < chunks:
            drive_step(tick)
        for lag in range(1, rounds + 3):
            i = tick - lag
            if 0 <= i < chunks:
                if lag <= rounds:
                    ring_step(lag - 1, i)
                elif lag == rounds + 1:
                    back_step(i)
                else:
                    emit_step(i)

    for i in range(chunks):
        for f in range(frames):
            y_copy(f, i).wait_send()
        pair_copy(i).wait_send()
        back_copy(i).wait_send()
        keep_copy(i).wait()
        out_copy(i).wait()

    @pl.when(has_next)
    def _():
        for i in range(chunks):
            for r in range(rounds):
                ring_copy(r, i).wait_send()

    for k in range(PIECES):
        for copy in (over_y, over_core, over_z, onward):
            copy(k).wait_send()


def whole_block(clip_id, video_tokens, order, weights, frame_decay):
    frames, positions, width = video_tokens.shape
    local = frame_decay.shape[1]
    half = positions // 2
    steps = [half // 16 * sum(SHARES[:k]) // sum(SHARES) for k in range(len(SHARES) + 1)]
    spans = [(16 * a, 16 * (b - a)) for a, b in zip(steps, steps[1:])]
    chunks = len(spans)
    pairs = lax.axis_size("tm") // 2
    rounds = min(pairs - 1, -(-(LONGEST_CLIP - 1) // (2 * frames)))
    slots = positions // PAIR * LANES
    dma = pltpu.SemaphoreType.DMA
    anywhere = pl.BlockSpec(memory_space=pl.ANY)
    many = 1 + len(weights)
    return pl.pallas_call(
        functools.partial(block_kernel, frames, rounds, spans),
        in_specs=[pl.BlockSpec(memory_space=pltpu.SMEM)] + [anywhere] * many + [held()] * 2,
        out_specs=anywhere,
        out_shape=jax.ShapeDtypeStruct((frames, positions, local), BF16),
        scratch_shapes=[
            pltpu.VMEM((frames * positions // PAIR, LANES), jnp.int32),
            pltpu.VMEM((frames, positions), jnp.int32),
            pltpu.SMEM((frames, positions), jnp.int32),
            dma,
            pltpu.VMEM((frames, positions, width), BF16),
            pltpu.VMEM((3, width, local), BF16),
            pltpu.VMEM((positions * width // LANES, LANES), F32),
            pltpu.VMEM((STEP_BLOCKS * BLOCK * width // LANES, LANES), F32),
            pltpu.VMEM((slots, local), BF16),
            pltpu.VMEM((frames, half, local), BF16),
            pltpu.VMEM((frames, half, local), BF16),
            pltpu.VMEM((frames, half, local), BF16),
            pltpu.VMEM((2, local, width), BF16),
            pltpu.VMEM((2, 3, width, local), BF16),
            pltpu.VMEM((2, local, width), BF16),
            pltpu.VMEM((frames, half, width), F32),
            pltpu.VMEM((frames, half, width), BF16),
            pltpu.VMEM((frames, half, width), BF16),
            pltpu.VMEM((2, half, local), BF16),
            pltpu.VMEM((half, local), BF16),
            pltpu.VMEM((half, local), F32),
            pltpu.VMEM((rounds, half, local), BF16),
            pltpu.VMEM((rounds, half, local), BF16),
            pltpu.VMEM((half, local), BF16),
            pltpu.VMEM((half, local), BF16),
            pltpu.VMEM((half, local), BF16),
            pltpu.VMEM((2, frames, half, local), BF16),
            pltpu.VMEM((frames, width), F32),
            pltpu.VMEM((frames, width), F32),
            pltpu.VMEM((frames, width), F32),
            pltpu.VMEM((frames, width), F32),
            pltpu.VMEM((frames, local), F32),
            pltpu.VMEM((frames, 128), jnp.int32),
            pltpu.VMEM((frames, 128), jnp.int32),
            dma((frames + 4,)),
            dma((2, 4, PIECES)),
            dma((2, 3)),
            dma((2, frames, chunks)),
            dma((2, chunks)),
            dma((2, rounds, chunks)),
            dma((2, chunks)),
            dma((2, chunks)),
            dma((chunks,)),
        ],
        compiler_params=pltpu.CompilerParams(
            vmem_limit_bytes=VMEM_LIMIT, collective_id=0, has_side_effects=True
        ),
        cost_estimate=pl.CostEstimate(
            flops=30 * frames * half * width * width,
            bytes_accessed=frames * half * width * 12,
            transcendentals=2 * frames * half * width,
        ),
        name="block",
    )(clip_id, video_tokens, *weights, order, frame_decay)


def per_device(
    video_tokens,
    window_order,
    clip_id,
    attend_weight,
    attend_out,
    recur_weight,
    frame_decay,
    recur_out,
):
    weights = (attend_weight, attend_out, recur_weight, recur_out)
    return whole_block(clip_id, video_tokens, window_order, weights, frame_decay)


def from_behind(value, axis, steps):
    count = lax.axis_size(axis)
    leading, last = (max(0, -steps), min(count, count - steps))
    return lax.ppermute(value, axis, [(source, source + steps) for source in range(leading, last)])


def prefix_2(value, axis, combine, identity):
    count, position = (lax.axis_size(axis), lax.axis_index(axis))
    everything = jax.tree.map(
        lambda part, kind: lax.all_gather(part.astype(kind), axis),
        value,
        (jnp.bfloat16, jnp.bfloat16),
    )
    start = jax.tree.map(
        lambda part, zero: jnp.broadcast_to(jnp.asarray(zero, part.dtype), part.shape),
        value,
        identity,
    )

    def hop(k, before):
        reached = k < position
        new = combine(
            before, jax.tree.map(lambda part, own: part[k].astype(own.dtype), everything, value)
        )
        return jax.tree.map(lambda a, b: jnp.where(reached, a, b), new, before)

    return lax.fori_loop(0, count, hop, start)


def normalize(values):
    return values * lax.rsqrt(jnp.mean(values * values, axis=-1, keepdims=True) + EPSILON)


def window_attention(queries, keys_all, values_all, window_order):
    frame_count, positions, number_of_heads, head_size = queries.shape
    order_index = window_order[:, :, None, None]

    def arrange(tensor):
        reordered = jnp.take_along_axis(tensor, order_index, axis=1)
        return reordered.reshape(
            frame_count, positions // WINDOW, WINDOW, number_of_heads, head_size
        )

    scores = jnp.einsum(
        "fwihe,fwjhe->fwhij",
        arrange(queries),
        arrange(keys_all),
        preferred_element_type=jnp.float32,
    ) / jnp.sqrt(jnp.float32(head_size))
    weights = jax.nn.softmax(scores, axis=-1).astype(jnp.bfloat16)
    blended = jnp.einsum(
        "fwhij,fwjhe->fwihe", weights, arrange(values_all), preferred_element_type=jnp.float32
    ).astype(jnp.bfloat16)
    blended = blended.reshape(frame_count, positions, number_of_heads, head_size)
    inverse = jnp.argsort(window_order, axis=1)
    return jnp.take_along_axis(blended, inverse[:, :, None, None], axis=1)


def per_device_any(
    video_tokens,
    window_order,
    clip_id,
    attend_weight,
    attend_out,
    recur_weight,
    frame_decay,
    recur_out,
):
    frame_count, positions, model_width = video_tokens.shape
    local_width = attend_weight.shape[2]
    row_count = frame_count * positions
    inputs = video_tokens.reshape(row_count, model_width).astype(jnp.float32)
    normed = normalize(inputs).astype(jnp.bfloat16)
    projected = jnp.einsum(
        "td,kde->kte", normed, attend_weight, preferred_element_type=jnp.float32
    ).astype(jnp.bfloat16)
    shaped = projected.reshape(
        3, frame_count, positions, local_width // HEAD_DIMENSION, HEAD_DIMENSION
    )
    attended = window_attention(shaped[0], shaped[1], shaped[2], window_order).reshape(
        row_count, local_width
    )
    partial_mix = jnp.dot(attended, attend_out, preferred_element_type=jnp.float32)
    offset = lax.axis_index("head") * local_width
    residual = inputs + lax.psum(partial_mix.astype(jnp.bfloat16), "head").astype(jnp.float32)
    normed_again = normalize(residual).astype(jnp.bfloat16)
    recur_proj = jnp.einsum(
        "td,kde->kte", normed_again, recur_weight, preferred_element_type=jnp.float32
    )
    residual_own = lax.dynamic_slice_in_dim(residual, offset, local_width, 1)
    gate_in = jax.nn.sigmoid(recur_proj[0]).reshape(frame_count, positions, local_width)
    value_in = recur_proj[1].reshape(frame_count, positions, local_width)
    out_gate = jax.nn.silu(recur_proj[2]).reshape(frame_count, positions, local_width)
    retain = jnp.exp(frame_decay)
    driven = jnp.sqrt(1.0 - retain * retain)[:, None, :] * gate_in * value_in
    previous = from_behind(clip_id[frame_count - 1 :], "tm", 1)
    continues = jnp.concatenate(
        [
            (clip_id[:1] == previous).astype(jnp.float32),
            (clip_id[1:] == clip_id[:-1]).astype(jnp.float32),
        ]
    )
    factor = retain * continues[:, None]

    def advance(carried, inputs_now):
        decay_total, state_now = carried
        factor_now, driven_now = inputs_now
        decay_total = factor_now * decay_total
        state_now = factor_now[None, :] * state_now + driven_now
        return ((decay_total, state_now), (decay_total, state_now))

    start_carry = (
        jnp.ones((local_width,), jnp.float32),
        jnp.zeros((positions, local_width), jnp.float32),
    )
    last_carry, all_carry = lax.scan(advance, start_carry, (factor, driven))
    decay_last, state_last = last_carry
    decay_all, state_all = all_carry

    def combine(earlier, later_part):
        return (later_part[0] * earlier[0], later_part[0][None, :] * earlier[1] + later_part[1])

    prefix = prefix_2(
        (decay_last, state_last),
        "tm",
        combine,
        (jnp.ones_like(decay_last), jnp.zeros_like(state_last)),
    )
    incoming = prefix[1]
    states = state_all + decay_all[:, None, :] * incoming[None, :, :]
    output_rows = (states * out_gate).astype(jnp.bfloat16).reshape(row_count, local_width)
    partial_out = jnp.dot(output_rows, recur_out, preferred_element_type=jnp.float32)
    result = residual_own + lax.psum_scatter(
        partial_out.astype(jnp.bfloat16), "head", scatter_dimension=1, tiled=True
    ).astype(jnp.float32)
    return result.astype(jnp.bfloat16).reshape(frame_count, positions, local_width)


def solution(mesh):
    halves = mesh.shape["head"] == 2 and mesh.shape["clip"] == 2 and mesh.shape["tm"] % 4 == 0
    return jax.shard_map(
        per_device if halves else per_device_any,
        mesh=mesh,
        in_specs=(
            P(("clip", "tm"), None, None),
            P(("clip", "tm"), None),
            P(("clip", "tm")),
            P(None, None, "head"),
            P("head", None),
            P(None, None, "head"),
            P(("clip", "tm"), "head"),
            P("head", None),
        ),
        out_specs=P(("clip", "tm"), None, "head"),
        check_vma=False,
    )
```

```python
import functools

import jax
import jax.numpy as jnp
from jax import lax
from jax.experimental import pallas as pl
from jax.experimental.pallas import tpu as pltpu
from jax.sharding import PartitionSpec as P

HEAD_DIMENSION = 64
WINDOW = 49
LONGEST_CLIP = 8
EPSILON = 1e-06

PAIR = 2 * WINDOW
BLOCK = 112
LANES = 128
STEP_BLOCKS = 4
ROWS = 112

F32, BF16 = jnp.float32, jnp.bfloat16
VMEM_LIMIT = 67043328
COLUMNS = 256
PIECES = 5
PUTS = 2
SHARES = (5, 5, 5, 5, 5, 5, 5, 5, 5, 4)
GROUP = 2
MESH = pl.DeviceIdType.MESH


def dot(a, b):
    return jnp.dot(a, b, preferred_element_type=F32)


def held():
    return pl.BlockSpec(memory_space=pltpu.VMEM)


def block_kernel(frames, rounds, spans, *refs):
    refs = list(refs)

    def take(count):
        taken, refs[:count] = refs[:count], []
        return taken

    (clip,) = take(1)
    x_any, attend_any, mix_any, recur_any, emit_any = take(5)
    order_ref, frame_decay = take(2)
    (out_any,) = take(1)
    slots_ref, order_starts, starts, order_sem = take(4)
    x, attend_w, normed, gathered, blended, own, theirs, arrived = take(8)
    mix_w, recur_w, emit_w, residual, gate, states = take(6)
    pair_out, pair_in, merged, ring_out, ring_in = take(5)
    back_out, back_keep, back_in, result = take(4)
    coef, factor, decay, decay_in, channel_in, clip_out, clip_in = take(7)
    load_sem, weight_sem, small_sem, y_sem, pair_sem, ring_sem, back_sem, out_sem, keep_sem = take(9)

    core, t, h = (lax.axis_index(name) for name in ("clip", "tm", "head"))
    count = lax.axis_size("tm")
    odd = lax.rem(t, 2)
    has_next, has_prev = t + 2 < count, t >= 2
    has_after, has_before = t + 1 < count, t >= 1
    half = arrived.shape[1]
    chunks = len(spans)
    positions, width = x.shape[1:]
    local = own.shape[2]
    steps = slots_ref.shape[1] // (BLOCK * STEP_BLOCKS)
    partner = t + 1 - 2 * odd
    pair_parity = lax.rem(lax.div(t, 2), 2)
    across = t + 2 - 4 * pair_parity
    last = frames - 1
    tiles = width // LANES

    def remote(src, dst, sems, at, **device):
        return pltpu.make_async_remote_copy(
            src_ref=src,
            dst_ref=dst,
            send_sem=sems.at[(0, *at)],
            recv_sem=sems.at[(1, *at)],
            device_id=device,
            device_id_type=MESH,
        )

    def chunk(i):
        return pl.ds(pl.multiple_of(i * ROWS, ROWS), ROWS)

    def span(i):
        return pl.ds(spans[i][0], spans[i][1])

    def y_copy(f, i):
        return remote(theirs.at[f, span(i)], arrived.at[f, span(i)], y_sem, (f, i), head=1 - h)

    def decay_copy():
        return remote(decay, decay_in, small_sem, (0,), tm=partner)

    def channel_copy():
        return remote(frame_decay, channel_in, small_sem, (1,), head=1 - h)

    def clip_copy():
        return remote(clip_out, clip_in, small_sem, (2,), tm=t + 1)

    def pair_copy(i):
        source = pair_out.at[1 - odd, span(i)]
        return remote(source, pair_in.at[span(i)], pair_sem, (i,), tm=partner)

    def ring_copy(r, i):
        source, place = ring_out.at[r, span(i)], ring_in.at[r, span(i)]
        return remote(source, place, ring_sem, (r, i), tm=t + 2)

    def back_copy(i):
        return remote(back_out.at[span(i)], back_in.at[span(i)], back_sem, (i,), tm=partner)

    def placed(i):
        low, size = spans[i]
        return out_any.at[:, pl.ds(pl.multiple_of(h * half + low, 16), size), :]

    def out_copy(i):
        return remote(result.at[1 - h, :, span(i)], placed(i), out_sem, (i,), head=1 - h)

    def keep_copy(i):
        return pltpu.make_async_copy(result.at[h, :, span(i)], placed(i), keep_sem.at[i])

    def quarter(stage, k, p, fresh, **device):
        few = pl.ds(pl.multiple_of(p * (local // 4), local // 4), local // 4)
        many = pl.ds(pl.multiple_of(p * (width // 4), width // 4), width // 4)
        places = [mix_w.at[1, few]] + [recur_w.at[1, j, many] for j in range(3)]
        places += [emit_w.at[1, few]]
        sources = [mix_any.at[few]] + [recur_any.at[j, many] for j in range(3)]
        sources += [emit_any.at[few]]
        source = sources[k] if fresh else places[k]
        return remote(source, places[k], weight_sem, (stage, k), **device)

    part = 2 * pair_parity + core
    facing = 2 * (1 - pair_parity) + core

    def over_y(k):
        return quarter(0, k, part, True, head=1 - h)

    def over_core(k):
        return quarter(1, k, part, False, clip=1 - core)

    def over_z(k):
        return quarter(2, k, part, False, tm=across)

    def onward(k):
        return quarter(3, k, facing, False, clip=1 - core)

    loads = [(x_any.at[f], x.at[f]) for f in range(frames)]
    loads[1:1] = [(attend_any, attend_w)]
    early = 2
    loads += [(mix_any, mix_w.at[0]), (recur_any, recur_w.at[0]), (emit_any, emit_w.at[0])]
    loads = [pltpu.make_async_copy(a, b, load_sem.at[k]) for k, (a, b) in enumerate(loads)]
    for load in loads:
        load.start()

    order = order_ref[...]
    order_starts[...] = lax.div(order, 8) * (8 * tiles) + lax.rem(order, 8)
    starts_copy = pltpu.make_async_copy(order_starts, starts, order_sem)
    starts_copy.start()
    slots_ref[...] = jnp.full_like(slots_ref, -1)
    for f in range(frames):
        for block in range(positions // PAIR):
            piece = order[f : f + 1, block * PAIR : (block + 1) * PAIR]
            slots_ref[f : f + 1, block * BLOCK : block * BLOCK + PAIR] = piece

    barrier = pltpu.get_barrier_semaphore()

    def greet(**device):
        pl.semaphore_signal(barrier, inc=1, device_id=device, device_id_type=MESH)

    greet(head=1 - h)
    greet(clip=1 - core)
    for there, step in ((has_after, 1), (has_before, -1), (has_next, 2), (has_prev, -2)):

        @pl.when(there)
        def _():
            greet(tm=t + step)

    near = [has_after, has_before, has_next, has_prev]
    pl.semaphore_wait(barrier, 2 + sum(there.astype(jnp.int32) for there in near))

    channel_copy().start()
    for f in range(frames):
        clip_out[f : f + 1] = jnp.full((1, clip_out.shape[1]), clip[f], jnp.int32)

    @pl.when(has_after)
    def _():
        clip_copy().start()

    for k in range(PIECES):
        over_y(k).start()

    @pl.when(t < 2)
    def _():
        ring_in[...] = jnp.zeros_like(ring_in)

    @pl.when(t < 1)
    def _():
        clip_in[...] = jnp.full(clip_in.shape, -1, jnp.int32)

    def prepare():
        channel_copy().wait()

        @pl.when(has_before)
        def _():
            clip_copy().wait_recv()

        @pl.when(has_after)
        def _():
            clip_copy().wait_send()

        logs = jnp.concatenate([frame_decay[...], channel_in[...]], axis=1)
        retain = jnp.exp(logs)
        coef[...] = jnp.sqrt(1.0 - retain * retain)
        before = clip_in[last : last + 1]
        product = None
        for f in range(frames):
            now = clip_out[f : f + 1]
            follows = jnp.where(now == before, 1.0, 0.0)
            follows = jnp.concatenate([follows] * (width // follows.shape[1]), axis=1)
            here = retain[f : f + 1] * follows
            product = here if f == 0 else product * here
            factor[f : f + 1] = here
            decay[f : f + 1] = product
            before = now
        decay_copy().start()

    two = 2 * HEAD_DIMENSION
    cuts = [chunks * k // PUTS for k in range(PUTS + 1)]

    def attend_step(g):
        f = lax.div(g, steps)
        step = lax.rem(g, steps)

        @pl.when(step == 0)
        def _():
            @pl.loop(0, positions // ROWS)
            def _(i):
                values = x[f, chunk(i)].astype(F32)
                scale = lax.rsqrt(jnp.mean(values * values, axis=-1, keepdims=True) + EPSILON)
                values = (values * scale).reshape(ROWS // 8, 8, width)
                values = [values[:, :, k * LANES : (k + 1) * LANES] for k in range(tiles)]
                values = jnp.stack(values, axis=1).reshape(ROWS * tiles, LANES)
                normed[pl.ds(pl.multiple_of(i * (ROWS * tiles), 8), ROWS * tiles)] = values

        def fetch_row(block, i, k):
            start = starts[f, (step * STEP_BLOCKS + block) * PAIR + i * 8 + k]
            there = pl.ds(i * (8 * tiles) + (block * BLOCK * tiles + k), tiles, stride=8)
            gathered[there, :] = normed[pl.ds(start, tiles, stride=8), :]

        @pl.loop(0, PAIR // 8)
        def _(i):
            for block in range(STEP_BLOCKS):
                for k in range(8):
                    fetch_row(block, i, k)

        for block in range(STEP_BLOCKS):
            for k in range(PAIR % 8):
                fetch_row(block, PAIR // 8, k)

        rows = gathered[...].reshape(-1, tiles, 8, LANES)
        rows = [rows[:, k].reshape(STEP_BLOCKS * BLOCK, LANES) for k in range(tiles)]
        rows = jnp.concatenate(rows, axis=1).astype(BF16)
        queries = (dot(rows, attend_w[0]) * (HEAD_DIMENSION**-0.5)).astype(BF16)
        keys = dot(rows, attend_w[1]).astype(BF16)
        values = dot(rows, attend_w[2]).astype(BF16)

        first = lax.broadcasted_iota(jnp.int32, (LANES, two), 1) < HEAD_DIMENSION
        row = lax.broadcasted_iota(jnp.int32, (BLOCK, LANES), 0)
        column = lax.broadcasted_iota(jnp.int32, (BLOCK, LANES), 1)
        same = ((row < WINDOW) & (column < WINDOW)) | (
            (row >= WINDOW) & (column >= WINDOW) & (column < PAIR)
        )
        lanes = range(0, local, two)
        none = jnp.zeros((LANES, two), BF16)
        ones = jnp.ones((LANES, two), BF16)
        counted = (jnp.where(first, ones, none), jnp.where(first, none, ones))

        def padded(values, low, lane):
            few = jnp.zeros((LANES - BLOCK, two), values.dtype)
            return jnp.concatenate([values[low : low + BLOCK, lane : lane + two], few], axis=0)

        def split(values, low, lane):
            values = padded(values, low, lane)
            return jnp.where(first, values, none), jnp.where(first, none, values)

        def scored(low, lane):
            q = queries[low : low + BLOCK, lane : lane + two]
            k = jnp.concatenate(split(keys, low, lane), axis=0)
            return lax.dot_general(q, k, (((1,), (1,)), ((), ())), preferred_element_type=F32)

        def raised(scores):
            sides = []
            for head in range(2):
                part = jnp.where(same, scores[:, head * LANES : (head + 1) * LANES], -1e30)
                part = jnp.exp(part - jnp.max(part, axis=-1, keepdims=True))
                sides.append(part.astype(BF16))
            return jnp.concatenate(sides, axis=1)

        for group in range(0, STEP_BLOCKS, GROUP):
            pairs = [(block, lane) for block in range(group, group + GROUP) for lane in lanes]
            weights = [scored(block * BLOCK, lane) for block, lane in pairs]
            weights = [raised(scores) for scores in weights]
            for (block, lane), weight in zip(pairs, weights):
                v = split(values, block * BLOCK, lane)
                v = [jnp.concatenate(pair, axis=1) for pair in zip(v, counted)]
                mixed = dot(weight, jnp.concatenate(v, axis=0))
                mixed = mixed[:, :two] * (1.0 / mixed[:, two:])
                at = pl.ds(pl.multiple_of((step * STEP_BLOCKS + block) * BLOCK, BLOCK), BLOCK)
                blended[at, lane : lane + two] = mixed.astype(BF16)

        @pl.when(step == steps - 1)
        def _():
            slots = blended.shape[0]
            line = slots_ref[pl.ds(f, 1)]

            @pl.loop(0, 2)
            def _(turn):
                side = jnp.where(turn == 0, 1 - h, h)
                for begin, end in zip(cuts, cuts[1:]):
                    low = spans[begin][0]
                    size = sum(spans[end - 1]) - low
                    token = lax.broadcasted_iota(jnp.int32, (size, slots), 0)
                    put = jnp.where(token + (side * half + low) == line, 1.0, 0.0)
                    block = dot(put.astype(BF16), blended[...]).astype(BF16)

                    @pl.when(turn == 0)
                    def _():
                        theirs[f, low : low + size] = block
                        for j in range(begin, end):
                            y_copy(f, j).start()

                    @pl.when(turn == 1)
                    def _():
                        own[f, low : low + size] = block

    blended[...] = jnp.zeros_like(blended)
    gathered[...] = jnp.zeros_like(gathered)
    for load in loads[:early]:
        load.wait()
    starts_copy.wait()

    @pl.loop(0, frames * steps)
    def _(g):
        @pl.when(g == 1)
        def _():
            prepare()

        for k in range(PIECES):

            @pl.when(g == k + 1)
            def _():
                over_y(k).wait_recv()
                over_core(k).start()
                over_z(k).start()

            @pl.when(g == k + 3)
            def _():
                over_z(k).wait_recv()
                onward(k).start()

        @pl.when(g == steps)
        def _():
            loads[early].wait()

        attend_step(g)

    for load in loads[early + 1 :]:
        load.wait()
    for f in range(last):
        for i in range(chunks):
            y_copy(f, i).wait_recv()

    for k in range(PIECES):
        over_core(k).wait_recv()
        onward(k).wait_recv()
    decay_copy().wait()

    is_odd = odd == 1

    def halves(ref):
        low, high = ref[last : last + 1, :local], ref[last : last + 1, local:]
        return jnp.where(is_odd, high, low)

    def decays():
        here, there = halves(decay), halves(decay_in)
        return jnp.where(is_odd, there, here), jnp.where(is_odd, here, there)

    def order(i):
        here, there = pair_out[odd, span(i)].astype(F32), pair_in[span(i)].astype(F32)
        return jnp.where(is_odd, there, here), jnp.where(is_odd, here, there)

    def drive_step(i):
        low, size = spans[i]
        y_copy(last, i).wait_recv()
        left = jnp.concatenate([own[f, span(i)] for f in range(frames)], axis=0)
        right = jnp.concatenate([arrived[f, span(i)] for f in range(frames)], axis=0)
        mix = dot(left, mix_w[0]).astype(BF16).astype(F32)
        mix = mix + dot(right, mix_w[1]).astype(BF16).astype(F32)
        at = pl.ds(pl.multiple_of(h * half + low, 16), size)
        total = jnp.concatenate([x[f, at].astype(F32) for f in range(frames)], axis=0) + mix
        pieces = [slice(f * size, (f + 1) * size) for f in range(frames)]
        for f in range(frames):
            residual[f, span(i)] = total[pieces[f]]
        scale = lax.rsqrt(jnp.mean(total * total, axis=-1, keepdims=True) + EPSILON)
        again = (total * scale).astype(BF16)

        def projected(which, low):
            side, lanes = low // local, slice(low % local, low % local + COLUMNS)
            return dot(again, recur_w[side, which, :, lanes])

        for low in range(0, width, COLUMNS):
            wide = slice(low, low + COLUMNS)
            drive_in = jax.nn.sigmoid(projected(0, low)) * projected(1, low)
            state = None
            for f in range(frames):
                driven = coef[f : f + 1, wide] * drive_in[pieces[f]]
                state = driven if f == 0 else factor[f : f + 1, wide] * state + driven
                states[f, span(i), wide] = state.astype(BF16)
            side, lanes = low // local, slice(low % local, low % local + COLUMNS)
            pair_out[side, span(i), lanes] = state.astype(BF16)
        pair_copy(i).start()
        for low in range(0, width, COLUMNS):
            opened = projected(2, low)
            opened = (opened * jax.nn.sigmoid(opened)).astype(BF16)
            for f in range(frames):
                gate[f, span(i), low : low + COLUMNS] = opened[pieces[f]]

    def ring_step(r, i):
        earlier_decay, later_decay = decays()
        if r == 0:
            pair_copy(i).wait_recv()
            earlier, later = order(i)
            total = later_decay * earlier + later
            merged[span(i)] = total
        else:

            @pl.when(has_prev)
            def _():
                ring_copy(r - 1, i).wait_recv()

            entering = ring_in[r - 1, span(i)].astype(F32)
            total = merged[span(i)] + (earlier_decay * later_decay) * entering

        @pl.when(has_next)
        def _():
            ring_out[r, span(i)] = total.astype(BF16)
            ring_copy(r, i).start()

    def back_step(i):
        @pl.when(has_prev)
        def _():
            ring_copy(rounds - 1, i).wait_recv()

        entering = ring_in[rounds - 1, span(i)]
        earlier, _ = order(i)
        second = (earlier + decays()[0] * entering.astype(F32)).astype(BF16)
        back_keep[span(i)] = jnp.where(is_odd, second, entering)
        back_out[span(i)] = jnp.where(is_odd, entering, second)
        back_copy(i).start()

    def emit_step(i):
        size = spans[i][1]
        back_copy(i).wait_recv()
        here, there = back_keep[span(i)], back_in[span(i)]
        incoming = (jnp.where(is_odd, there, here), jnp.where(is_odd, here, there))
        sides = []
        for side in range(2):
            wide = slice(side * local, (side + 1) * local)
            coming = incoming[side].astype(F32)
            parts = []
            for f in range(frames):
                state = states[f, span(i), wide].astype(F32) + decay[f : f + 1, wide] * coming
                parts.append((state * gate[f, span(i), wide].astype(F32)).astype(BF16))
            sides.append(jnp.concatenate(parts, axis=0))
        for side in range(2):
            wide = slice(side * local, (side + 1) * local)
            mix = dot(sides[0], emit_w[0, :, wide]).astype(BF16).astype(F32)
            mix = mix + dot(sides[1], emit_w[1, :, wide]).astype(BF16).astype(F32)
            for f in range(frames):
                done = residual[f, span(i), wide] + mix[f * size : (f + 1) * size]
                result[side, f, span(i)] = done.astype(BF16)
        out_copy(i).start()
        keep_copy(i).start()

    for tick in range(chunks + rounds + 2):
        if tick < chunks:
            drive_step(tick)
        for lag in range(1, rounds + 3):
            i = tick - lag
            if 0 <= i < chunks:
                if lag <= rounds:
                    ring_step(lag - 1, i)
                elif lag == rounds + 1:
                    back_step(i)
                else:
                    emit_step(i)

    for i in range(chunks):
        for f in range(frames):
            y_copy(f, i).wait_send()
        pair_copy(i).wait_send()
        back_copy(i).wait_send()
        keep_copy(i).wait()
        out_copy(i).wait()

    @pl.when(has_next)
    def _():
        for i in range(chunks):
            for r in range(rounds):
                ring_copy(r, i).wait_send()

    for k in range(PIECES):
        for copy in (over_y, over_core, over_z, onward):
            copy(k).wait_send()


def whole_block(clip_id, video_tokens, order, weights, frame_decay):
    frames, positions, width = video_tokens.shape
    local = frame_decay.shape[1]
    half = positions // 2
    steps = [half // 16 * sum(SHARES[:k]) // sum(SHARES) for k in range(len(SHARES) + 1)]
    spans = [(16 * a, 16 * (b - a)) for a, b in zip(steps, steps[1:])]
    chunks = len(spans)
    pairs = lax.axis_size("tm") // 2
    rounds = min(pairs - 1, -(-(LONGEST_CLIP - 1) // (2 * frames)))
    slots = positions // PAIR * BLOCK
    dma = pltpu.SemaphoreType.DMA
    anywhere = pl.BlockSpec(memory_space=pl.ANY)
    many = 1 + len(weights)
    return pl.pallas_call(
        functools.partial(block_kernel, frames, rounds, spans),
        in_specs=[pl.BlockSpec(memory_space=pltpu.SMEM)] + [anywhere] * many + [held()] * 2,
        out_specs=anywhere,
        out_shape=jax.ShapeDtypeStruct((frames, positions, local), BF16),
        scratch_shapes=[
            pltpu.VMEM((frames, slots), jnp.int32),
            pltpu.VMEM((frames, positions), jnp.int32),
            pltpu.SMEM((frames, positions), jnp.int32),
            dma,
            pltpu.VMEM((frames, positions, width), BF16),
            pltpu.VMEM((3, width, local), BF16),
            pltpu.VMEM((positions * width // LANES, LANES), F32),
            pltpu.VMEM((STEP_BLOCKS * BLOCK * width // LANES, LANES), F32),
            pltpu.VMEM((slots, local), BF16),
            pltpu.VMEM((frames, half, local), BF16),
            pltpu.VMEM((frames, half, local), BF16),
            pltpu.VMEM((frames, half, local), BF16),
            pltpu.VMEM((2, local, width), BF16),
            pltpu.VMEM((2, 3, width, local), BF16),
            pltpu.VMEM((2, local, width), BF16),
            pltpu.VMEM((frames, half, width), F32),
            pltpu.VMEM((frames, half, width), BF16),
            pltpu.VMEM((frames, half, width), BF16),
            pltpu.VMEM((2, half, local), BF16),
            pltpu.VMEM((half, local), BF16),
            pltpu.VMEM((half, local), F32),
            pltpu.VMEM((rounds, half, local), BF16),
            pltpu.VMEM((rounds, half, local), BF16),
            pltpu.VMEM((half, local), BF16),
            pltpu.VMEM((half, local), BF16),
            pltpu.VMEM((half, local), BF16),
            pltpu.VMEM((2, frames, half, local), BF16),
            pltpu.VMEM((frames, width), F32),
            pltpu.VMEM((frames, width), F32),
            pltpu.VMEM((frames, width), F32),
            pltpu.VMEM((frames, width), F32),
            pltpu.VMEM((frames, local), F32),
            pltpu.VMEM((frames, 128), jnp.int32),
            pltpu.VMEM((frames, 128), jnp.int32),
            dma((frames + 4,)),
            dma((2, 4, PIECES)),
            dma((2, 3)),
            dma((2, frames, chunks)),
            dma((2, chunks)),
            dma((2, rounds, chunks)),
            dma((2, chunks)),
            dma((2, chunks)),
            dma((chunks,)),
        ],
        compiler_params=pltpu.CompilerParams(
            vmem_limit_bytes=VMEM_LIMIT, collective_id=0, has_side_effects=True
        ),
        cost_estimate=pl.CostEstimate(
            flops=30 * frames * half * width * width,
            bytes_accessed=frames * half * width * 12,
            transcendentals=2 * frames * half * width,
        ),
        name="block",
    )(clip_id, video_tokens, *weights, order, frame_decay)


def per_device(
    video_tokens,
    window_order,
    clip_id,
    attend_weight,
    attend_out,
    recur_weight,
    frame_decay,
    recur_out,
):
    weights = (attend_weight, attend_out, recur_weight, recur_out)
    return whole_block(clip_id, video_tokens, window_order, weights, frame_decay)


def from_behind(value, axis, steps):
    count = lax.axis_size(axis)
    leading, last = (max(0, -steps), min(count, count - steps))
    return lax.ppermute(value, axis, [(source, source + steps) for source in range(leading, last)])


def prefix_2(value, axis, combine, identity):
    count, position = (lax.axis_size(axis), lax.axis_index(axis))
    everything = jax.tree.map(
        lambda part, kind: lax.all_gather(part.astype(kind), axis),
        value,
        (jnp.bfloat16, jnp.bfloat16),
    )
    start = jax.tree.map(
        lambda part, zero: jnp.broadcast_to(jnp.asarray(zero, part.dtype), part.shape),
        value,
        identity,
    )

    def hop(k, before):
        reached = k < position
        new = combine(
            before, jax.tree.map(lambda part, own: part[k].astype(own.dtype), everything, value)
        )
        return jax.tree.map(lambda a, b: jnp.where(reached, a, b), new, before)

    return lax.fori_loop(0, count, hop, start)


def normalize(values):
    return values * lax.rsqrt(jnp.mean(values * values, axis=-1, keepdims=True) + EPSILON)


def window_attention(queries, keys_all, values_all, window_order):
    frame_count, positions, number_of_heads, head_size = queries.shape
    order_index = window_order[:, :, None, None]

    def arrange(tensor):
        reordered = jnp.take_along_axis(tensor, order_index, axis=1)
        return reordered.reshape(
            frame_count, positions // WINDOW, WINDOW, number_of_heads, head_size
        )

    scores = jnp.einsum(
        "fwihe,fwjhe->fwhij",
        arrange(queries),
        arrange(keys_all),
        preferred_element_type=jnp.float32,
    ) / jnp.sqrt(jnp.float32(head_size))
    weights = jax.nn.softmax(scores, axis=-1).astype(jnp.bfloat16)
    blended = jnp.einsum(
        "fwhij,fwjhe->fwihe", weights, arrange(values_all), preferred_element_type=jnp.float32
    ).astype(jnp.bfloat16)
    blended = blended.reshape(frame_count, positions, number_of_heads, head_size)
    inverse = jnp.argsort(window_order, axis=1)
    return jnp.take_along_axis(blended, inverse[:, :, None, None], axis=1)


def per_device_any(
    video_tokens,
    window_order,
    clip_id,
    attend_weight,
    attend_out,
    recur_weight,
    frame_decay,
    recur_out,
):
    frame_count, positions, model_width = video_tokens.shape
    local_width = attend_weight.shape[2]
    row_count = frame_count * positions
    inputs = video_tokens.reshape(row_count, model_width).astype(jnp.float32)
    normed = normalize(inputs).astype(jnp.bfloat16)
    projected = jnp.einsum(
        "td,kde->kte", normed, attend_weight, preferred_element_type=jnp.float32
    ).astype(jnp.bfloat16)
    shaped = projected.reshape(
        3, frame_count, positions, local_width // HEAD_DIMENSION, HEAD_DIMENSION
    )
    attended = window_attention(shaped[0], shaped[1], shaped[2], window_order).reshape(
        row_count, local_width
    )
    partial_mix = jnp.dot(attended, attend_out, preferred_element_type=jnp.float32)
    offset = lax.axis_index("head") * local_width
    residual = inputs + lax.psum(partial_mix.astype(jnp.bfloat16), "head").astype(jnp.float32)
    normed_again = normalize(residual).astype(jnp.bfloat16)
    recur_proj = jnp.einsum(
        "td,kde->kte", normed_again, recur_weight, preferred_element_type=jnp.float32
    )
    residual_own = lax.dynamic_slice_in_dim(residual, offset, local_width, 1)
    gate_in = jax.nn.sigmoid(recur_proj[0]).reshape(frame_count, positions, local_width)
    value_in = recur_proj[1].reshape(frame_count, positions, local_width)
    out_gate = jax.nn.silu(recur_proj[2]).reshape(frame_count, positions, local_width)
    retain = jnp.exp(frame_decay)
    driven = jnp.sqrt(1.0 - retain * retain)[:, None, :] * gate_in * value_in
    previous = from_behind(clip_id[frame_count - 1 :], "tm", 1)
    continues = jnp.concatenate(
        [
            (clip_id[:1] == previous).astype(jnp.float32),
            (clip_id[1:] == clip_id[:-1]).astype(jnp.float32),
        ]
    )
    factor = retain * continues[:, None]

    def advance(carried, inputs_now):
        decay_total, state_now = carried
        factor_now, driven_now = inputs_now
        decay_total = factor_now * decay_total
        state_now = factor_now[None, :] * state_now + driven_now
        return ((decay_total, state_now), (decay_total, state_now))

    start_carry = (
        jnp.ones((local_width,), jnp.float32),
        jnp.zeros((positions, local_width), jnp.float32),
    )
    last_carry, all_carry = lax.scan(advance, start_carry, (factor, driven))
    decay_last, state_last = last_carry
    decay_all, state_all = all_carry

    def combine(earlier, later_part):
        return (later_part[0] * earlier[0], later_part[0][None, :] * earlier[1] + later_part[1])

    prefix = prefix_2(
        (decay_last, state_last),
        "tm",
        combine,
        (jnp.ones_like(decay_last), jnp.zeros_like(state_last)),
    )
    incoming = prefix[1]
    states = state_all + decay_all[:, None, :] * incoming[None, :, :]
    output_rows = (states * out_gate).astype(jnp.bfloat16).reshape(row_count, local_width)
    partial_out = jnp.dot(output_rows, recur_out, preferred_element_type=jnp.float32)
    result = residual_own + lax.psum_scatter(
        partial_out.astype(jnp.bfloat16), "head", scatter_dimension=1, tiled=True
    ).astype(jnp.float32)
    return result.astype(jnp.bfloat16).reshape(frame_count, positions, local_width)


def solution(mesh):
    halves = mesh.shape["head"] == 2 and mesh.shape["clip"] == 2 and mesh.shape["tm"] % 4 == 0
    return jax.shard_map(
        per_device if halves else per_device_any,
        mesh=mesh,
        in_specs=(
            P(("clip", "tm"), None, None),
            P(("clip", "tm"), None),
            P(("clip", "tm")),
            P(None, None, "head"),
            P("head", None),
            P(None, None, "head"),
            P(("clip", "tm"), "head"),
            P("head", None),
        ),
        out_specs=P(("clip", "tm"), None, "head"),
        check_vma=False,
    )
```
